32 devices in a mesh: fsdp: 8 (over z, y), ctx: 2 (over x), tensor: 2 (over core).
Axes of the slice: x: 2, y: 2, z: 4, core: 2. Of those that a mesh axis runs over, the one named last changes fastest.
Arguments:
- block_input: bfloat16 [8, 1024, 1024], P('fsdp', 'ctx'), may hold values from -6 to 6
- operator_gain: bfloat16 [1024], P('fsdp'), may hold values from 0.5 to 1.5
- query_weight: bfloat16 [1024, 1024], P('fsdp', 'tensor'), may hold values from -0.1875 to 0.1875
- key_weight: bfloat16 [1024, 512], P('fsdp', 'tensor'), may hold values from -0.1875 to 0.1875
- value_weight: bfloat16 [1024, 512], P('fsdp', 'tensor'), may hold values from -0.1875 to 0.1875
- output_weight: bfloat16 [1024, 1024], P('tensor', 'fsdp'), may hold values from -0.75 to 0.75
- feedforward_gain: bfloat16 [1024], P('fsdp'), may hold values from 0.5 to 1.5
- gate_weight: bfloat16 [1024, 4608], P('fsdp', 'tensor'), may hold values from -0.1875 to 0.1875
- up_weight: bfloat16 [1024, 4608], P('fsdp', 'tensor'), may hold values from -0.1875 to 0.1875
- down_weight: bfloat16 [4608, 1024], P('tensor', 'fsdp'), may hold values from -0.09375 to 0.09375
- query_gain: bfloat16 [64], P('fsdp'), may hold values from 0.6 to 4
- key_gain: bfloat16 [64], P('fsdp'), may hold values from 0.6 to 4
- cotangent: bfloat16 [8, 1024, 1024], P('fsdp', 'ctx'), may hold values from -6 to 6
Outputs:
- block_output: bfloat16 [8, 1024, 1024], P('fsdp', 'ctx')
- input_grad: float32 [8, 1024, 1024], P('fsdp', 'ctx')
- operator_gain_grad: float32 [1024], P('fsdp')
- query_weight_grad: float32 [1024, 1024], P('fsdp', 'tensor')
- key_weight_grad: float32 [1024, 512], P('fsdp', 'tensor')
- value_weight_grad: float32 [1024, 512], P('fsdp', 'tensor')
- output_weight_grad: float32 [1024, 1024], P('tensor', 'fsdp')
- feedforward_gain_grad: float32 [1024], P('fsdp')
- gate_weight_grad: float32 [1024, 4608], P('fsdp', 'tensor')
- up_weight_grad: float32 [1024, 4608], P('fsdp', 'tensor')
- down_weight_grad: float32 [4608, 1024], P('tensor', 'fsdp')
- query_gain_grad: float32 [64], P('fsdp')
- key_gain_grad: float32 [64], P('fsdp')
The draws below stay inside these ranges and needn't reach their ends.
All inputs are finite; a program needn't handle non-finite values.
Results may differ from the reference program's by a relative error of at most 0.024.
The reference program's roundings to bfloat16 on the way (of `normed_input`, `attended`, `normed_hidden`, `activation`, `attended_grad` and `score_grad`) count: a program that leaves them out, or rounds other values in their place, can miss the bound.
Values may be sent and summed in bfloat16 or wider, within the bound.
A program may use at most 192 MiB of HBM per device.

```python
import jax
import jax.numpy as jnp
from jax import lax

D = 1024
H = 16
KV = 8
HD = 64
FF = 4608
LEN = 1024
SEQS = 8


def draw_query_gain(key, part):
    base = jax.random.uniform(jax.random.fold_in(key, 11), (HD,), jnp.float32, 0.6, 1.6)
    return base.astype(jnp.bfloat16)


def draw_key_gain(key, part):
    base = jax.random.uniform(jax.random.fold_in(key, 13), (HD,), jnp.float32, 0.6, 1.6)
    return base.astype(jnp.bfloat16)


def shard_levels(stream_key, extent, shards, least, largest):
    def one(axis_at, parts):
        steps = jax.random.uniform(jax.random.fold_in(jax.random.fold_in(stream_key, 6), axis_at), (parts,), jnp.float32, least / len(shards), largest / len(shards))
        return jnp.repeat(jnp.exp(steps), extent[axis_at] // parts).reshape((-1,) + (1,) * (len(extent) - axis_at - 1))

    loudness = one(*shards[0])
    for cut in shards[1:]:
        loudness = loudness * one(*cut)
    return loudness


def normal_values(own_key, extent, scale, bound, shards=(), held_as=jnp.bfloat16):
    values = jax.random.normal(own_key, extent, jnp.float32) * scale
    if len(shards) > 0:
        values = shard_levels(own_key, extent, shards, -0.22, 0.18) * values
    return jnp.clip(values, min=-bound, max=bound).astype(held_as)


def setup_inputs(seed: int = 0) -> dict:
    arg_keys = jax.random.split(jax.random.key(seed), 14)
    block_input = normal_values(arg_keys[0], (SEQS, LEN, D), 1.0, 6.0, ((0, 8), (1, 2)))
    operator_gain = jnp.clip(1.0 + 0.1 * jax.random.normal(arg_keys[1], (D,), jnp.float32), 0.5, 1.5).astype(jnp.bfloat16)
    query_weight = normal_values(arg_keys[2], (D, H * HD), D ** -0.5, 0.1875, ((0, 8), (1, 2)))
    key_weight = normal_values(arg_keys[3], (D, KV * HD), D ** -0.5, 0.1875, ((0, 8), (1, 2)))
    value_weight = normal_values(arg_keys[4], (D, KV * HD), D ** -0.5, 0.1875, ((0, 8), (1, 2)))
    output_weight = normal_values(arg_keys[5], (H * HD, D), (H * HD // 16) ** -0.5, 0.75, ((0, 2), (1, 8)))
    feedforward_gain = jnp.clip(1.0 + 0.1 * jax.random.normal(arg_keys[6], (D,), jnp.float32), 0.5, 1.5).astype(jnp.bfloat16)
    gate_weight = normal_values(arg_keys[7], (D, FF), D ** -0.5, 0.1875, ((0, 8), (1, 2)))
    up_weight = normal_values(arg_keys[8], (D, FF), D ** -0.5, 0.1875, ((0, 8), (1, 2)))
    down_weight = normal_values(arg_keys[9], (FF, D), FF ** -0.5, 0.09375, ((0, 2), (1, 8)))
    query_gain = draw_query_gain(jax.random.fold_in(arg_keys[13], 71), 0)
    key_gain = draw_key_gain(jax.random.fold_in(arg_keys[13], 71), 0)
    cotangent = normal_values(arg_keys[12], (SEQS, LEN, D), 1.0, 6.0, ((0, 8), (1, 2)))
    return {"block_input": block_input, "operator_gain": operator_gain, "query_weight": query_weight, "key_weight": key_weight, "value_weight": value_weight, "output_weight": output_weight, "feedforward_gain": feedforward_gain, "gate_weight": gate_weight, "up_weight": up_weight, "down_weight": down_weight, "query_gain": query_gain, "key_gain": key_gain, "cotangent": cotangent}


EPS = 1e-05
THETA = 1000000.0

def rms_scale(values_in, gain):
    return values_in * lax.rsqrt(lax.optimization_barrier(jnp.mean(values_in * values_in, axis=-1, keepdims=True)) + EPS) * gain

def rotary_tables(positions, head_width):
    half_width = head_width // 2
    freqs = THETA ** (-jnp.arange(half_width).astype(jnp.float32) * 2.0 / head_width)
    angles = positions.astype(jnp.float32)[:, None] * freqs[None, :]
    return (jnp.cos(angles), jnp.sin(angles))

def rotate_halves(heads_in, cosine, sine):
    half_width = heads_in.shape[-1] // 2
    front_half = heads_in[..., :half_width]
    back_half = heads_in[..., half_width:]
    cos_rows = cosine[:, None, :]
    sin_rows = sine[:, None, :]
    return jnp.concatenate([front_half * cos_rows - back_half * sin_rows, back_half * cos_rows + front_half * sin_rows], axis=-1)

def head_prepare(raw, gain, cosine, sine):
    head_width = gain.shape[0]
    shaped = raw.reshape(raw.shape[:-1] + (raw.shape[-1] // head_width, head_width))
    return rotate_halves(rms_scale(shaped, gain), cosine, sine)

def swiglu(gate, upper):
    return jax.nn.silu(gate) * upper

def block_scores(query_block, keys, row_start):
    scale = queries_scale(query_block)
    scores = jnp.einsum('qhd,khd->hqk', query_block.astype(jnp.float32), keys.astype(jnp.float32)) * scale
    row_ids = row_start + jnp.arange(query_block.shape[0])
    col_ids = jnp.arange(keys.shape[0])
    allowed = col_ids[None, :] <= row_ids[:, None]
    return jnp.where(allowed[None, :, :], scores, -1e+30)

def queries_scale(query_block):
    return 1.0 / query_block.shape[-1] ** 0.5

def attend(queries, keys, values):
    length = queries.shape[0]
    block_rows = min(512, length)
    outputs = []
    totals = []
    for block_index in range(length // block_rows):
        start = block_index * block_rows
        scores = block_scores(queries[start:start + block_rows], keys, start)
        peak = lax.optimization_barrier(jnp.max(scores, axis=-1, keepdims=True))
        log_total = peak + jnp.log(lax.optimization_barrier(jnp.sum(jnp.exp(scores - peak), axis=-1, keepdims=True)))
        probs = jnp.exp(scores - log_total).astype(jnp.bfloat16)
        block_out = jnp.einsum('hqk,khd->qhd', probs.astype(jnp.float32), values.astype(jnp.float32))
        outputs.append(block_out.astype(jnp.bfloat16))
        totals.append(log_total[..., 0])
    return (jnp.concatenate(outputs, axis=0), jnp.concatenate(totals, axis=1))

def attend_grad(queries, keys, values, outputs, totals, out_grad):
    length = queries.shape[0]
    block_rows = min(512, length)
    scale = queries_scale(queries)
    key_acc = jnp.zeros(keys.shape, jnp.float32)
    value_acc = jnp.zeros(values.shape, jnp.float32)
    query_parts = []
    keys32 = keys.astype(jnp.float32)
    values32 = values.astype(jnp.float32)
    for block_index in range(length // block_rows):
        start = block_index * block_rows
        query_block = queries[start:start + block_rows]
        scores = block_scores(query_block, keys, start)
        probs = jnp.exp(scores - totals[:, start:start + block_rows][..., None])
        grad_block = out_grad[start:start + block_rows].astype(jnp.float32)
        value_acc = value_acc + jnp.einsum('hqk,qhd->khd', probs.astype(jnp.bfloat16).astype(jnp.float32), grad_block)
        prob_grad = jnp.einsum('qhd,khd->hqk', grad_block, values32)
        delta = lax.optimization_barrier(jnp.sum(grad_block * outputs[start:start + block_rows].astype(jnp.float32), axis=-1)).T
        score_grad = (probs * (prob_grad - delta[..., None])).astype(jnp.bfloat16).astype(jnp.float32)
        query_parts.append((jnp.einsum('hqk,khd->qhd', score_grad, keys32) * scale).astype(jnp.bfloat16))
        key_acc = key_acc + jnp.einsum('hqk,qhd->khd', score_grad, query_block.astype(jnp.float32)) * scale
    return (jnp.concatenate(query_parts, axis=0), key_acc.astype(jnp.bfloat16), value_acc.astype(jnp.bfloat16))

def reference(block_input, operator_gain, query_weight, key_weight, value_weight, output_weight, feedforward_gain, gate_weight, up_weight, down_weight, query_gain, key_gain, cotangent):
    head_width = query_gain.shape[0]
    group = H // KV
    length = block_input.shape[1]
    cosine, sine = rotary_tables(jnp.arange(length), head_width)
    operator_scale = operator_gain.astype(jnp.float32)
    feedforward_scale = feedforward_gain.astype(jnp.float32)
    query_scale = query_gain.astype(jnp.float32)
    key_scale = key_gain.astype(jnp.float32)

    def prepare(raw, gain):
        return head_prepare(raw, gain, cosine, sine)

    def one_sequence(carry, pair):
        tokens, upstream = pair
        input_flat = tokens.astype(jnp.float32)
        norm_one, norm_one_back = jax.vjp(rms_scale, input_flat, operator_scale)
        normed_input = norm_one.astype(jnp.bfloat16)
        query_raw = jnp.dot(normed_input, query_weight, preferred_element_type=jnp.float32)
        key_raw = jnp.dot(normed_input, key_weight, preferred_element_type=jnp.float32)
        value_raw = jnp.dot(normed_input, value_weight, preferred_element_type=jnp.float32)
        query_f32, query_back = jax.vjp(prepare, query_raw, query_scale)
        key_f32, key_back = jax.vjp(prepare, key_raw, key_scale)
        queries = query_f32.astype(jnp.bfloat16)
        keys = jnp.repeat(key_f32.astype(jnp.bfloat16), group, axis=1)
        values = jnp.repeat(value_raw.astype(jnp.bfloat16).reshape(length, KV, head_width), group, axis=1)
        head_out, head_total = attend(queries, keys, values)
        attended = head_out.reshape(length, H * head_width)
        hidden = input_flat + jnp.dot(attended, output_weight, preferred_element_type=jnp.float32)
        norm_two, norm_two_back = jax.vjp(rms_scale, hidden, feedforward_scale)
        normed_hidden = norm_two.astype(jnp.bfloat16)
        gate = jnp.dot(normed_hidden, gate_weight, preferred_element_type=jnp.float32)
        upper = jnp.dot(normed_hidden, up_weight, preferred_element_type=jnp.float32)
        act_f32, act_back = jax.vjp(swiglu, gate, upper)
        activation = act_f32.astype(jnp.bfloat16)
        output_f32 = hidden + jnp.dot(activation, down_weight, preferred_element_type=jnp.float32)
        block_output = output_f32.astype(jnp.bfloat16)
        down_grad = jnp.dot(activation.T, upstream, preferred_element_type=jnp.float32)
        act_grad = jnp.dot(upstream, down_weight.T, preferred_element_type=jnp.float32)
        gate_grad, upper_grad = act_back(act_grad)
        gate_grad = gate_grad.astype(jnp.bfloat16)
        upper_grad = upper_grad.astype(jnp.bfloat16)
        gate_weight_grad = jnp.dot(normed_hidden.T, gate_grad, preferred_element_type=jnp.float32)
        up_weight_grad = jnp.dot(normed_hidden.T, upper_grad, preferred_element_type=jnp.float32)
        normed_hidden_grad = jnp.dot(gate_grad, gate_weight.T, preferred_element_type=jnp.float32) + jnp.dot(upper_grad, up_weight.T, preferred_element_type=jnp.float32)
        hidden_norm_grad, feedforward_gain_grad = norm_two_back(normed_hidden_grad)
        hidden_grad = upstream.astype(jnp.float32) + hidden_norm_grad
        hidden_grad_b = hidden_grad.astype(jnp.bfloat16)
        output_weight_grad = jnp.dot(attended.T, hidden_grad_b, preferred_element_type=jnp.float32)
        attended_grad = jnp.dot(hidden_grad_b, output_weight.T, preferred_element_type=jnp.float32).astype(jnp.bfloat16).reshape(length, H, head_width)
        head_qgrad, head_kgrad, head_vgrad = attend_grad(queries, keys, values, head_out, head_total, attended_grad)
        key_sum = head_kgrad.astype(jnp.float32).reshape(length, KV, group, head_width).sum(axis=2)
        value_sum = head_vgrad.astype(jnp.float32).reshape(length, KV, group, head_width).sum(axis=2)
        query_pre, query_gain_grad = query_back(head_qgrad.astype(jnp.float32))
        key_pre, key_gain_grad = key_back(key_sum)
        query_raw_grad = query_pre.astype(jnp.bfloat16)
        key_raw_grad = key_pre.astype(jnp.bfloat16)
        value_raw_grad = value_sum.astype(jnp.bfloat16).reshape(length, KV * head_width)
        query_weight_grad = jnp.dot(normed_input.T, query_raw_grad, preferred_element_type=jnp.float32)
        key_weight_grad = jnp.dot(normed_input.T, key_raw_grad, preferred_element_type=jnp.float32)
        value_weight_grad = jnp.dot(normed_input.T, value_raw_grad, preferred_element_type=jnp.float32)
        normed_input_grad = jnp.dot(query_raw_grad, query_weight.T, preferred_element_type=jnp.float32) + jnp.dot(key_raw_grad, key_weight.T, preferred_element_type=jnp.float32) + jnp.dot(value_raw_grad, value_weight.T, preferred_element_type=jnp.float32)
        input_norm_grad, operator_gain_grad = norm_one_back(normed_input_grad)
        input_grad = hidden_grad + input_norm_grad
        grads = (operator_gain_grad, query_weight_grad, key_weight_grad, value_weight_grad, output_weight_grad, feedforward_gain_grad, gate_weight_grad, up_weight_grad, down_grad, query_gain_grad, key_gain_grad)
        carry = tuple((running + latest for running, latest in zip(carry, grads)))
        return (carry, (block_output, input_grad))
    initial = tuple((jnp.zeros(param.shape, jnp.float32) for param in (operator_gain, query_weight, key_weight, value_weight, output_weight, feedforward_gain, gate_weight, up_weight, down_weight, query_gain, key_gain)))
    totals, (outputs, input_grads) = lax.scan(one_sequence, initial, (block_input, cotangent))
    return (outputs, input_grads, totals[0], totals[1], totals[2], totals[3], totals[4], totals[5], totals[6], totals[7], totals[8], totals[9], totals[10])
```

```python
import jax
import jax.numpy as jnp
from jax import lax
from jax.sharding import PartitionSpec as P

EPS = 1e-05
THETA = 1000000.0


def rms_scale(values_in, gain):
    return (
        values_in * lax.rsqrt(jnp.mean(values_in * values_in, axis=-1, keepdims=True) + EPS) * gain
    )


def rotary_tables(positions, head_width):
    half_width = head_width // 2
    freqs = THETA ** (-jnp.arange(half_width).astype(jnp.float32) * 2.0 / head_width)
    angles = positions.astype(jnp.float32)[:, None] * freqs[None, :]
    return (jnp.cos(angles), jnp.sin(angles))


def rotate_halves(heads_in, cosine, sine):
    half_width = heads_in.shape[-1] // 2
    front_half = heads_in[..., :half_width]
    back_half = heads_in[..., half_width:]
    cos_rows = cosine[:, None, :]
    sin_rows = sine[:, None, :]
    return jnp.concatenate(
        [
            front_half * cos_rows - back_half * sin_rows,
            back_half * cos_rows + front_half * sin_rows,
        ],
        axis=-1,
    )


def head_prepare(raw, gain, cosine, sine):
    head_width = gain.shape[0]
    shaped = raw.reshape(raw.shape[:-1] + (raw.shape[-1] // head_width, head_width))
    return rotate_halves(rms_scale(shaped, gain), cosine, sine)


def swiglu(gate, upper):
    return jax.nn.silu(gate) * upper


def contract(left, right, left_dim, right_dim):
    return lax.dot_general(
        left, right, (((left_dim,), (right_dim,)), ((), ())), preferred_element_type=jnp.float32
    )


def block_scores(query_block, keys, query_pos, key_pos):
    scale = 1.0 / query_block.shape[-1] ** 0.5
    scores = (
        jnp.einsum("qhd,khd->hqk", query_block, keys, preferred_element_type=jnp.float32) * scale
    )
    allowed = key_pos[None, :] <= query_pos[:, None]
    return jnp.where(allowed[None, :, :], scores, -1e30)


def attend(queries, keys, values, positions):
    length = queries.shape[0]
    block_rows = min(512, length)
    outputs = []
    totals = []
    for start in range(0, length, block_rows):
        rows = slice(start, start + block_rows)
        scores = block_scores(queries[rows], keys, positions[rows], positions)
        peak = jnp.max(scores, axis=-1, keepdims=True)
        log_total = peak + jnp.log(jnp.sum(jnp.exp(scores - peak), axis=-1, keepdims=True))
        probs = jnp.exp(scores - log_total).astype(jnp.bfloat16)
        block_out = jnp.einsum("hqk,khd->qhd", probs, values, preferred_element_type=jnp.float32)
        outputs.append(block_out.astype(jnp.bfloat16))
        totals.append(log_total[..., 0])
    return (jnp.concatenate(outputs, axis=0), jnp.concatenate(totals, axis=1))


def attend_grad(queries, keys, values, outputs, totals, out_grad, positions):
    length = queries.shape[0]
    block_rows = min(512, length)
    scale = 1.0 / queries.shape[-1] ** 0.5
    key_acc = jnp.zeros(keys.shape, jnp.float32)
    value_acc = jnp.zeros(values.shape, jnp.float32)
    query_parts = []
    for start in range(0, length, block_rows):
        rows = slice(start, start + block_rows)
        query_block = queries[rows]
        scores = block_scores(query_block, keys, positions[rows], positions)
        probs = jnp.exp(scores - totals[:, rows][..., None])
        grad_block = out_grad[rows]
        value_acc = value_acc + jnp.einsum(
            "hqk,qhd->khd",
            probs.astype(jnp.bfloat16),
            grad_block,
            preferred_element_type=jnp.float32,
        )
        prob_grad = jnp.einsum(
            "qhd,khd->hqk", grad_block, values, preferred_element_type=jnp.float32
        )
        delta = jnp.sum(
            grad_block.astype(jnp.float32) * outputs[rows].astype(jnp.float32),
            axis=-1,
        ).T
        score_grad = (probs * (prob_grad - delta[..., None])).astype(jnp.bfloat16)
        query_parts.append(
            (
                jnp.einsum("hqk,khd->qhd", score_grad, keys, preferred_element_type=jnp.float32)
                * scale
            ).astype(jnp.bfloat16)
        )
        key_acc = (
            key_acc
            + jnp.einsum(
                "hqk,qhd->khd", score_grad, query_block, preferred_element_type=jnp.float32
            )
            * scale
        )
    return (
        jnp.concatenate(query_parts, axis=0),
        key_acc.astype(jnp.bfloat16),
        value_acc.astype(jnp.bfloat16),
    )


def shift(array, axis_name, step):
    size = lax.axis_size(axis_name)
    return lax.ppermute(array, axis_name, [(i, (i + step) % size) for i in range(size)])


def around(array, axis_name, dim):
    size = lax.axis_size(axis_name)
    return jnp.concatenate(
        [array] + [shift(array, axis_name, step) for step in range(1, size)], axis=dim
    )


def group_rows(array):
    return around(around(array, "ctx", 1), "tensor", 1)


def sum_around(array, axis_name):
    size = lax.axis_size(axis_name)
    part = array.shape[1] // size
    total = array[:, :part].astype(jnp.float32)
    for step in range(1, size):
        piece = array[:, step * part : (step + 1) * part].astype(jnp.bfloat16)
        total = total + shift(piece, axis_name, -step).astype(jnp.float32)
    return total


def group_sum(array):
    return sum_around(sum_around(array, "tensor"), "ctx")


def in_order(array, axis_name, dim):
    size = lax.axis_size(axis_name)
    me = lax.axis_index(axis_name)
    width = array.shape[dim]
    shape = list(array.shape)
    shape[dim] = width * size
    out = jnp.zeros(shape, array.dtype)
    for step in range(size):
        piece = array if step == 0 else shift(array, axis_name, step)
        owner = lax.rem(me - step + size, size)
        out = lax.dynamic_update_slice_in_dim(out, piece, owner * width, dim)
    return out


def ring_index(place, size):
    if size % 2:
        return place
    turn = size // 2
    return jnp.where(place < turn, 2 * place, 2 * (size - 1 - place) + 1)


def ring_place(index, size):
    if size % 2:
        return index
    return jnp.where(index % 2 == 0, index // 2, size - 1 - index // 2)


def ring_order(size):
    if size % 2:
        return list(range(size))
    return [2 * i for i in range(size // 2)] + [2 * i + 1 for i in reversed(range(size // 2))]


def ring_shift(array, axis_name, step):
    size = lax.axis_size(axis_name)
    order = ring_order(size)
    pairs = [(order[i], order[(i + step) % size]) for i in range(size)]
    return lax.ppermute(array, axis_name, pairs)


def ring_gather(shard, axis_name, dim=0):
    size = lax.axis_size(axis_name)
    place = ring_place(lax.axis_index(axis_name), size)
    shape = list(shard.shape)
    shape[dim] *= size
    half = shard.shape[0] // 2
    out = jnp.zeros(shape, shard.dtype)

    def put(out, piece, at, offset):
        owner = ring_index(lax.rem(at + size, size), size)
        starts = [offset, 0]
        starts[dim] += owner * shard.shape[dim]
        return lax.dynamic_update_slice(out, piece, starts)

    out = put(out, shard, place, 0)
    rightward = leftward = shard
    for step in range(1, (size + 1) // 2):
        rightward = ring_shift(rightward, axis_name, 1)
        leftward = ring_shift(leftward, axis_name, -1)
        out = put(out, rightward, place - step, 0)
        out = put(out, leftward, place + step, 0)
    if size % 2 == 0:
        rightward = ring_shift(rightward[:half], axis_name, 1)
        leftward = ring_shift(leftward[half:], axis_name, -1)
        out = put(out, rightward, place + size // 2, 0)
        out = put(out, leftward, place + size // 2, half)
    return out, rightward


def ring_scatter(piece_for, axis_name):
    size = lax.axis_size(axis_name)
    place = ring_place(lax.axis_index(axis_name), size)

    def piece(offset):
        return piece_for(ring_index(lax.rem(place + offset + size, size), size))

    mine = piece(0).astype(jnp.float32)
    if size == 1:
        return mine
    half = mine.shape[0] // 2
    far = size // 2
    bf16 = jnp.bfloat16
    f32 = jnp.float32
    if size % 2 == 0:
        across = piece(far)
        rightward = ring_shift(across[:half].astype(bf16), axis_name, 1).astype(f32)
        leftward = ring_shift(across[half:].astype(bf16), axis_name, -1).astype(f32)
        zero = jnp.zeros_like(mine[:half])
        rightward = jnp.concatenate([rightward, zero], axis=0)
        leftward = jnp.concatenate([zero, leftward], axis=0)
        steps = far - 1
    else:
        rightward = leftward = jnp.zeros_like(mine)
        steps = far
    for step in range(steps, 0, -1):
        rightward = ring_shift((rightward + piece(step)).astype(bf16), axis_name, 1).astype(f32)
        leftward = ring_shift((leftward + piece(-step)).astype(bf16), axis_name, -1).astype(f32)
    return mine + rightward + leftward


def part_of(array, dim, count, start):
    return lax.dynamic_slice_in_dim(array, start, count, dim)


def shards(
    block_input,
    operator_gain,
    query_weight,
    key_weight,
    value_weight,
    output_weight,
    feedforward_gain,
    gate_weight,
    up_weight,
    down_weight,
    query_gain,
    key_gain,
    cotangent,
):
    bf16 = jnp.bfloat16
    f32 = jnp.float32
    fsdp = lax.axis_size("fsdp")
    ctx = lax.axis_size("ctx")
    tensor = lax.axis_size("tensor")
    me_c = lax.axis_index("ctx")
    me_t = lax.axis_index("tensor")
    seqs, tok_here, width = block_input.shape
    quarter = tok_here // tensor
    tokens = tok_here * ctx
    rows = seqs * tokens
    gain_rows = query_gain.shape[0]
    head_width = gain_rows * fsdp
    heads_shard = query_weight.shape[1] // head_width
    kv_shard = key_weight.shape[1] // head_width
    spread = heads_shard // kv_shard
    heads = heads_shard // ctx
    kv = max(1, kv_shard // ctx)
    group = heads // kv
    copies = max(1, ctx // kv_shard)
    q_cols = heads * head_width
    kv_cols = kv * head_width
    kv_start = ((me_c * heads) // spread) * head_width
    hidden_units = gate_weight.shape[1] // ctx
    shard_rows = query_weight.shape[0]

    gains = jnp.stack(
        [
            operator_gain,
            feedforward_gain,
            jnp.pad(query_gain, (0, shard_rows - gain_rows)),
            jnp.pad(key_gain, (0, shard_rows - gain_rows)),
        ],
        axis=1,
    )
    attention_pack = jnp.concatenate(
        [
            part_of(query_weight, 1, q_cols, me_c * q_cols),
            part_of(key_weight, 1, kv_cols, kv_start),
            part_of(value_weight, 1, kv_cols, kv_start),
            part_of(output_weight, 0, q_cols, me_c * q_cols).T,
            jnp.pad(gains, ((0, 0), (0, 124))),
        ],
        axis=1,
    )
    gate_up_shard = jnp.concatenate(
        [
            part_of(gate_weight, 1, hidden_units, me_c * hidden_units),
            part_of(up_weight, 1, hidden_units, me_c * hidden_units),
        ],
        axis=1,
    )
    down_shard = part_of(down_weight, 0, hidden_units, me_c * hidden_units)
    attention_full, last = ring_gather(attention_pack, "fsdp")
    gate_up_shard, last = lax.optimization_barrier((gate_up_shard, last))
    gate_up_full, last = ring_gather(gate_up_shard, "fsdp")
    down_shard, last = lax.optimization_barrier((down_shard, last))
    down_full, _ = ring_gather(down_shard, "fsdp", 1)
    qkv_cols = q_cols + 2 * kv_cols
    qkv_full = attention_full[:, :qkv_cols]
    output_full = attention_full[:, qkv_cols : qkv_cols + q_cols]
    gains_full = attention_full[:, qkv_cols + q_cols :].astype(f32)
    operator_scale = gains_full[:, 0]
    feedforward_scale = gains_full[:, 1]
    query_scale = gains_full[:, 2].reshape(fsdp, shard_rows)[:, :gain_rows].reshape(-1)
    key_scale = gains_full[:, 3].reshape(fsdp, shard_rows)[:, :gain_rows].reshape(-1)

    own_input = part_of(block_input, 1, quarter, me_t * quarter)
    all_input = group_rows(own_input).reshape(rows, width)
    upstream_own = part_of(cotangent, 1, quarter, me_t * quarter)
    upstream = group_rows(upstream_own).reshape(rows, width)

    ctx_order = lax.rem(me_c - jnp.arange(ctx) + ctx, ctx)
    tensor_order = lax.rem(me_t - jnp.arange(tensor) + tensor, tensor)
    positions = (
        tensor_order[:, None, None] * quarter
        + ctx_order[None, :, None] * tok_here
        + jnp.arange(quarter)[None, None, :]
    ).reshape(tokens)
    cosine, sine = rotary_tables(positions, head_width)

    def prepare(raw, gain):
        return head_prepare(raw, gain, cosine, sine)

    normed_input = rms_scale(all_input.astype(f32), operator_scale).astype(bf16)
    qkv_raw = jnp.dot(normed_input, qkv_full, preferred_element_type=f32).reshape(seqs, tokens, -1)
    query_f32, query_back = jax.vjp(prepare, qkv_raw[..., :q_cols], query_scale)
    key_f32, key_back = jax.vjp(prepare, qkv_raw[..., q_cols : q_cols + kv_cols], key_scale)
    queries = query_f32.astype(bf16)
    keys = jnp.repeat(key_f32.astype(bf16), group, axis=2)
    values = jnp.repeat(
        qkv_raw[..., q_cols + kv_cols :].astype(bf16).reshape(seqs, tokens, kv, head_width),
        group,
        axis=2,
    )
    attended, totals = jax.vmap(attend, in_axes=(0, 0, 0, None))(queries, keys, values, positions)
    attended_rows = attended.reshape(rows, q_cols)
    attention_part = contract(attended_rows, output_full, 1, 1).reshape(seqs, tokens, width)
    own_f32 = own_input.astype(f32)
    hidden = own_f32 + group_sum(attention_part)
    norm_two, norm_two_back = jax.vjp(lambda v: rms_scale(v, feedforward_scale), hidden)
    normed_hidden = group_rows(norm_two.astype(bf16)).reshape(rows, width)
    gate_up = jnp.dot(normed_hidden, gate_up_full, preferred_element_type=f32)
    act_f32, act_back = jax.vjp(swiglu, gate_up[:, :hidden_units], gate_up[:, hidden_units:])
    activation = act_f32.astype(bf16)
    act_grad = contract(upstream, down_full, 1, 1)
    gate_grad, up_grad = act_back(act_grad)
    gate_up_grad = jnp.concatenate([gate_grad.astype(bf16), up_grad.astype(bf16)], axis=1)
    hidden_part = contract(gate_up_grad, gate_up_full, 1, 1).reshape(seqs, tokens, width)
    down_grad = contract(activation, upstream, 0, 0).astype(bf16)
    gate_up_weight_grad = contract(normed_hidden, gate_up_grad, 0, 0).astype(bf16)
    normed_hidden_grad = group_sum(hidden_part)
    down_share = ring_scatter(
        lambda owner: part_of(down_grad, 1, shard_rows, owner * shard_rows), "fsdp"
    ).astype(bf16)
    gate_up_weight_grad, down_share = lax.optimization_barrier((gate_up_weight_grad, down_share))
    gate_up_share = ring_scatter(
        lambda owner: part_of(gate_up_weight_grad, 0, shard_rows, owner * shard_rows), "fsdp"
    ).astype(bf16)
    down_part = jnp.dot(activation, down_full, preferred_element_type=f32).reshape(seqs, tokens, width)
    own_output = (hidden + group_sum(down_part)).astype(bf16)
    block_output = in_order(own_output, "tensor", 1)

    (hidden_norm_grad,) = norm_two_back(normed_hidden_grad)
    hidden_grad = upstream_own.astype(f32) + hidden_norm_grad
    hidden_grad_b = group_rows(hidden_grad.astype(bf16)).reshape(rows, width)
    output_weight_grad = contract(hidden_grad_b, attended_rows, 0, 0)
    attended_grad = (
        jnp.dot(hidden_grad_b, output_full, preferred_element_type=f32)
        .astype(bf16)
        .reshape(seqs, tokens, heads, head_width)
    )
    query_hgrad, key_hgrad, value_hgrad = jax.vmap(attend_grad, in_axes=(0, 0, 0, 0, 0, 0, None))(
        queries, keys, values, attended, totals, attended_grad, positions
    )

    def head_sum(grad):
        return grad.astype(f32).reshape(seqs, tokens, kv, group, head_width).sum(axis=3)

    query_pre, query_gain_grad = query_back(query_hgrad.astype(f32))
    key_pre, key_gain_grad = key_back(head_sum(key_hgrad))
    qkv_raw_grad = jnp.concatenate(
        [
            query_pre.astype(bf16).reshape(rows, q_cols),
            key_pre.astype(bf16).reshape(rows, kv_cols),
            head_sum(value_hgrad).astype(bf16).reshape(rows, kv_cols),
        ],
        axis=1,
    )
    input_part = contract(qkv_raw_grad, qkv_full, 1, 1).reshape(seqs, tokens, width)
    normed_input_grad = group_sum(input_part)
    qkv_weight_grad = contract(normed_input, qkv_raw_grad, 0, 0)
    gain_grads = jnp.stack([query_gain_grad, key_gain_grad], axis=1).reshape(fsdp, gain_rows, 2)
    gain_grads = jnp.pad(
        gain_grads, ((0, 0), (0, shard_rows - gain_rows), (0, 126))
    ).reshape(width, 128)
    attention_grad = jnp.concatenate(
        [qkv_weight_grad, output_weight_grad, gain_grads], axis=1
    ).astype(bf16)
    attention_grad, gate_up_share = lax.optimization_barrier((attention_grad, gate_up_share))
    attention_share = ring_scatter(
        lambda owner: part_of(attention_grad, 0, shard_rows, owner * shard_rows), "fsdp"
    ).astype(bf16)
    _, norm_one_back = jax.vjp(lambda v: rms_scale(v, operator_scale), own_f32)
    (input_norm_grad,) = norm_one_back(normed_input_grad)
    input_grad = in_order(hidden_grad + input_norm_grad, "tensor", 1)

    def ctx_parts(share):
        size = lax.axis_size("ctx")
        parts = jnp.zeros((size,) + share.shape, share.dtype)
        for step in range(size):
            piece = share if step == 0 else shift(share, "ctx", step)
            owner = lax.rem(me_c - step + size, size)
            parts = lax.dynamic_update_slice(parts, piece[None], (owner, 0, 0))
        return parts.astype(f32)

    def columns(parts):
        return jnp.moveaxis(parts, 0, 1).reshape(parts.shape[1], -1)

    attention_parts = ctx_parts(attention_share)
    gate_up_parts = ctx_parts(gate_up_share)
    down_parts = ctx_parts(down_share)

    def head_columns(parts):
        every = columns(parts)
        if copies == 1:
            return every
        return every.reshape(shard_rows, kv_shard, copies, head_width).sum(axis=2).reshape(
            shard_rows, -1
        )

    query_weight_grad = columns(attention_parts[:, :, :q_cols])
    key_weight_grad = head_columns(attention_parts[:, :, q_cols : q_cols + kv_cols])
    value_weight_grad = head_columns(attention_parts[:, :, q_cols + kv_cols : qkv_cols])
    gate_weight_grad = columns(gate_up_parts[:, :, :hidden_units])
    up_weight_grad = columns(gate_up_parts[:, :, hidden_units:])
    gain_parts = attention_parts[:, :, qkv_cols + q_cols : qkv_cols + q_cols + 2].sum(axis=0)

    def gain_part(pairs, gain):
        total = 0.0
        for weight, grad in pairs:
            total = total + jnp.sum(weight.astype(f32) * grad, axis=1)
        return total / gain.astype(f32)

    gain_columns = jnp.concatenate(
        [
            gain_part(
                [
                    (query_weight, query_weight_grad),
                    (key_weight, key_weight_grad),
                    (value_weight, value_weight_grad),
                ],
                operator_gain,
            )[:, None],
            gain_part(
                [(gate_weight, gate_weight_grad), (up_weight, up_weight_grad)], feedforward_gain
            )[:, None],
            gain_parts,
        ],
        axis=1,
    )
    gain_totals = gain_columns
    for step in range(1, tensor):
        gain_totals = gain_totals + shift(gain_columns, "tensor", step)

    return (
        block_output,
        input_grad,
        gain_totals[:, 0],
        query_weight_grad,
        key_weight_grad,
        value_weight_grad,
        jnp.swapaxes(attention_parts[:, :, qkv_cols : qkv_cols + q_cols], 1, 2).reshape(
            -1, shard_rows
        ),
        gain_totals[:, 1],
        gate_weight_grad,
        up_weight_grad,
        down_parts.reshape(-1, shard_rows),
        gain_totals[:gain_rows, 2],
        gain_totals[:gain_rows, 3],
    )


def solution(mesh):
    in_specs = (
        P("fsdp", "ctx", None),
        P("fsdp"),
        P("fsdp", "tensor"),
        P("fsdp", "tensor"),
        P("fsdp", "tensor"),
        P("tensor", "fsdp"),
        P("fsdp"),
        P("fsdp", "tensor"),
        P("fsdp", "tensor"),
        P("tensor", "fsdp"),
        P("fsdp"),
        P("fsdp"),
        P("fsdp", "ctx", None),
    )
    out_specs = (
        P("fsdp", "ctx", None),
        P("fsdp", "ctx", None),
        P("fsdp"),
        P("fsdp", "tensor"),
        P("fsdp", "tensor"),
        P("fsdp", "tensor"),
        P("tensor", "fsdp"),
        P("fsdp"),
        P("fsdp", "tensor"),
        P("fsdp", "tensor"),
        P("tensor", "fsdp"),
        P("fsdp"),
        P("fsdp"),
    )
    return jax.shard_map(shards, mesh=mesh, in_specs=in_specs, out_specs=out_specs, check_vma=False)
```

```python
import jax
import jax.numpy as jnp
from jax import lax
from jax.experimental import pallas as pl
from jax.experimental.pallas import tpu as pltpu
from jax.sharding import PartitionSpec as P

EPS = 1e-05
THETA = 1000000.0


def rms_scale(values_in, gain):
    return (
        values_in * lax.rsqrt(jnp.mean(values_in * values_in, axis=-1, keepdims=True) + EPS) * gain
    )


def rotary_tables(positions, head_width):
    half_width = head_width // 2
    freqs = THETA ** (-jnp.arange(half_width).astype(jnp.float32) * 2.0 / head_width)
    angles = positions.astype(jnp.float32)[:, None] * freqs[None, :]
    return (jnp.cos(angles), jnp.sin(angles))


def rotate_halves(heads_in, cosine, sine):
    half_width = heads_in.shape[-1] // 2
    front_half = heads_in[..., :half_width]
    back_half = heads_in[..., half_width:]
    cos_rows = cosine[:, None, :]
    sin_rows = sine[:, None, :]
    return jnp.concatenate(
        [
            front_half * cos_rows - back_half * sin_rows,
            back_half * cos_rows + front_half * sin_rows,
        ],
        axis=-1,
    )


def head_prepare(raw, gain, cosine, sine):
    head_width = gain.shape[0]
    shaped = raw.reshape(raw.shape[:-1] + (raw.shape[-1] // head_width, head_width))
    return rotate_halves(rms_scale(shaped, gain), cosine, sine)


def swiglu(gate, upper):
    return jax.nn.silu(gate) * upper


def contract(left, right, left_dim, right_dim):
    return lax.dot_general(
        left, right, (((left_dim,), (right_dim,)), ((), ())), preferred_element_type=jnp.float32
    )


def block_scores(query_block, keys, query_pos, key_pos):
    scale = 1.0 / query_block.shape[-1] ** 0.5
    scores = (
        jnp.einsum("qhd,khd->hqk", query_block, keys, preferred_element_type=jnp.float32) * scale
    )
    allowed = key_pos[None, :] <= query_pos[:, None]
    return jnp.where(allowed[None, :, :], scores, -1e30)


def attend(queries, keys, values, positions):
    length = queries.shape[0]
    block_rows = min(512, length)
    outputs = []
    totals = []
    for start in range(0, length, block_rows):
        rows = slice(start, start + block_rows)
        scores = block_scores(queries[rows], keys, positions[rows], positions)
        peak = jnp.max(scores, axis=-1, keepdims=True)
        log_total = peak + jnp.log(jnp.sum(jnp.exp(scores - peak), axis=-1, keepdims=True))
        probs = jnp.exp(scores - log_total).astype(jnp.bfloat16)
        block_out = jnp.einsum("hqk,khd->qhd", probs, values, preferred_element_type=jnp.float32)
        outputs.append(block_out.astype(jnp.bfloat16))
        totals.append(log_total[..., 0])
    return (jnp.concatenate(outputs, axis=0), jnp.concatenate(totals, axis=1))


def attend_grad(queries, keys, values, outputs, totals, out_grad, positions):
    length = queries.shape[0]
    block_rows = min(512, length)
    scale = 1.0 / queries.shape[-1] ** 0.5
    key_acc = jnp.zeros(keys.shape, jnp.float32)
    value_acc = jnp.zeros(values.shape, jnp.float32)
    query_parts = []
    for start in range(0, length, block_rows):
        rows = slice(start, start + block_rows)
        query_block = queries[rows]
        scores = block_scores(query_block, keys, positions[rows], positions)
        probs = jnp.exp(scores - totals[:, rows][..., None])
        grad_block = out_grad[rows]
        value_acc = value_acc + jnp.einsum(
            "hqk,qhd->khd",
            probs.astype(jnp.bfloat16),
            grad_block,
            preferred_element_type=jnp.float32,
        )
        prob_grad = jnp.einsum(
            "qhd,khd->hqk", grad_block, values, preferred_element_type=jnp.float32
        )
        delta = jnp.sum(
            grad_block.astype(jnp.float32) * outputs[rows].astype(jnp.float32),
            axis=-1,
        ).T
        score_grad = (probs * (prob_grad - delta[..., None])).astype(jnp.bfloat16)
        query_parts.append(
            (
                jnp.einsum("hqk,khd->qhd", score_grad, keys, preferred_element_type=jnp.float32)
                * scale
            ).astype(jnp.bfloat16)
        )
        key_acc = (
            key_acc
            + jnp.einsum(
                "hqk,qhd->khd", score_grad, query_block, preferred_element_type=jnp.float32
            )
            * scale
        )
    return (
        jnp.concatenate(query_parts, axis=0),
        key_acc.astype(jnp.bfloat16),
        value_acc.astype(jnp.bfloat16),
    )


def shift(array, axis_name, step):
    size = lax.axis_size(axis_name)
    return lax.ppermute(array, axis_name, [(i, (i + step) % size) for i in range(size)])


def around(array, axis_name, dim):
    size = lax.axis_size(axis_name)
    return jnp.concatenate(
        [array] + [shift(array, axis_name, step) for step in range(1, size)], axis=dim
    )


def group_rows(array):
    return around(around(array, "ctx", 1), "tensor", 1)


def sum_around(array, axis_name):
    size = lax.axis_size(axis_name)
    part = array.shape[1] // size
    total = array[:, :part].astype(jnp.float32)
    for step in range(1, size):
        piece = array[:, step * part : (step + 1) * part].astype(jnp.bfloat16)
        total = total + shift(piece, axis_name, -step).astype(jnp.float32)
    return total


def group_sum(array):
    return sum_around(sum_around(array, "tensor"), "ctx")


def in_order(array, axis_name, dim):
    size = lax.axis_size(axis_name)
    me = lax.axis_index(axis_name)
    width = array.shape[dim]
    shape = list(array.shape)
    shape[dim] = width * size
    out = jnp.zeros(shape, array.dtype)
    for step in range(size):
        piece = array if step == 0 else shift(array, axis_name, step)
        owner = lax.rem(me - step + size, size)
        out = lax.dynamic_update_slice_in_dim(out, piece, owner * width, dim)
    return out


def ring_index(place, size):
    if size % 2:
        return place
    turn = size // 2
    return jnp.where(place < turn, 2 * place, 2 * (size - 1 - place) + 1)


def ring_place(index, size):
    if size % 2:
        return index
    return jnp.where(lax.rem(index, 2) == 0, lax.div(index, 2), size - 1 - lax.div(index, 2))


def ring_order(size):
    if size % 2:
        return list(range(size))
    return [2 * i for i in range(size // 2)] + [2 * i + 1 for i in reversed(range(size // 2))]


def ring_shift(array, axis_name, step):
    size = lax.axis_size(axis_name)
    order = ring_order(size)
    pairs = [(order[i], order[(i + step) % size]) for i in range(size)]
    return lax.ppermute(array, axis_name, pairs)


def ring_gather(shard, axis_name, dim=0):
    size = lax.axis_size(axis_name)
    place = ring_place(lax.axis_index(axis_name), size)
    shape = list(shard.shape)
    shape[dim] *= size
    half = shard.shape[0] // 2
    out = jnp.zeros(shape, shard.dtype)

    def put(out, piece, at, offset):
        owner = ring_index(lax.rem(at + size, size), size)
        starts = [offset, 0]
        starts[dim] += owner * shard.shape[dim]
        return lax.dynamic_update_slice(out, piece, starts)

    out = put(out, shard, place, 0)
    rightward = leftward = shard
    for step in range(1, (size + 1) // 2):
        rightward = ring_shift(rightward, axis_name, 1)
        leftward = ring_shift(leftward, axis_name, -1)
        out = put(out, rightward, place - step, 0)
        out = put(out, leftward, place + step, 0)
    if size % 2 == 0:
        rightward = ring_shift(rightward[:half], axis_name, 1)
        leftward = ring_shift(leftward[half:], axis_name, -1)
        out = put(out, rightward, place + size // 2, 0)
        out = put(out, leftward, place + size // 2, half)
    return out, rightward


def ring_scatter(piece_for, axis_name):
    size = lax.axis_size(axis_name)
    place = ring_place(lax.axis_index(axis_name), size)

    def piece(offset):
        return piece_for(ring_index(lax.rem(place + offset + size, size), size))

    mine = piece(0).astype(jnp.float32)
    if size == 1:
        return mine
    half = mine.shape[0] // 2
    far = size // 2
    bf16 = jnp.bfloat16
    f32 = jnp.float32
    if size % 2 == 0:
        across = piece(far)
        rightward = ring_shift(across[:half].astype(bf16), axis_name, 1).astype(f32)
        leftward = ring_shift(across[half:].astype(bf16), axis_name, -1).astype(f32)
        zero = jnp.zeros_like(mine[:half])
        rightward = jnp.concatenate([rightward, zero], axis=0)
        leftward = jnp.concatenate([zero, leftward], axis=0)
        steps = far - 1
    else:
        rightward = leftward = jnp.zeros_like(mine)
        steps = far
    for step in range(steps, 0, -1):
        rightward = ring_shift((rightward + piece(step)).astype(bf16), axis_name, 1).astype(f32)
        leftward = ring_shift((leftward + piece(-step)).astype(bf16), axis_name, -1).astype(f32)
    return mine + rightward + leftward


def other(axis_name, step):
    size = lax.axis_size(axis_name)
    return {axis_name: lax.rem(lax.axis_index(axis_name) + step + size, size)}


def send(source, target, send_sem, recv_sem, device):
    copy = pltpu.make_async_remote_copy(
        src_ref=source,
        dst_ref=target,
        send_sem=send_sem,
        recv_sem=recv_sem,
        device_id=device,
        device_id_type=pl.DeviceIdType.MESH,
    )
    copy.start()
    return copy


def ring_ends():
    size = lax.axis_size("fsdp")
    place = ring_place(lax.axis_index("fsdp"), size)

    def at(offset):
        return ring_index(lax.rem(place + offset + size, size), size)

    return at, ({"fsdp": at(1)}, {"fsdp": at(-1)})


def greet():
    _, ends = ring_ends()
    partners = list(ends)
    for axis_name in ("ctx", "tensor"):
        partners += [other(axis_name, step) for step in range(1, lax.axis_size(axis_name))]
    barrier = pltpu.get_barrier_semaphore()
    for device in partners:
        pl.semaphore_signal(
            barrier, inc=1, device_id=device, device_id_type=pl.DeviceIdType.MESH
        )
    pl.semaphore_wait(barrier, len(partners))


def start_kernel(
    pack_ref,
    input_ref,
    upstream_ref,
    full_ref,
    all_input_ref,
    all_upstream_ref,
    ring_send,
    ring_recv,
    ctx_send,
    ctx_recv,
    tensor_send,
    tensor_recv,
    local_sem,
):
    size = lax.axis_size("fsdp")
    ctx = lax.axis_size("ctx")
    tensor = lax.axis_size("tensor")
    me_t = lax.axis_index("tensor")
    far = size // 2
    rows = pack_ref.shape[0]
    sub_rows = rows // 2
    quarter = all_input_ref.shape[2]
    at, ends = ring_ends()
    greet()
    pairs = ((input_ref, all_input_ref), (upstream_ref, all_upstream_ref))

    def block(owner, sub):
        start = pl.multiple_of(owner * rows + sub * sub_rows, sub_rows)
        return full_ref.at[pl.ds(start, sub_rows)]

    sends = []
    arrivals = {}

    def ring_step(step):
        for sub in range(2):
            for way in range(2):
                if step == far and sub != way:
                    continue
                if step > 1:
                    arrivals.pop((way, step - 1, sub)).wait_recv()
                owner = at((1 - step) if way == 0 else (step - 1))
                source = (
                    pack_ref.at[pl.ds(sub * sub_rows, sub_rows)] if step == 1 else block(owner, sub)
                )
                copy = send(
                    source,
                    block(owner, sub),
                    ring_send.at[way, step - 1, sub],
                    ring_recv.at[way, step - 1, sub],
                    ends[way],
                )
                sends.append(copy)
                arrivals[way, step, sub] = copy

    def own_rows(source, step):
        quarter_at = lax.rem(me_t - step + tensor, tensor)
        return source.at[0, pl.ds(pl.multiple_of(quarter_at * quarter, quarter), quarter)]

    ring_step(1)
    crossed = {}
    locals_ = []
    for which, (source, target) in enumerate(pairs):
        for step in range(1, ctx):
            copy = send(
                own_rows(source, 0),
                target.at[0, step],
                ctx_send.at[which, step - 1],
                ctx_recv.at[which, step - 1],
                other("ctx", step),
            )
            sends.append(copy)
            crossed[which, step] = copy
    for which, (source, target) in enumerate(pairs):
        for step in range(tensor):
            copy = pltpu.make_async_copy(
                own_rows(source, step), target.at[step, 0], local_sem.at[which, step]
            )
            copy.start()
            locals_.append(copy)
    own_copy = pltpu.make_async_copy(
        pack_ref,
        full_ref.at[pl.ds(pl.multiple_of(at(0) * rows, rows), rows)],
        local_sem.at[2, 0],
    )
    own_copy.start()
    locals_.append(own_copy)
    handed = []

    def hand_over(which):
        _, target = pairs[which]
        for step in range(1, ctx):
            crossed[which, step].wait_recv()
            for core in range(1, tensor):
                copy = send(
                    target.at[0, step],
                    target.at[core, step],
                    tensor_send.at[which, core - 1, step - 1],
                    tensor_recv.at[which, core - 1, step - 1],
                    other("tensor", core),
                )
                sends.append(copy)
                handed.append(copy)

    for step in range(2, far + 1):
        if step == far:
            hand_over(0)
        ring_step(step)
    if far < 2:
        hand_over(0)
    hand_over(1)
    for copy in arrivals.values():
        copy.wait_recv()
    for copy in handed:
        copy.wait_recv()
    for copy in sends:
        copy.wait_send()
    for copy in locals_:
        copy.wait()


def start_gather(pack, block_input, cotangent):
    size = lax.axis_size("fsdp")
    ctx = lax.axis_size("ctx")
    tensor = lax.axis_size("tensor")
    far = size // 2
    rows, columns = pack.shape
    _, tok_here, width = block_input.shape
    every = (tensor, ctx, tok_here // tensor, width)
    anywhere = pl.BlockSpec(memory_space=pl.ANY)
    dma = pltpu.SemaphoreType.DMA
    return pl.pallas_call(
        start_kernel,
        out_shape=(
            jax.ShapeDtypeStruct((rows * size, columns), pack.dtype),
            jax.ShapeDtypeStruct(every, block_input.dtype),
            jax.ShapeDtypeStruct(every, cotangent.dtype),
        ),
        in_specs=[anywhere] * 3,
        out_specs=(anywhere,) * 3,
        scratch_shapes=[
            dma((2, far, 2)),
            dma((2, far, 2)),
            dma((2, ctx)),
            dma((2, ctx)),
            dma((2, tensor, ctx)),
            dma((2, tensor, ctx)),
            dma((3, tensor)),
        ],
        compiler_params=pltpu.CompilerParams(collective_id=0, has_side_effects=True),
        name="start_gather",
    )(pack, block_input, cotangent)


def add_rows(count, block_rows, body):
    def step(index, carry):
        body(pl.ds(pl.multiple_of(index * block_rows, block_rows), block_rows))
        return carry

    lax.fori_loop(0, count // block_rows, step, 0)


def finish_kernel(
    grad_ref,
    part_ref,
    parts_ref,
    total_ref,
    going,
    coming,
    share,
    core_going,
    core_coming,
    ctx_going,
    ctx_coming,
    ring_send,
    ring_recv,
    core_send,
    core_recv,
    ctx_send,
    ctx_recv,
    share_send,
    share_recv,
    local_sem,
):
    f32 = jnp.float32
    bf16 = jnp.bfloat16
    size = lax.axis_size("fsdp")
    ctx = lax.axis_size("ctx")
    tensor = lax.axis_size("tensor")
    me_c = lax.axis_index("ctx")
    far = size // 2
    rows = share.shape[0]
    sub_rows = rows // 2
    quarter = part_ref.shape[2]
    at, ends = ring_ends()
    greet()
    sends = []
    arrivals = {}

    def own_block(owner, sub):
        return pl.ds(pl.multiple_of(owner * rows + sub * sub_rows, sub_rows), sub_rows)

    def ring_step(step):
        for sub in range(2):
            for way in range(2):
                if step == 1 and sub != way:
                    continue
                ahead = far + 1 - step
                owner = at(ahead if way == 0 else -ahead)
                mine = own_block(owner, sub)
                if step == 1:
                    source = grad_ref.at[mine]
                else:
                    source = going.at[way, step - 2, sub]
                    if (way, step - 1, sub) in arrivals:
                        arrivals.pop((way, step - 1, sub)).wait_recv()
                        source[...] = (
                            grad_ref[mine, :].astype(f32)
                            + coming[way, step - 2, sub].astype(f32)
                        ).astype(bf16)
                    else:
                        source = grad_ref.at[mine]
                copy = send(
                    source,
                    coming.at[way, step - 1, sub],
                    ring_send.at[way, step - 1, sub],
                    ring_recv.at[way, step - 1, sub],
                    ends[way],
                )
                sends.append(copy)
                arrivals[way, step, sub] = copy

    ring_step(1)
    by_core = []
    for core in range(1, tensor):
        for step in range(ctx):

            def narrow(block, core=core, step=step):
                core_going[core - 1, step, block] = part_ref[core, step, block].astype(bf16)

            add_rows(quarter, 32, narrow)
        copy = send(
            core_going.at[core - 1],
            core_coming.at[core - 1],
            core_send.at[core - 1],
            core_recv.at[core - 1],
            other("tensor", -core),
        )
        sends.append(copy)
        by_core.append(copy)
    if far > 1:
        ring_step(2)
    for copy in by_core:
        copy.wait_recv()
    by_ctx = []
    for step in list(range(1, ctx)) + [0]:

        def total(block, step=step):
            value = part_ref[0, step, block]
            for core in range(1, tensor):
                value = value + core_coming[core - 1, step, block].astype(f32)
            if step == 0:
                total_ref[block] = value
            else:
                ctx_going[step - 1, block] = value.astype(bf16)

        add_rows(quarter, 32, total)
        if step > 0:
            copy = send(
                ctx_going.at[step - 1],
                ctx_coming.at[step - 1],
                ctx_send.at[step - 1],
                ctx_recv.at[step - 1],
                other("ctx", -step),
            )
            sends.append(copy)
            by_ctx.append(copy)
    for step in range(3, far + 1):
        ring_step(step)
    mine = at(0)
    for sub in range(2):
        value = grad_ref[own_block(mine, sub), :].astype(f32)
        for way in range(2):
            if (way, far, sub) in arrivals:
                arrivals.pop((way, far, sub)).wait_recv()
                value = value + coming[way, far - 1, sub].astype(f32)
        share[sub * sub_rows : (sub + 1) * sub_rows, :] = value.astype(bf16)
    shared = []
    for step in range(1, ctx):
        copy = send(
            share,
            parts_ref.at[me_c],
            share_send.at[step - 1],
            share_recv.at[step - 1],
            other("ctx", step),
        )
        sends.append(copy)
        shared.append(copy)
    keep = pltpu.make_async_copy(share, parts_ref.at[me_c], local_sem)
    keep.start()
    for step in range(1, ctx):
        by_ctx[step - 1].wait_recv()

        def gather(block, step=step):
            total_ref[block] += ctx_coming[step - 1, block].astype(f32)

        add_rows(quarter, 32, gather)
    for step in range(1, ctx):
        shared[step - 1].wait_recv()
    for copy in sends:
        copy.wait_send()
    keep.wait()


def finish_sums(grad, part):
    size = lax.axis_size("fsdp")
    tensor, ctx, quarter, width = part.shape
    far = size // 2
    rows, columns = grad.shape[0] // size, grad.shape[1]
    in_vmem = pl.BlockSpec(memory_space=pltpu.VMEM)
    anywhere = pl.BlockSpec(memory_space=pl.ANY)
    dma = pltpu.SemaphoreType.DMA
    bf16 = jnp.bfloat16
    return pl.pallas_call(
        finish_kernel,
        out_shape=(
            jax.ShapeDtypeStruct((ctx, rows, columns), bf16),
            jax.ShapeDtypeStruct((quarter, width), jnp.float32),
        ),
        in_specs=[in_vmem] * 2,
        out_specs=(anywhere, in_vmem),
        scratch_shapes=[
            pltpu.VMEM((2, max(1, far - 1), 2, rows // 2, columns), bf16),
            pltpu.VMEM((2, far, 2, rows // 2, columns), bf16),
            pltpu.VMEM((rows, columns), bf16),
            pltpu.VMEM((max(1, tensor - 1), ctx, quarter, width), bf16),
            pltpu.VMEM((max(1, tensor - 1), ctx, quarter, width), bf16),
            pltpu.VMEM((max(1, ctx - 1), quarter, width), bf16),
            pltpu.VMEM((max(1, ctx - 1), quarter, width), bf16),
            dma((2, far, 2)),
            dma((2, far, 2)),
            dma((tensor,)),
            dma((tensor,)),
            dma((ctx,)),
            dma((ctx,)),
            dma((ctx,)),
            dma((ctx,)),
            dma(()),
        ],
        compiler_params=pltpu.CompilerParams(
            collective_id=1, has_side_effects=True, vmem_limit_bytes=48 * 1024 * 1024
        ),
        name="finish_sums",
    )(grad, part)


def part_of(array, dim, count, start):
    return lax.dynamic_slice_in_dim(array, start, count, dim)


def shards(
    block_input,
    operator_gain,
    query_weight,
    key_weight,
    value_weight,
    output_weight,
    feedforward_gain,
    gate_weight,
    up_weight,
    down_weight,
    query_gain,
    key_gain,
    cotangent,
):
    bf16 = jnp.bfloat16
    f32 = jnp.float32
    fsdp = lax.axis_size("fsdp")
    ctx = lax.axis_size("ctx")
    tensor = lax.axis_size("tensor")
    me_c = lax.axis_index("ctx")
    me_t = lax.axis_index("tensor")
    seqs, tok_here, width = block_input.shape
    quarter = tok_here // tensor
    tokens = tok_here * ctx
    rows = seqs * tokens
    gain_rows = query_gain.shape[0]
    head_width = gain_rows * fsdp
    heads_shard = query_weight.shape[1] // head_width
    kv_shard = key_weight.shape[1] // head_width
    spread = heads_shard // kv_shard
    heads = heads_shard // ctx
    kv = max(1, kv_shard // ctx)
    group = heads // kv
    copies = max(1, ctx // kv_shard)
    q_cols = heads * head_width
    kv_cols = kv * head_width
    kv_start = ((me_c * heads) // spread) * head_width
    hidden_units = gate_weight.shape[1] // ctx
    shard_rows = query_weight.shape[0]

    gains = jnp.stack(
        [
            operator_gain,
            feedforward_gain,
            jnp.pad(query_gain, (0, shard_rows - gain_rows)),
            jnp.pad(key_gain, (0, shard_rows - gain_rows)),
        ],
        axis=1,
    )
    attention_pack = jnp.concatenate(
        [
            part_of(query_weight, 1, q_cols, me_c * q_cols),
            part_of(key_weight, 1, kv_cols, kv_start),
            part_of(value_weight, 1, kv_cols, kv_start),
            part_of(output_weight, 0, q_cols, me_c * q_cols).T,
            jnp.pad(gains, ((0, 0), (0, 124))),
        ],
        axis=1,
    )
    gate_up_shard = jnp.concatenate(
        [
            part_of(gate_weight, 1, hidden_units, me_c * hidden_units),
            part_of(up_weight, 1, hidden_units, me_c * hidden_units),
        ],
        axis=1,
    )
    down_shard = part_of(down_weight, 0, hidden_units, me_c * hidden_units)
    attention_full, all_input, upstream = start_gather(attention_pack, block_input, cotangent)
    all_input = all_input.reshape(rows, width)
    upstream = upstream.reshape(rows, width)
    last = all_input
    gate_up_shard, last = lax.optimization_barrier((gate_up_shard, last))
    gate_up_full, last = ring_gather(gate_up_shard, "fsdp")
    down_shard, last = lax.optimization_barrier((down_shard, last))
    down_full, _ = ring_gather(down_shard, "fsdp", 1)
    qkv_cols = q_cols + 2 * kv_cols
    qkv_full = attention_full[:, :qkv_cols]
    output_full = attention_full[:, qkv_cols : qkv_cols + q_cols]
    gains_full = attention_full[:, qkv_cols + q_cols :].astype(f32)
    operator_scale = gains_full[:, 0]
    feedforward_scale = gains_full[:, 1]
    query_scale = gains_full[:, 2].reshape(fsdp, shard_rows)[:, :gain_rows].reshape(-1)
    key_scale = gains_full[:, 3].reshape(fsdp, shard_rows)[:, :gain_rows].reshape(-1)

    own_input = part_of(block_input, 1, quarter, me_t * quarter)
    upstream_own = part_of(cotangent, 1, quarter, me_t * quarter)

    ctx_order = lax.rem(me_c - jnp.arange(ctx) + ctx, ctx)
    tensor_order = lax.rem(me_t - jnp.arange(tensor) + tensor, tensor)
    positions = (
        tensor_order[:, None, None] * quarter
        + ctx_order[None, :, None] * tok_here
        + jnp.arange(quarter)[None, None, :]
    ).reshape(tokens)
    cosine, sine = rotary_tables(positions, head_width)

    def prepare(raw, gain):
        return head_prepare(raw, gain, cosine, sine)

    normed_input = rms_scale(all_input.astype(f32), operator_scale).astype(bf16)
    qkv_raw = jnp.dot(normed_input, qkv_full, preferred_element_type=f32).reshape(seqs, tokens, -1)
    query_f32, query_back = jax.vjp(prepare, qkv_raw[..., :q_cols], query_scale)
    key_f32, key_back = jax.vjp(prepare, qkv_raw[..., q_cols : q_cols + kv_cols], key_scale)
    queries = query_f32.astype(bf16)
    keys = jnp.repeat(key_f32.astype(bf16), group, axis=2)
    values = jnp.repeat(
        qkv_raw[..., q_cols + kv_cols :].astype(bf16).reshape(seqs, tokens, kv, head_width),
        group,
        axis=2,
    )
    attended, totals = jax.vmap(attend, in_axes=(0, 0, 0, None))(queries, keys, values, positions)
    attended_rows = attended.reshape(rows, q_cols)
    attention_part = contract(attended_rows, output_full, 1, 1).reshape(seqs, tokens, width)
    own_f32 = own_input.astype(f32)
    hidden = own_f32 + group_sum(attention_part)
    norm_two, norm_two_back = jax.vjp(lambda v: rms_scale(v, feedforward_scale), hidden)
    normed_hidden = group_rows(norm_two.astype(bf16)).reshape(rows, width)
    gate_up = jnp.dot(normed_hidden, gate_up_full, preferred_element_type=f32)
    act_f32, act_back = jax.vjp(swiglu, gate_up[:, :hidden_units], gate_up[:, hidden_units:])
    activation = act_f32.astype(bf16)
    act_grad = contract(upstream, down_full, 1, 1)
    gate_grad, up_grad = act_back(act_grad)
    gate_up_grad = jnp.concatenate([gate_grad.astype(bf16), up_grad.astype(bf16)], axis=1)
    hidden_part = contract(gate_up_grad, gate_up_full, 1, 1).reshape(seqs, tokens, width)
    down_grad = contract(activation, upstream, 0, 0).astype(bf16)
    gate_up_weight_grad = contract(normed_hidden, gate_up_grad, 0, 0).astype(bf16)
    normed_hidden_grad = group_sum(hidden_part)
    down_share = ring_scatter(
        lambda owner: part_of(down_grad, 1, shard_rows, owner * shard_rows), "fsdp"
    ).astype(bf16)
    gate_up_weight_grad, down_share = lax.optimization_barrier((gate_up_weight_grad, down_share))
    gate_up_share = ring_scatter(
        lambda owner: part_of(gate_up_weight_grad, 0, shard_rows, owner * shard_rows), "fsdp"
    ).astype(bf16)
    down_part = jnp.dot(activation, down_full, preferred_element_type=f32).reshape(seqs, tokens, width)
    own_output = (hidden + group_sum(down_part)).astype(bf16)
    block_output = in_order(own_output, "tensor", 1)

    (hidden_norm_grad,) = norm_two_back(normed_hidden_grad)
    hidden_grad = upstream_own.astype(f32) + hidden_norm_grad
    hidden_grad_b = group_rows(hidden_grad.astype(bf16)).reshape(rows, width)
    output_weight_grad = contract(hidden_grad_b, attended_rows, 0, 0)
    attended_grad = (
        jnp.dot(hidden_grad_b, output_full, preferred_element_type=f32)
        .astype(bf16)
        .reshape(seqs, tokens, heads, head_width)
    )
    query_hgrad, key_hgrad, value_hgrad = jax.vmap(attend_grad, in_axes=(0, 0, 0, 0, 0, 0, None))(
        queries, keys, values, attended, totals, attended_grad, positions
    )

    def head_sum(grad):
        return grad.astype(f32).reshape(seqs, tokens, kv, group, head_width).sum(axis=3)

    query_pre, query_gain_grad = query_back(query_hgrad.astype(f32))
    key_pre, key_gain_grad = key_back(head_sum(key_hgrad))
    qkv_raw_grad = jnp.concatenate(
        [
            query_pre.astype(bf16).reshape(rows, q_cols),
            key_pre.astype(bf16).reshape(rows, kv_cols),
            head_sum(value_hgrad).astype(bf16).reshape(rows, kv_cols),
        ],
        axis=1,
    )
    input_part = contract(qkv_raw_grad, qkv_full, 1, 1).reshape(tensor, ctx, quarter, width)
    qkv_weight_grad = contract(normed_input, qkv_raw_grad, 0, 0)
    gain_grads = jnp.stack([query_gain_grad, key_gain_grad], axis=1).reshape(fsdp, gain_rows, 2)
    gain_grads = jnp.pad(
        gain_grads, ((0, 0), (0, shard_rows - gain_rows), (0, 126))
    ).reshape(width, 128)
    attention_grad = jnp.concatenate(
        [qkv_weight_grad, output_weight_grad, gain_grads], axis=1
    ).astype(bf16)
    attention_grad, gate_up_share = lax.optimization_barrier((attention_grad, gate_up_share))
    attention_parts, normed_input_grad = finish_sums(attention_grad, input_part)
    attention_parts = attention_parts.astype(f32)
    normed_input_grad = normed_input_grad[None]
    _, norm_one_back = jax.vjp(lambda v: rms_scale(v, operator_scale), own_f32)
    (input_norm_grad,) = norm_one_back(normed_input_grad)
    input_grad = in_order(hidden_grad + input_norm_grad, "tensor", 1)

    def ctx_parts(share):
        size = lax.axis_size("ctx")
        parts = jnp.zeros((size,) + share.shape, share.dtype)
        for step in range(size):
            piece = share if step == 0 else shift(share, "ctx", step)
            owner = lax.rem(me_c - step + size, size)
            parts = lax.dynamic_update_slice(parts, piece[None], (owner, 0, 0))
        return parts.astype(f32)

    def columns(parts):
        return jnp.moveaxis(parts, 0, 1).reshape(parts.shape[1], -1)

    gate_up_parts = ctx_parts(gate_up_share)
    down_parts = ctx_parts(down_share)

    def head_columns(parts):
        every = columns(parts)
        if copies == 1:
            return every
        return every.reshape(shard_rows, kv_shard, copies, head_width).sum(axis=2).reshape(
            shard_rows, -1
        )

    query_weight_grad = columns(attention_parts[:, :, :q_cols])
    key_weight_grad = head_columns(attention_parts[:, :, q_cols : q_cols + kv_cols])
    value_weight_grad = head_columns(attention_parts[:, :, q_cols + kv_cols : qkv_cols])
    gate_weight_grad = columns(gate_up_parts[:, :, :hidden_units])
    up_weight_grad = columns(gate_up_parts[:, :, hidden_units:])
    gain_parts = attention_parts[:, :, qkv_cols + q_cols : qkv_cols + q_cols + 2].sum(axis=0)

    def gain_part(pairs, gain):
        total = 0.0
        for weight, grad in pairs:
            total = total + jnp.sum(weight.astype(f32) * grad, axis=1)
        return total / gain.astype(f32)

    gain_columns = jnp.concatenate(
        [
            gain_part(
                [
                    (query_weight, query_weight_grad),
                    (key_weight, key_weight_grad),
                    (value_weight, value_weight_grad),
                ],
                operator_gain,
            )[:, None],
            gain_part(
                [(gate_weight, gate_weight_grad), (up_weight, up_weight_grad)], feedforward_gain
            )[:, None],
            gain_parts,
        ],
        axis=1,
    )
    gain_totals = gain_columns
    for step in range(1, tensor):
        gain_totals = gain_totals + shift(gain_columns, "tensor", step)

    return (
        block_output,
        input_grad,
        gain_totals[:, 0],
        query_weight_grad,
        key_weight_grad,
        value_weight_grad,
        jnp.swapaxes(attention_parts[:, :, qkv_cols : qkv_cols + q_cols], 1, 2).reshape(
            -1, shard_rows
        ),
        gain_totals[:, 1],
        gate_weight_grad,
        up_weight_grad,
        down_parts.reshape(-1, shard_rows),
        gain_totals[:gain_rows, 2],
        gain_totals[:gain_rows, 3],
    )


def solution(mesh):
    in_specs = (
        P("fsdp", "ctx", None),
        P("fsdp"),
        P("fsdp", "tensor"),
        P("fsdp", "tensor"),
        P("fsdp", "tensor"),
        P("tensor", "fsdp"),
        P("fsdp"),
        P("fsdp", "tensor"),
        P("fsdp", "tensor"),
        P("tensor", "fsdp"),
        P("fsdp"),
        P("fsdp"),
        P("fsdp", "ctx", None),
    )
    out_specs = (
        P("fsdp", "ctx", None),
        P("fsdp", "ctx", None),
        P("fsdp"),
        P("fsdp", "tensor"),
        P("fsdp", "tensor"),
        P("fsdp", "tensor"),
        P("tensor", "fsdp"),
        P("fsdp"),
        P("fsdp", "tensor"),
        P("fsdp", "tensor"),
        P("tensor", "fsdp"),
        P("fsdp"),
        P("fsdp"),
    )
    return jax.shard_map(shards, mesh=mesh, in_specs=in_specs, out_specs=out_specs, check_vma=False)
```

```python
import jax
import jax.numpy as jnp
from jax import lax
from jax.experimental import pallas as pl
from jax.experimental.pallas import tpu as pltpu
from jax.sharding import PartitionSpec as P

EPS = 1e-05
THETA = 1000000.0


def rms_scale(values_in, gain):
    return (
        values_in * lax.rsqrt(jnp.mean(values_in * values_in, axis=-1, keepdims=True) + EPS) * gain
    )


def rotary_tables(positions, head_width):
    half_width = head_width // 2
    freqs = THETA ** (-jnp.arange(half_width).astype(jnp.float32) * 2.0 / head_width)
    angles = positions.astype(jnp.float32)[:, None] * freqs[None, :]
    return (jnp.cos(angles), jnp.sin(angles))


def rotate_halves(heads_in, cosine, sine):
    half_width = heads_in.shape[-1] // 2
    front_half = heads_in[..., :half_width]
    back_half = heads_in[..., half_width:]
    cos_rows = cosine[:, None, :]
    sin_rows = sine[:, None, :]
    return jnp.concatenate(
        [
            front_half * cos_rows - back_half * sin_rows,
            back_half * cos_rows + front_half * sin_rows,
        ],
        axis=-1,
    )


def head_prepare(raw, gain, cosine, sine):
    head_width = gain.shape[0]
    shaped = raw.reshape(raw.shape[:-1] + (raw.shape[-1] // head_width, head_width))
    return rotate_halves(rms_scale(shaped, gain), cosine, sine)


def swiglu(gate, upper):
    return jax.nn.silu(gate) * upper


def contract(left, right, left_dim, right_dim):
    return lax.dot_general(
        left, right, (((left_dim,), (right_dim,)), ((), ())), preferred_element_type=jnp.float32
    )


def block_scores(query_block, keys, query_pos, key_pos):
    scale = 1.0 / query_block.shape[-1] ** 0.5
    scores = (
        jnp.einsum("qhd,khd->hqk", query_block, keys, preferred_element_type=jnp.float32) * scale
    )
    allowed = key_pos[None, :] <= query_pos[:, None]
    return jnp.where(allowed[None, :, :], scores, -1e30)


def attend(queries, keys, values, positions):
    length = queries.shape[0]
    block_rows = min(512, length)
    outputs = []
    totals = []
    for start in range(0, length, block_rows):
        rows = slice(start, start + block_rows)
        scores = block_scores(queries[rows], keys, positions[rows], positions)
        peak = jnp.max(scores, axis=-1, keepdims=True)
        log_total = peak + jnp.log(jnp.sum(jnp.exp(scores - peak), axis=-1, keepdims=True))
        probs = jnp.exp(scores - log_total).astype(jnp.bfloat16)
        block_out = jnp.einsum("hqk,khd->qhd", probs, values, preferred_element_type=jnp.float32)
        outputs.append(block_out.astype(jnp.bfloat16))
        totals.append(log_total[..., 0])
    return (jnp.concatenate(outputs, axis=0), jnp.concatenate(totals, axis=1))


def attend_grad(queries, keys, values, outputs, totals, out_grad, positions):
    length = queries.shape[0]
    block_rows = min(512, length)
    scale = 1.0 / queries.shape[-1] ** 0.5
    key_acc = jnp.zeros(keys.shape, jnp.float32)
    value_acc = jnp.zeros(values.shape, jnp.float32)
    query_parts = []
    for start in range(0, length, block_rows):
        rows = slice(start, start + block_rows)
        query_block = queries[rows]
        scores = block_scores(query_block, keys, positions[rows], positions)
        probs = jnp.exp(scores - totals[:, rows][..., None])
        grad_block = out_grad[rows]
        value_acc = value_acc + jnp.einsum(
            "hqk,qhd->khd",
            probs.astype(jnp.bfloat16),
            grad_block,
            preferred_element_type=jnp.float32,
        )
        prob_grad = jnp.einsum(
            "qhd,khd->hqk", grad_block, values, preferred_element_type=jnp.float32
        )
        delta = jnp.sum(
            grad_block.astype(jnp.float32) * outputs[rows].astype(jnp.float32),
            axis=-1,
        ).T
        score_grad = (probs * (prob_grad - delta[..., None])).astype(jnp.bfloat16)
        query_parts.append(
            (
                jnp.einsum("hqk,khd->qhd", score_grad, keys, preferred_element_type=jnp.float32)
                * scale
            ).astype(jnp.bfloat16)
        )
        key_acc = (
            key_acc
            + jnp.einsum(
                "hqk,qhd->khd", score_grad, query_block, preferred_element_type=jnp.float32
            )
            * scale
        )
    return (
        jnp.concatenate(query_parts, axis=0),
        key_acc.astype(jnp.bfloat16),
        value_acc.astype(jnp.bfloat16),
    )


def shift(array, axis_name, step):
    size = lax.axis_size(axis_name)
    return lax.ppermute(array, axis_name, [(i, (i + step) % size) for i in range(size)])


def around(array, axis_name, dim):
    size = lax.axis_size(axis_name)
    return jnp.concatenate(
        [array] + [shift(array, axis_name, step) for step in range(1, size)], axis=dim
    )


def group_rows(array):
    return around(around(array, "ctx", 1), "tensor", 1)


def sum_around(array, axis_name):
    size = lax.axis_size(axis_name)
    part = array.shape[1] // size
    total = array[:, :part].astype(jnp.float32)
    for step in range(1, size):
        piece = array[:, step * part : (step + 1) * part].astype(jnp.bfloat16)
        total = total + shift(piece, axis_name, -step).astype(jnp.float32)
    return total


def group_sum(array):
    return sum_around(sum_around(array, "tensor"), "ctx")


def in_order(array, axis_name, dim):
    size = lax.axis_size(axis_name)
    me = lax.axis_index(axis_name)
    width = array.shape[dim]
    shape = list(array.shape)
    shape[dim] = width * size
    out = jnp.zeros(shape, array.dtype)
    for step in range(size):
        piece = array if step == 0 else shift(array, axis_name, step)
        owner = lax.rem(me - step + size, size)
        out = lax.dynamic_update_slice_in_dim(out, piece, owner * width, dim)
    return out


def ring_index(place, size):
    if size % 2:
        return place
    turn = size // 2
    return jnp.where(place < turn, 2 * place, 2 * (size - 1 - place) + 1)


def ring_place(index, size):
    if size % 2:
        return index
    return jnp.where(lax.rem(index, 2) == 0, lax.div(index, 2), size - 1 - lax.div(index, 2))


def ring_order(size):
    if size % 2:
        return list(range(size))
    return [2 * i for i in range(size // 2)] + [2 * i + 1 for i in reversed(range(size // 2))]


def ring_shift(array, axis_name, step):
    size = lax.axis_size(axis_name)
    order = ring_order(size)
    pairs = [(order[i], order[(i + step) % size]) for i in range(size)]
    return lax.ppermute(array, axis_name, pairs)


def ring_gather(shard, axis_name, dim=0):
    size = lax.axis_size(axis_name)
    place = ring_place(lax.axis_index(axis_name), size)
    shape = list(shard.shape)
    shape[dim] *= size
    half = shard.shape[0] // 2
    out = jnp.zeros(shape, shard.dtype)

    def put(out, piece, at, offset):
        owner = ring_index(lax.rem(at + size, size), size)
        starts = [offset, 0]
        starts[dim] += owner * shard.shape[dim]
        return lax.dynamic_update_slice(out, piece, starts)

    out = put(out, shard, place, 0)
    rightward = leftward = shard
    for step in range(1, (size + 1) // 2):
        rightward = ring_shift(rightward, axis_name, 1)
        leftward = ring_shift(leftward, axis_name, -1)
        out = put(out, rightward, place - step, 0)
        out = put(out, leftward, place + step, 0)
    if size % 2 == 0:
        rightward = ring_shift(rightward[:half], axis_name, 1)
        leftward = ring_shift(leftward[half:], axis_name, -1)
        out = put(out, rightward, place + size // 2, 0)
        out = put(out, leftward, place + size // 2, half)
    return out, rightward


def ring_scatter(piece_for, axis_name):
    size = lax.axis_size(axis_name)
    place = ring_place(lax.axis_index(axis_name), size)

    def piece(offset):
        return piece_for(ring_index(lax.rem(place + offset + size, size), size))

    mine = piece(0).astype(jnp.float32)
    if size == 1:
        return mine
    half = mine.shape[0] // 2
    far = size // 2
    bf16 = jnp.bfloat16
    f32 = jnp.float32
    if size % 2 == 0:
        across = piece(far)
        rightward = ring_shift(across[:half].astype(bf16), axis_name, 1).astype(f32)
        leftward = ring_shift(across[half:].astype(bf16), axis_name, -1).astype(f32)
        zero = jnp.zeros_like(mine[:half])
        rightward = jnp.concatenate([rightward, zero], axis=0)
        leftward = jnp.concatenate([zero, leftward], axis=0)
        steps = far - 1
    else:
        rightward = leftward = jnp.zeros_like(mine)
        steps = far
    for step in range(steps, 0, -1):
        rightward = ring_shift((rightward + piece(step)).astype(bf16), axis_name, 1).astype(f32)
        leftward = ring_shift((leftward + piece(-step)).astype(bf16), axis_name, -1).astype(f32)
    return mine + rightward + leftward


def other(axis_name, step):
    size = lax.axis_size(axis_name)
    return {axis_name: lax.rem(lax.axis_index(axis_name) + step + size, size)}


def send(source, target, send_sem, recv_sem, device):
    copy = pltpu.make_async_remote_copy(
        src_ref=source,
        dst_ref=target,
        send_sem=send_sem,
        recv_sem=recv_sem,
        device_id=device,
        device_id_type=pl.DeviceIdType.MESH,
    )
    copy.start()
    return copy


def ring_ends():
    size = lax.axis_size("fsdp")
    place = ring_place(lax.axis_index("fsdp"), size)

    def at(offset):
        return ring_index(lax.rem(place + offset + size, size), size)

    return at, ({"fsdp": at(1)}, {"fsdp": at(-1)})


def greet():
    _, ends = ring_ends()
    partners = list(ends)
    for axis_name in ("ctx", "tensor"):
        partners += [other(axis_name, step) for step in range(1, lax.axis_size(axis_name))]
    barrier = pltpu.get_barrier_semaphore()
    for device in partners:
        pl.semaphore_signal(
            barrier, inc=1, device_id=device, device_id_type=pl.DeviceIdType.MESH
        )
    pl.semaphore_wait(barrier, len(partners))


def start_kernel(
    pack_ref,
    input_ref,
    upstream_ref,
    full_ref,
    all_input_ref,
    all_upstream_ref,
    ring_send,
    ring_recv,
    ctx_send,
    ctx_recv,
    tensor_send,
    tensor_recv,
    local_sem,
):
    size = lax.axis_size("fsdp")
    ctx = lax.axis_size("ctx")
    tensor = lax.axis_size("tensor")
    me_t = lax.axis_index("tensor")
    far = size // 2
    rows = pack_ref.shape[0]
    sub_rows = rows // 2
    quarter = all_input_ref.shape[2]
    at, ends = ring_ends()
    greet()
    pairs = ((input_ref, all_input_ref), (upstream_ref, all_upstream_ref))

    def block(owner, sub):
        start = pl.multiple_of(owner * rows + sub * sub_rows, sub_rows)
        return full_ref.at[pl.ds(start, sub_rows)]

    sends = []
    arrivals = {}

    def ring_step(step):
        for sub in range(2):
            for way in range(2):
                if step == far and sub != way:
                    continue
                if step > 1:
                    arrivals.pop((way, step - 1, sub)).wait_recv()
                owner = at((1 - step) if way == 0 else (step - 1))
                source = (
                    pack_ref.at[pl.ds(sub * sub_rows, sub_rows)] if step == 1 else block(owner, sub)
                )
                copy = send(
                    source,
                    block(owner, sub),
                    ring_send.at[way, step - 1, sub],
                    ring_recv.at[way, step - 1, sub],
                    ends[way],
                )
                sends.append(copy)
                arrivals[way, step, sub] = copy

    def own_rows(source, step):
        quarter_at = lax.rem(me_t - step + tensor, tensor)
        return source.at[0, pl.ds(pl.multiple_of(quarter_at * quarter, quarter), quarter)]

    ring_step(1)
    crossed = {}
    locals_ = []
    for which, (source, target) in enumerate(pairs):
        for step in range(1, ctx):
            copy = send(
                own_rows(source, 0),
                target.at[0, step],
                ctx_send.at[which, step - 1],
                ctx_recv.at[which, step - 1],
                other("ctx", step),
            )
            sends.append(copy)
            crossed[which, step] = copy
    for which, (source, target) in enumerate(pairs):
        for step in range(tensor):
            copy = pltpu.make_async_copy(
                own_rows(source, step), target.at[step, 0], local_sem.at[which, step]
            )
            copy.start()
            locals_.append(copy)
    own_copy = pltpu.make_async_copy(
        pack_ref,
        full_ref.at[pl.ds(pl.multiple_of(at(0) * rows, rows), rows)],
        local_sem.at[2, 0],
    )
    own_copy.start()
    locals_.append(own_copy)
    handed = []

    def hand_over(which):
        _, target = pairs[which]
        for step in range(1, ctx):
            crossed[which, step].wait_recv()
            for core in range(1, tensor):
                copy = send(
                    target.at[0, step],
                    target.at[core, step],
                    tensor_send.at[which, core - 1, step - 1],
                    tensor_recv.at[which, core - 1, step - 1],
                    other("tensor", core),
                )
                sends.append(copy)
                handed.append(copy)

    for step in range(2, far + 1):
        if step == far:
            hand_over(0)
        ring_step(step)
    if far < 2:
        hand_over(0)
    hand_over(1)
    for copy in arrivals.values():
        copy.wait_recv()
    for copy in handed:
        copy.wait_recv()
    for copy in sends:
        copy.wait_send()
    for copy in locals_:
        copy.wait()


def start_gather(pack, block_input, cotangent):
    size = lax.axis_size("fsdp")
    ctx = lax.axis_size("ctx")
    tensor = lax.axis_size("tensor")
    far = size // 2
    rows, columns = pack.shape
    _, tok_here, width = block_input.shape
    every = (tensor, ctx, tok_here // tensor, width)
    in_vmem = pl.BlockSpec(memory_space=pltpu.VMEM)
    dma = pltpu.SemaphoreType.DMA
    return pl.pallas_call(
        start_kernel,
        out_shape=(
            jax.ShapeDtypeStruct((rows * size, columns), pack.dtype),
            jax.ShapeDtypeStruct(every, block_input.dtype),
            jax.ShapeDtypeStruct(every, cotangent.dtype),
        ),
        in_specs=[in_vmem] * 3,
        out_specs=(in_vmem,) * 3,
        scratch_shapes=[
            dma((2, far, 2)),
            dma((2, far, 2)),
            dma((2, ctx)),
            dma((2, ctx)),
            dma((2, tensor, ctx)),
            dma((2, tensor, ctx)),
            dma((3, tensor)),
        ],
        compiler_params=pltpu.CompilerParams(
            collective_id=0, has_side_effects=True, vmem_limit_bytes=32 * 1024 * 1024
        ),
        name="start_gather",
    )(pack, block_input, cotangent)


def add_rows(count, block_rows, body):
    def step(index, carry):
        body(pl.ds(pl.multiple_of(index * block_rows, block_rows), block_rows))
        return carry

    lax.fori_loop(0, count // block_rows, step, 0)


def finish_kernel(
    grad_ref,
    part_ref,
    parts_ref,
    total_ref,
    going,
    coming,
    share,
    core_going,
    core_coming,
    ctx_going,
    ctx_coming,
    ring_send,
    ring_recv,
    core_send,
    core_recv,
    ctx_send,
    ctx_recv,
    share_send,
    share_recv,
    local_sem,
):
    f32 = jnp.float32
    bf16 = jnp.bfloat16
    size = lax.axis_size("fsdp")
    ctx = lax.axis_size("ctx")
    tensor = lax.axis_size("tensor")
    me_c = lax.axis_index("ctx")
    far = size // 2
    rows = share.shape[0]
    sub_rows = rows // 2
    quarter = part_ref.shape[2]
    at, ends = ring_ends()
    greet()
    sends = []
    arrivals = {}

    def own_block(owner, sub):
        return pl.ds(pl.multiple_of(owner * rows + sub * sub_rows, sub_rows), sub_rows)

    def ring_step(step):
        for sub in range(2):
            for way in range(2):
                if step == 1 and sub != way:
                    continue
                ahead = far + 1 - step
                owner = at(ahead if way == 0 else -ahead)
                mine = own_block(owner, sub)
                if step == 1:
                    source = grad_ref.at[mine]
                else:
                    source = going.at[way, step - 2, sub]
                    if (way, step - 1, sub) in arrivals:
                        arrivals.pop((way, step - 1, sub)).wait_recv()
                        source[...] = (
                            grad_ref[mine, :].astype(f32)
                            + coming[way, step - 2, sub].astype(f32)
                        ).astype(bf16)
                    else:
                        source = grad_ref.at[mine]
                copy = send(
                    source,
                    coming.at[way, step - 1, sub],
                    ring_send.at[way, step - 1, sub],
                    ring_recv.at[way, step - 1, sub],
                    ends[way],
                )
                sends.append(copy)
                arrivals[way, step, sub] = copy

    ring_step(1)
    by_core = []
    for core in range(1, tensor):
        for step in range(ctx):

            def narrow(block, core=core, step=step):
                core_going[core - 1, step, block] = part_ref[core, step, block].astype(bf16)

            add_rows(quarter, 32, narrow)
        copy = send(
            core_going.at[core - 1],
            core_coming.at[core - 1],
            core_send.at[core - 1],
            core_recv.at[core - 1],
            other("tensor", -core),
        )
        sends.append(copy)
        by_core.append(copy)
    if far > 1:
        ring_step(2)
    for copy in by_core:
        copy.wait_recv()
    by_ctx = []
    for step in list(range(1, ctx)) + [0]:

        def total(block, step=step):
            value = part_ref[0, step, block]
            for core in range(1, tensor):
                value = value + core_coming[core - 1, step, block].astype(f32)
            if step == 0:
                total_ref[block] = value
            else:
                ctx_going[step - 1, block] = value.astype(bf16)

        add_rows(quarter, 32, total)
        if step > 0:
            copy = send(
                ctx_going.at[step - 1],
                ctx_coming.at[step - 1],
                ctx_send.at[step - 1],
                ctx_recv.at[step - 1],
                other("ctx", -step),
            )
            sends.append(copy)
            by_ctx.append(copy)
    for step in range(3, far + 1):
        ring_step(step)
    mine = at(0)
    for sub in range(2):
        value = grad_ref[own_block(mine, sub), :].astype(f32)
        for way in range(2):
            if (way, far, sub) in arrivals:
                arrivals.pop((way, far, sub)).wait_recv()
                value = value + coming[way, far - 1, sub].astype(f32)
        share[sub * sub_rows : (sub + 1) * sub_rows, :] = value.astype(bf16)
    shared = []
    for step in range(1, ctx):
        copy = send(
            share,
            parts_ref.at[me_c],
            share_send.at[step - 1],
            share_recv.at[step - 1],
            other("ctx", step),
        )
        sends.append(copy)
        shared.append(copy)
    keep = pltpu.make_async_copy(share, parts_ref.at[me_c], local_sem)
    keep.start()
    for step in range(1, ctx):
        by_ctx[step - 1].wait_recv()

        def gather(block, step=step):
            total_ref[block] += ctx_coming[step - 1, block].astype(f32)

        add_rows(quarter, 32, gather)
    for step in range(1, ctx):
        shared[step - 1].wait_recv()
    for copy in sends:
        copy.wait_send()
    keep.wait()


def finish_sums(grad, part):
    size = lax.axis_size("fsdp")
    tensor, ctx, quarter, width = part.shape
    far = size // 2
    rows, columns = grad.shape[0] // size, grad.shape[1]
    in_vmem = pl.BlockSpec(memory_space=pltpu.VMEM)
    anywhere = pl.BlockSpec(memory_space=pl.ANY)
    dma = pltpu.SemaphoreType.DMA
    bf16 = jnp.bfloat16
    return pl.pallas_call(
        finish_kernel,
        out_shape=(
            jax.ShapeDtypeStruct((ctx, rows, columns), bf16),
            jax.ShapeDtypeStruct((quarter, width), jnp.float32),
        ),
        in_specs=[in_vmem] * 2,
        out_specs=(anywhere, in_vmem),
        scratch_shapes=[
            pltpu.VMEM((2, max(1, far - 1), 2, rows // 2, columns), bf16),
            pltpu.VMEM((2, far, 2, rows // 2, columns), bf16),
            pltpu.VMEM((rows, columns), bf16),
            pltpu.VMEM((max(1, tensor - 1), ctx, quarter, width), bf16),
            pltpu.VMEM((max(1, tensor - 1), ctx, quarter, width), bf16),
            pltpu.VMEM((max(1, ctx - 1), quarter, width), bf16),
            pltpu.VMEM((max(1, ctx - 1), quarter, width), bf16),
            dma((2, far, 2)),
            dma((2, far, 2)),
            dma((tensor,)),
            dma((tensor,)),
            dma((ctx,)),
            dma((ctx,)),
            dma((ctx,)),
            dma((ctx,)),
            dma(()),
        ],
        compiler_params=pltpu.CompilerParams(
            collective_id=1, has_side_effects=True, vmem_limit_bytes=48 * 1024 * 1024
        ),
        name="finish_sums",
    )(grad, part)


def gather_ring(shard_ref, full_ref, send_sem, recv_sem):
    size = lax.axis_size("fsdp")
    far = size // 2
    rows = shard_ref.shape[0]
    sub_rows = rows // 2
    at, ends = ring_ends()
    sends = []
    arrivals = {}
    queue = [(step, sub) for step in range(1, far + 1) for sub in range(2)]

    def block(owner, sub):
        start = pl.multiple_of(owner * rows + sub * sub_rows, sub_rows)
        return full_ref.at[pl.ds(start, sub_rows)]

    def go(count):
        for _ in range(min(count, len(queue))):
            step, sub = queue.pop(0)
            for way in range(2):
                if step > 1 and (step < far or sub == way):
                    arrivals.pop((way, step - 1, sub)).wait_recv()
                if step == far and sub != way:
                    continue
                owner = at((1 - step) if way == 0 else (step - 1))
                source = (
                    shard_ref.at[pl.ds(sub * sub_rows, sub_rows)] if step == 1 else block(owner, sub)
                )
                copy = send(
                    source,
                    block(owner, sub),
                    send_sem.at[way, step - 1, sub],
                    recv_sem.at[way, step - 1, sub],
                    ends[way],
                )
                sends.append(copy)
                arrivals[way, step, sub] = copy

    def finish():
        go(len(queue))
        for copy in arrivals.values():
            copy.wait_recv()
        for copy in sends:
            copy.wait_send()

    return go, finish


def scatter_ring(grad_ref, going, coming, send_sem, recv_sem):
    f32 = jnp.float32
    bf16 = jnp.bfloat16
    size = lax.axis_size("fsdp")
    far = size // 2
    rows = grad_ref.shape[0] // size
    sub_rows = rows // 2
    step_rows = 16
    at, ends = ring_ends()
    sends = []
    arrivals = {}
    queue = [(step, sub) for step in range(1, far + 1) for sub in range(2)]

    def start_of(owner, sub):
        return pl.multiple_of(owner * rows + sub * sub_rows, sub_rows)

    def go(count):
        for _ in range(min(count, len(queue))):
            step, sub = queue.pop(0)
            for way in range(2):
                if step == 1 and sub != way:
                    continue
                ahead = far + 1 - step
                first = start_of(at(ahead if way == 0 else -ahead), sub)
                source = grad_ref.at[pl.ds(first, sub_rows)]
                if (way, step - 1, sub) in arrivals:
                    arrivals.pop((way, step - 1, sub)).wait_recv()
                    source = going.at[way, step - 2, sub]

                    def add(index, carry, way=way, step=step, sub=sub, first=first):
                        here = pl.ds(pl.multiple_of(index * step_rows, step_rows), step_rows)
                        there = pl.ds(
                            pl.multiple_of(first + index * step_rows, step_rows), step_rows
                        )
                        going[way, step - 2, sub, here] = (
                            grad_ref[there].astype(f32) + coming[way, step - 2, sub, here].astype(f32)
                        ).astype(bf16)
                        return carry

                    lax.fori_loop(0, sub_rows // step_rows, add, 0)
                copy = send(
                    source,
                    coming.at[way, step - 1, sub],
                    send_sem.at[way, step - 1, sub],
                    recv_sem.at[way, step - 1, sub],
                    ends[way],
                )
                sends.append(copy)
                arrivals[way, step, sub] = copy

    def finish(share_ref):
        go(len(queue))
        for sub in range(2):
            landed = []
            for way in range(2):
                if (way, far, sub) in arrivals:
                    arrivals.pop((way, far, sub)).wait_recv()
                    landed.append(way)

            def add(index, carry, sub=sub, landed=landed):
                here = pl.ds(pl.multiple_of(index * step_rows, step_rows), step_rows)
                there = pl.ds(
                    pl.multiple_of(start_of(at(0), sub) + index * step_rows, step_rows), step_rows
                )
                out = pl.ds(
                    pl.multiple_of(sub * sub_rows + index * step_rows, step_rows), step_rows
                )
                value = grad_ref[there].astype(f32)
                for way in landed:
                    value = value + coming[way, far - 1, sub, here].astype(f32)
                share_ref[out] = value.astype(share_ref.dtype)
                return carry

            lax.fori_loop(0, sub_rows // step_rows, add, 0)
        for copy in sends:
            copy.wait_send()

    return go, finish


def slot_base(slot, quarter):
    ctx = lax.axis_size("ctx")
    tensor = lax.axis_size("tensor")
    of_core = lax.rem(lax.axis_index("tensor") - lax.div(slot, ctx) + tensor, tensor)
    of_ctx = lax.rem(lax.axis_index("ctx") - lax.rem(slot, ctx) + ctx, ctx)
    return of_core * quarter + of_ctx * (quarter * tensor)


def reachable(query_slot, key_slot, quarter):
    gap = slot_base(query_slot, quarter) - slot_base(key_slot, quarter)
    return gap, gap > -quarter


def masked_scores(keys, queries, gap):
    scores = lax.dot_general(
        keys, queries, (((1,), (1,)), ((), ())), preferred_element_type=jnp.float32
    ) * (1.0 / queries.shape[-1] ** 0.5)
    key_at = lax.broadcasted_iota(jnp.int32, scores.shape, 0)
    query_at = lax.broadcasted_iota(jnp.int32, scores.shape, 1)
    return jnp.where(key_at - query_at <= gap, scores, -1e30)


def attend_slot(slot, q_ref, k_ref, vt_ref, attended_ref, turned_ref, total_ref, work):
    scores_ref, peak_ref, sum_ref, out_ref = work
    slots, heads, quarter, head_width = q_ref.shape
    group = heads // k_ref.shape[1]

    def one_head(head, carry):
        kv_head = lax.div(head, group)
        peak_ref[...] = jnp.full(peak_ref.shape, -1e30, jnp.float32)
        sum_ref[...] = jnp.zeros(sum_ref.shape, jnp.float32)
        out_ref[...] = jnp.zeros(out_ref.shape, jnp.float32)

        def score(key_slot, carry):
            gap, seen = reachable(slot, key_slot, quarter)

            @pl.when(seen)
            def _():
                scores = masked_scores(k_ref[key_slot, kv_head], q_ref[slot, head], gap)
                scores_ref[key_slot] = scores
                peak_ref[...] = jnp.maximum(peak_ref[...], jnp.max(scores, axis=0, keepdims=True))

            return carry

        lax.fori_loop(0, slots, score, 0)

        def weigh(key_slot, carry):
            _, seen = reachable(slot, key_slot, quarter)

            @pl.when(seen)
            def _():
                raised = jnp.exp(scores_ref[key_slot] - peak_ref[...])
                sum_ref[...] += jnp.sum(raised, axis=0, keepdims=True)
                out_ref[...] += jnp.dot(
                    vt_ref[key_slot, kv_head],
                    raised.astype(jnp.bfloat16),
                    preferred_element_type=jnp.float32,
                )

            return carry

        lax.fori_loop(0, slots, weigh, 0)
        total_ref[slot, head] = peak_ref[...] + jnp.log(sum_ref[...])
        rows = pl.ds(pl.multiple_of(head * head_width, head_width), head_width)
        turned_ref[slot, rows] = (out_ref[...] / sum_ref[...]).astype(jnp.bfloat16)
        return carry

    lax.fori_loop(0, heads, one_head, 0)
    attended_ref[slot] = turned_ref[slot].astype(jnp.float32).T.astype(jnp.bfloat16)


def forward_kernel(
    shard_ref,
    q_ref,
    k_ref,
    vt_ref,
    weight_ref,
    own_ref,
    gain_ref,
    full_ref,
    attended_ref,
    turned_ref,
    total_ref,
    hidden_ref,
    normed_ref,
    scores_ref,
    peak_ref,
    sum_ref,
    out_ref,
    part_ref,
    core_going,
    core_coming,
    ctx_going,
    ctx_coming,
    ring_send,
    ring_recv,
    core_send,
    core_recv,
    ctx_send,
    ctx_recv,
    spread_send,
    spread_recv,
    local_sem,
):
    f32 = jnp.float32
    bf16 = jnp.bfloat16
    ctx = lax.axis_size("ctx")
    tensor = lax.axis_size("tensor")
    slots, _, quarter, _ = q_ref.shape
    rows = shard_ref.shape[0]
    greet()
    go, finish = gather_ring(shard_ref, full_ref, ring_send, ring_recv)
    go(2)
    keep = pltpu.make_async_copy(
        shard_ref,
        full_ref.at[pl.ds(pl.multiple_of(ring_ends()[0](0) * rows, rows), rows)],
        local_sem,
    )
    keep.start()
    work = (scores_ref, peak_ref, sum_ref, out_ref)

    def project(slot):
        attend_slot(slot, q_ref, k_ref, vt_ref, attended_ref, turned_ref, total_ref, work)
        return lax.dot_general(
            attended_ref[slot],
            weight_ref[...],
            (((1,), (1,)), ((), ())),
            preferred_element_type=f32,
        )

    sends = []
    by_core = {}
    by_ctx = {}
    for core in range(1, tensor):
        for step in list(range(1, ctx)) + [0]:
            core_going[core - 1, step] = project(core * ctx + step).astype(bf16)
            copy = send(
                core_going.at[core - 1, step],
                core_coming.at[core - 1, step],
                core_send.at[core - 1, step],
                core_recv.at[core - 1, step],
                other("tensor", -core),
            )
            sends.append(copy)
            by_core[core, step] = copy
    for step in list(range(1, ctx)) + [0]:
        part_ref[...] = project(step)
        for core in range(1, tensor):
            by_core[core, step].wait_recv()
            part_ref[...] += core_coming[core - 1, step].astype(f32)
        if step > 0:
            ctx_going[step - 1] = part_ref[...].astype(bf16)
            copy = send(
                ctx_going.at[step - 1],
                ctx_coming.at[step - 1],
                ctx_send.at[step - 1],
                ctx_recv.at[step - 1],
                other("ctx", -step),
            )
            sends.append(copy)
            by_ctx[step] = copy
        if step < 2:
            go(1)
    for step in range(1, ctx):
        by_ctx[step].wait_recv()
        part_ref[...] += ctx_coming[step - 1].astype(f32)

    def norm(block):
        hidden = own_ref[block].astype(f32) + part_ref[block]
        hidden_ref[block] = hidden
        scale = lax.rsqrt(jnp.mean(hidden * hidden, axis=-1, keepdims=True) + EPS)
        normed_ref[0, 0, block] = (hidden * scale * gain_ref[...]).astype(bf16)

    add_rows(quarter, 16, norm)
    spread = []
    for step in range(1, ctx):
        copy = send(
            normed_ref.at[0, 0],
            normed_ref.at[0, step],
            spread_send.at[0, step],
            spread_recv.at[0, step],
            other("ctx", step),
        )
        sends.append(copy)
        spread.append(copy)
    handed = []

    def hand_over(step):
        for core in range(1, tensor):
            copy = send(
                normed_ref.at[0, step],
                normed_ref.at[core, step],
                spread_send.at[core, step],
                spread_recv.at[core, step],
                other("tensor", core),
            )
            sends.append(copy)
            handed.append(copy)

    hand_over(0)
    go(1)
    for step in range(1, ctx):
        spread[step - 1].wait_recv()
        hand_over(step)
    finish()
    for copy in handed:
        copy.wait_recv()
    for copy in sends:
        copy.wait_send()
    keep.wait()


def forward_gather(shard, queries, keys, values_turned, weight, own, gain):
    size = lax.axis_size("fsdp")
    ctx = lax.axis_size("ctx")
    tensor = lax.axis_size("tensor")
    far = size // 2
    rows, columns = shard.shape
    slots, heads, quarter, head_width = queries.shape
    width = own.shape[-1]
    q_cols = heads * head_width
    in_vmem = pl.BlockSpec(memory_space=pltpu.VMEM)
    dma = pltpu.SemaphoreType.DMA
    bf16 = jnp.bfloat16
    f32 = jnp.float32
    cores = max(1, tensor - 1)
    return pl.pallas_call(
        forward_kernel,
        out_shape=(
            jax.ShapeDtypeStruct((rows * size, columns), bf16),
            jax.ShapeDtypeStruct((slots, quarter, q_cols), bf16),
            jax.ShapeDtypeStruct((slots, q_cols, quarter), bf16),
            jax.ShapeDtypeStruct((slots, heads, 1, quarter), f32),
            jax.ShapeDtypeStruct((quarter, width), f32),
            jax.ShapeDtypeStruct((tensor, ctx, quarter, width), bf16),
        ),
        in_specs=[in_vmem] * 7,
        out_specs=(in_vmem,) * 6,
        scratch_shapes=[
            pltpu.VMEM((slots, quarter, quarter), f32),
            pltpu.VMEM((1, quarter), f32),
            pltpu.VMEM((1, quarter), f32),
            pltpu.VMEM((head_width, quarter), f32),
            pltpu.VMEM((quarter, width), f32),
            pltpu.VMEM((cores, ctx, quarter, width), bf16),
            pltpu.VMEM((cores, ctx, quarter, width), bf16),
            pltpu.VMEM((max(1, ctx - 1), quarter, width), bf16),
            pltpu.VMEM((max(1, ctx - 1), quarter, width), bf16),
            dma((2, far, 2)),
            dma((2, far, 2)),
            dma((cores, ctx)),
            dma((cores, ctx)),
            dma((ctx,)),
            dma((ctx,)),
            dma((tensor, ctx)),
            dma((tensor, ctx)),
            dma(()),
        ],
        compiler_params=pltpu.CompilerParams(
            collective_id=2, has_side_effects=True, vmem_limit_bytes=48 * 1024 * 1024
        ),
        name="forward_gather",
    )(shard, queries, keys, values_turned, weight, own, gain)


def part_of(array, dim, count, start):
    return lax.dynamic_slice_in_dim(array, start, count, dim)


def shards(
    block_input,
    operator_gain,
    query_weight,
    key_weight,
    value_weight,
    output_weight,
    feedforward_gain,
    gate_weight,
    up_weight,
    down_weight,
    query_gain,
    key_gain,
    cotangent,
):
    bf16 = jnp.bfloat16
    f32 = jnp.float32
    fsdp = lax.axis_size("fsdp")
    ctx = lax.axis_size("ctx")
    tensor = lax.axis_size("tensor")
    me_c = lax.axis_index("ctx")
    me_t = lax.axis_index("tensor")
    seqs, tok_here, width = block_input.shape
    quarter = tok_here // tensor
    tokens = tok_here * ctx
    rows = seqs * tokens
    gain_rows = query_gain.shape[0]
    head_width = gain_rows * fsdp
    heads_shard = query_weight.shape[1] // head_width
    kv_shard = key_weight.shape[1] // head_width
    spread = heads_shard // kv_shard
    heads = heads_shard // ctx
    kv = max(1, kv_shard // ctx)
    group = heads // kv
    copies = max(1, ctx // kv_shard)
    q_cols = heads * head_width
    kv_cols = kv * head_width
    kv_start = ((me_c * heads) // spread) * head_width
    hidden_units = gate_weight.shape[1] // ctx
    shard_rows = query_weight.shape[0]

    gains = jnp.stack(
        [
            operator_gain,
            feedforward_gain,
            jnp.pad(query_gain, (0, shard_rows - gain_rows)),
            jnp.pad(key_gain, (0, shard_rows - gain_rows)),
        ],
        axis=1,
    )
    attention_pack = jnp.concatenate(
        [
            part_of(query_weight, 1, q_cols, me_c * q_cols),
            part_of(key_weight, 1, kv_cols, kv_start),
            part_of(value_weight, 1, kv_cols, kv_start),
            part_of(output_weight, 0, q_cols, me_c * q_cols).T,
            jnp.pad(gains, ((0, 0), (0, 124))),
        ],
        axis=1,
    )
    feedforward_shard = jnp.concatenate(
        [
            part_of(gate_weight, 1, hidden_units, me_c * hidden_units),
            part_of(up_weight, 1, hidden_units, me_c * hidden_units),
            part_of(down_weight, 0, hidden_units, me_c * hidden_units).T,
        ],
        axis=1,
    )
    attention_full, all_input, upstream = start_gather(attention_pack, block_input, cotangent)
    all_input = all_input.reshape(rows, width)
    upstream = upstream.reshape(rows, width)
    qkv_cols = q_cols + 2 * kv_cols
    qkv_full = attention_full[:, :qkv_cols]
    output_full = attention_full[:, qkv_cols : qkv_cols + q_cols]
    gains_full = attention_full[:, qkv_cols + q_cols :].astype(f32)
    operator_scale = gains_full[:, 0]
    feedforward_scale = gains_full[:, 1]
    query_scale = gains_full[:, 2].reshape(fsdp, shard_rows)[:, :gain_rows].reshape(-1)
    key_scale = gains_full[:, 3].reshape(fsdp, shard_rows)[:, :gain_rows].reshape(-1)

    own_input = part_of(block_input, 1, quarter, me_t * quarter)
    upstream_own = part_of(cotangent, 1, quarter, me_t * quarter)

    ctx_order = lax.rem(me_c - jnp.arange(ctx) + ctx, ctx)
    tensor_order = lax.rem(me_t - jnp.arange(tensor) + tensor, tensor)
    positions = (
        tensor_order[:, None, None] * quarter
        + ctx_order[None, :, None] * tok_here
        + jnp.arange(quarter)[None, None, :]
    ).reshape(tokens)
    cosine, sine = rotary_tables(positions, head_width)

    def prepare(raw, gain):
        return head_prepare(raw, gain, cosine, sine)

    normed_input = rms_scale(all_input.astype(f32), operator_scale).astype(bf16)
    qkv_raw = jnp.dot(normed_input, qkv_full, preferred_element_type=f32).reshape(seqs, tokens, -1)
    query_f32, query_back = jax.vjp(prepare, qkv_raw[..., :q_cols], query_scale)
    key_f32, key_back = jax.vjp(prepare, qkv_raw[..., q_cols : q_cols + kv_cols], key_scale)
    slots = tensor * ctx

    def by_slot(array):
        return array.astype(bf16).reshape(slots, quarter, -1, head_width)

    queries = by_slot(query_f32).transpose(0, 2, 1, 3)
    keys = by_slot(key_f32).transpose(0, 2, 1, 3)
    values = by_slot(qkv_raw[..., q_cols + kv_cols :])
    own_f32 = own_input.astype(f32)
    feedforward_full, attended, attended_turned, totals, hidden, normed_hidden = forward_gather(
        feedforward_shard,
        queries,
        keys,
        values.transpose(0, 2, 3, 1),
        output_full,
        own_input.reshape(quarter, width),
        feedforward_scale.reshape(1, width),
    )
    attended_rows = attended.reshape(rows, q_cols)
    normed_hidden = normed_hidden.reshape(rows, width)
    hidden = hidden[None]
    _, norm_two_back = jax.vjp(lambda v: rms_scale(v, feedforward_scale), hidden)
    gate_up_full = feedforward_full[:, : 2 * hidden_units]
    down_full = feedforward_full[:, 2 * hidden_units :]
    queries = query_f32.astype(bf16)
    keys = jnp.repeat(key_f32.astype(bf16), group, axis=2)
    values = jnp.repeat(values.reshape(seqs, tokens, kv, head_width), group, axis=2)
    attended = attended.reshape(seqs, tokens, heads, head_width)
    totals = totals.reshape(slots, heads, quarter).transpose(1, 0, 2).reshape(seqs, heads, tokens)
    gate_up = jnp.dot(normed_hidden, gate_up_full, preferred_element_type=f32)
    act_f32, act_back = jax.vjp(swiglu, gate_up[:, :hidden_units], gate_up[:, hidden_units:])
    activation = act_f32.astype(bf16)
    act_grad = jnp.dot(upstream, down_full, preferred_element_type=f32)
    gate_grad, up_grad = act_back(act_grad)
    gate_up_grad = jnp.concatenate([gate_grad.astype(bf16), up_grad.astype(bf16)], axis=1)
    hidden_part = contract(gate_up_grad, gate_up_full, 1, 1).reshape(seqs, tokens, width)
    down_grad = contract(activation, upstream, 0, 0).astype(bf16)
    gate_up_weight_grad = contract(normed_hidden, gate_up_grad, 0, 0).astype(bf16)
    normed_hidden_grad = group_sum(hidden_part)
    down_share = ring_scatter(
        lambda owner: part_of(down_grad, 1, shard_rows, owner * shard_rows), "fsdp"
    ).astype(bf16)
    gate_up_weight_grad, down_share = lax.optimization_barrier((gate_up_weight_grad, down_share))
    gate_up_share = ring_scatter(
        lambda owner: part_of(gate_up_weight_grad, 0, shard_rows, owner * shard_rows), "fsdp"
    ).astype(bf16)
    down_part = contract(activation, down_full, 1, 1).reshape(seqs, tokens, width)
    own_output = (hidden + group_sum(down_part)).astype(bf16)
    block_output = in_order(own_output, "tensor", 1)

    (hidden_norm_grad,) = norm_two_back(normed_hidden_grad)
    hidden_grad = upstream_own.astype(f32) + hidden_norm_grad
    hidden_grad_b = group_rows(hidden_grad.astype(bf16)).reshape(rows, width)
    output_weight_grad = contract(hidden_grad_b, attended_rows, 0, 0)
    attended_grad = (
        jnp.dot(hidden_grad_b, output_full, preferred_element_type=f32)
        .astype(bf16)
        .reshape(seqs, tokens, heads, head_width)
    )
    query_hgrad, key_hgrad, value_hgrad = jax.vmap(attend_grad, in_axes=(0, 0, 0, 0, 0, 0, None))(
        queries, keys, values, attended, totals, attended_grad, positions
    )

    def head_sum(grad):
        return grad.astype(f32).reshape(seqs, tokens, kv, group, head_width).sum(axis=3)

    query_pre, query_gain_grad = query_back(query_hgrad.astype(f32))
    key_pre, key_gain_grad = key_back(head_sum(key_hgrad))
    qkv_raw_grad = jnp.concatenate(
        [
            query_pre.astype(bf16).reshape(rows, q_cols),
            key_pre.astype(bf16).reshape(rows, kv_cols),
            head_sum(value_hgrad).astype(bf16).reshape(rows, kv_cols),
        ],
        axis=1,
    )
    input_part = contract(qkv_raw_grad, qkv_full, 1, 1).reshape(tensor, ctx, quarter, width)
    qkv_weight_grad = contract(normed_input, qkv_raw_grad, 0, 0)
    gain_grads = jnp.stack([query_gain_grad, key_gain_grad], axis=1).reshape(fsdp, gain_rows, 2)
    gain_grads = jnp.pad(
        gain_grads, ((0, 0), (0, shard_rows - gain_rows), (0, 126))
    ).reshape(width, 128)
    attention_grad = jnp.concatenate(
        [qkv_weight_grad, output_weight_grad, gain_grads], axis=1
    ).astype(bf16)
    attention_grad, gate_up_share = lax.optimization_barrier((attention_grad, gate_up_share))
    attention_parts, normed_input_grad = finish_sums(attention_grad, input_part)
    attention_parts = attention_parts.astype(f32)
    normed_input_grad = normed_input_grad[None]
    _, norm_one_back = jax.vjp(lambda v: rms_scale(v, operator_scale), own_f32)
    (input_norm_grad,) = norm_one_back(normed_input_grad)
    input_grad = in_order(hidden_grad + input_norm_grad, "tensor", 1)

    def ctx_parts(share):
        size = lax.axis_size("ctx")
        parts = jnp.zeros((size,) + share.shape, share.dtype)
        for step in range(size):
            piece = share if step == 0 else shift(share, "ctx", step)
            owner = lax.rem(me_c - step + size, size)
            parts = lax.dynamic_update_slice(parts, piece[None], (owner, 0, 0))
        return parts.astype(f32)

    def columns(parts):
        return jnp.moveaxis(parts, 0, 1).reshape(parts.shape[1], -1)

    gate_up_parts = ctx_parts(gate_up_share)
    down_parts = ctx_parts(down_share)

    def head_columns(parts):
        every = columns(parts)
        if copies == 1:
            return every
        return every.reshape(shard_rows, kv_shard, copies, head_width).sum(axis=2).reshape(
            shard_rows, -1
        )

    query_weight_grad = columns(attention_parts[:, :, :q_cols])
    key_weight_grad = head_columns(attention_parts[:, :, q_cols : q_cols + kv_cols])
    value_weight_grad = head_columns(attention_parts[:, :, q_cols + kv_cols : qkv_cols])
    gate_weight_grad = columns(gate_up_parts[:, :, :hidden_units])
    up_weight_grad = columns(gate_up_parts[:, :, hidden_units:])
    gain_parts = attention_parts[:, :, qkv_cols + q_cols : qkv_cols + q_cols + 2].sum(axis=0)

    def gain_part(pairs, gain):
        total = 0.0
        for weight, grad in pairs:
            total = total + jnp.sum(weight.astype(f32) * grad, axis=1)
        return total / gain.astype(f32)

    gain_columns = jnp.concatenate(
        [
            gain_part(
                [
                    (query_weight, query_weight_grad),
                    (key_weight, key_weight_grad),
                    (value_weight, value_weight_grad),
                ],
                operator_gain,
            )[:, None],
            gain_part(
                [(gate_weight, gate_weight_grad), (up_weight, up_weight_grad)], feedforward_gain
            )[:, None],
            gain_parts,
        ],
        axis=1,
    )
    gain_totals = gain_columns
    for step in range(1, tensor):
        gain_totals = gain_totals + shift(gain_columns, "tensor", step)

    return (
        block_output,
        input_grad,
        gain_totals[:, 0],
        query_weight_grad,
        key_weight_grad,
        value_weight_grad,
        jnp.swapaxes(attention_parts[:, :, qkv_cols : qkv_cols + q_cols], 1, 2).reshape(
            -1, shard_rows
        ),
        gain_totals[:, 1],
        gate_weight_grad,
        up_weight_grad,
        down_parts.reshape(-1, shard_rows),
        gain_totals[:gain_rows, 2],
        gain_totals[:gain_rows, 3],
    )


def solution(mesh):
    in_specs = (
        P("fsdp", "ctx", None),
        P("fsdp"),
        P("fsdp", "tensor"),
        P("fsdp", "tensor"),
        P("fsdp", "tensor"),
        P("tensor", "fsdp"),
        P("fsdp"),
        P("fsdp", "tensor"),
        P("fsdp", "tensor"),
        P("tensor", "fsdp"),
        P("fsdp"),
        P("fsdp"),
        P("fsdp", "ctx", None),
    )
    out_specs = (
        P("fsdp", "ctx", None),
        P("fsdp", "ctx", None),
        P("fsdp"),
        P("fsdp", "tensor"),
        P("fsdp", "tensor"),
        P("fsdp", "tensor"),
        P("tensor", "fsdp"),
        P("fsdp"),
        P("fsdp", "tensor"),
        P("fsdp", "tensor"),
        P("tensor", "fsdp"),
        P("fsdp"),
        P("fsdp"),
    )
    return jax.shard_map(shards, mesh=mesh, in_specs=in_specs, out_specs=out_specs, check_vma=False)
```

```python
import jax
import jax.numpy as jnp
from jax import lax
from jax.experimental import pallas as pl
from jax.experimental.pallas import tpu as pltpu
from jax.sharding import PartitionSpec as P

EPS = 1e-05
THETA = 1000000.0


def rms_scale(values_in, gain):
    return (
        values_in * lax.rsqrt(jnp.mean(values_in * values_in, axis=-1, keepdims=True) + EPS) * gain
    )


def rotary_tables(positions, head_width):
    half_width = head_width // 2
    freqs = THETA ** (-jnp.arange(half_width).astype(jnp.float32) * 2.0 / head_width)
    angles = positions.astype(jnp.float32)[:, None] * freqs[None, :]
    return (jnp.cos(angles), jnp.sin(angles))


def rotate_halves(heads_in, cosine, sine):
    half_width = heads_in.shape[-1] // 2
    front_half = heads_in[..., :half_width]
    back_half = heads_in[..., half_width:]
    cos_rows = cosine[:, None, :]
    sin_rows = sine[:, None, :]
    return jnp.concatenate(
        [
            front_half * cos_rows - back_half * sin_rows,
            back_half * cos_rows + front_half * sin_rows,
        ],
        axis=-1,
    )


def head_prepare(raw, gain, cosine, sine):
    head_width = gain.shape[0]
    shaped = raw.reshape(raw.shape[:-1] + (raw.shape[-1] // head_width, head_width))
    return rotate_halves(rms_scale(shaped, gain), cosine, sine)


def swiglu(gate, upper):
    return jax.nn.silu(gate) * upper


def contract(left, right, left_dim, right_dim):
    return lax.dot_general(
        left, right, (((left_dim,), (right_dim,)), ((), ())), preferred_element_type=jnp.float32
    )


def block_scores(query_block, keys, query_pos, key_pos):
    scale = 1.0 / query_block.shape[-1] ** 0.5
    scores = (
        jnp.einsum("qhd,khd->hqk", query_block, keys, preferred_element_type=jnp.float32) * scale
    )
    allowed = key_pos[None, :] <= query_pos[:, None]
    return jnp.where(allowed[None, :, :], scores, -1e30)


def attend(queries, keys, values, positions):
    length = queries.shape[0]
    block_rows = min(512, length)
    outputs = []
    totals = []
    for start in range(0, length, block_rows):
        rows = slice(start, start + block_rows)
        scores = block_scores(queries[rows], keys, positions[rows], positions)
        peak = jnp.max(scores, axis=-1, keepdims=True)
        log_total = peak + jnp.log(jnp.sum(jnp.exp(scores - peak), axis=-1, keepdims=True))
        probs = jnp.exp(scores - log_total).astype(jnp.bfloat16)
        block_out = jnp.einsum("hqk,khd->qhd", probs, values, preferred_element_type=jnp.float32)
        outputs.append(block_out.astype(jnp.bfloat16))
        totals.append(log_total[..., 0])
    return (jnp.concatenate(outputs, axis=0), jnp.concatenate(totals, axis=1))


def attend_grad(queries, keys, values, outputs, totals, out_grad, positions):
    length = queries.shape[0]
    block_rows = min(512, length)
    scale = 1.0 / queries.shape[-1] ** 0.5
    key_acc = jnp.zeros(keys.shape, jnp.float32)
    value_acc = jnp.zeros(values.shape, jnp.float32)
    query_parts = []
    for start in range(0, length, block_rows):
        rows = slice(start, start + block_rows)
        query_block = queries[rows]
        scores = block_scores(query_block, keys, positions[rows], positions)
        probs = jnp.exp(scores - totals[:, rows][..., None])
        grad_block = out_grad[rows]
        value_acc = value_acc + jnp.einsum(
            "hqk,qhd->khd",
            probs.astype(jnp.bfloat16),
            grad_block,
            preferred_element_type=jnp.float32,
        )
        prob_grad = jnp.einsum(
            "qhd,khd->hqk", grad_block, values, preferred_element_type=jnp.float32
        )
        delta = jnp.sum(
            grad_block.astype(jnp.float32) * outputs[rows].astype(jnp.float32),
            axis=-1,
        ).T
        score_grad = (probs * (prob_grad - delta[..., None])).astype(jnp.bfloat16)
        query_parts.append(
            (
                jnp.einsum("hqk,khd->qhd", score_grad, keys, preferred_element_type=jnp.float32)
                * scale
            ).astype(jnp.bfloat16)
        )
        key_acc = (
            key_acc
            + jnp.einsum(
                "hqk,qhd->khd", score_grad, query_block, preferred_element_type=jnp.float32
            )
            * scale
        )
    return (
        jnp.concatenate(query_parts, axis=0),
        key_acc.astype(jnp.bfloat16),
        value_acc.astype(jnp.bfloat16),
    )


def shift(array, axis_name, step):
    size = lax.axis_size(axis_name)
    return lax.ppermute(array, axis_name, [(i, (i + step) % size) for i in range(size)])


def around(array, axis_name, dim):
    size = lax.axis_size(axis_name)
    return jnp.concatenate(
        [array] + [shift(array, axis_name, step) for step in range(1, size)], axis=dim
    )


def group_rows(array):
    return around(around(array, "ctx", 1), "tensor", 1)


def sum_around(array, axis_name):
    size = lax.axis_size(axis_name)
    part = array.shape[1] // size
    total = array[:, :part].astype(jnp.float32)
    for step in range(1, size):
        piece = array[:, step * part : (step + 1) * part].astype(jnp.bfloat16)
        total = total + shift(piece, axis_name, -step).astype(jnp.float32)
    return total


def group_sum(array):
    return sum_around(sum_around(array, "tensor"), "ctx")


def in_order(array, axis_name, dim):
    size = lax.axis_size(axis_name)
    me = lax.axis_index(axis_name)
    width = array.shape[dim]
    shape = list(array.shape)
    shape[dim] = width * size
    out = jnp.zeros(shape, array.dtype)
    for step in range(size):
        piece = array if step == 0 else shift(array, axis_name, step)
        owner = lax.rem(me - step + size, size)
        out = lax.dynamic_update_slice_in_dim(out, piece, owner * width, dim)
    return out


def ring_index(place, size):
    if size % 2:
        return place
    turn = size // 2
    return jnp.where(place < turn, 2 * place, 2 * (size - 1 - place) + 1)


def ring_place(index, size):
    if size % 2:
        return index
    return jnp.where(lax.rem(index, 2) == 0, lax.div(index, 2), size - 1 - lax.div(index, 2))


def ring_order(size):
    if size % 2:
        return list(range(size))
    return [2 * i for i in range(size // 2)] + [2 * i + 1 for i in reversed(range(size // 2))]


def ring_shift(array, axis_name, step):
    size = lax.axis_size(axis_name)
    order = ring_order(size)
    pairs = [(order[i], order[(i + step) % size]) for i in range(size)]
    return lax.ppermute(array, axis_name, pairs)


def ring_gather(shard, axis_name, dim=0):
    size = lax.axis_size(axis_name)
    place = ring_place(lax.axis_index(axis_name), size)
    shape = list(shard.shape)
    shape[dim] *= size
    half = shard.shape[0] // 2
    out = jnp.zeros(shape, shard.dtype)

    def put(out, piece, at, offset):
        owner = ring_index(lax.rem(at + size, size), size)
        starts = [offset, 0]
        starts[dim] += owner * shard.shape[dim]
        return lax.dynamic_update_slice(out, piece, starts)

    out = put(out, shard, place, 0)
    rightward = leftward = shard
    for step in range(1, (size + 1) // 2):
        rightward = ring_shift(rightward, axis_name, 1)
        leftward = ring_shift(leftward, axis_name, -1)
        out = put(out, rightward, place - step, 0)
        out = put(out, leftward, place + step, 0)
    if size % 2 == 0:
        rightward = ring_shift(rightward[:half], axis_name, 1)
        leftward = ring_shift(leftward[half:], axis_name, -1)
        out = put(out, rightward, place + size // 2, 0)
        out = put(out, leftward, place + size // 2, half)
    return out, rightward


def ring_scatter(piece_for, axis_name):
    size = lax.axis_size(axis_name)
    place = ring_place(lax.axis_index(axis_name), size)

    def piece(offset):
        return piece_for(ring_index(lax.rem(place + offset + size, size), size))

    mine = piece(0).astype(jnp.float32)
    if size == 1:
        return mine
    half = mine.shape[0] // 2
    far = size // 2
    bf16 = jnp.bfloat16
    f32 = jnp.float32
    if size % 2 == 0:
        across = piece(far)
        rightward = ring_shift(across[:half].astype(bf16), axis_name, 1).astype(f32)
        leftward = ring_shift(across[half:].astype(bf16), axis_name, -1).astype(f32)
        zero = jnp.zeros_like(mine[:half])
        rightward = jnp.concatenate([rightward, zero], axis=0)
        leftward = jnp.concatenate([zero, leftward], axis=0)
        steps = far - 1
    else:
        rightward = leftward = jnp.zeros_like(mine)
        steps = far
    for step in range(steps, 0, -1):
        rightward = ring_shift((rightward + piece(step)).astype(bf16), axis_name, 1).astype(f32)
        leftward = ring_shift((leftward + piece(-step)).astype(bf16), axis_name, -1).astype(f32)
    return mine + rightward + leftward


def other(axis_name, step):
    size = lax.axis_size(axis_name)
    return {axis_name: lax.rem(lax.axis_index(axis_name) + step + size, size)}


def send(source, target, send_sem, recv_sem, device):
    copy = pltpu.make_async_remote_copy(
        src_ref=source,
        dst_ref=target,
        send_sem=send_sem,
        recv_sem=recv_sem,
        device_id=device,
        device_id_type=pl.DeviceIdType.MESH,
    )
    copy.start()
    return copy


def ring_ends():
    size = lax.axis_size("fsdp")
    place = ring_place(lax.axis_index("fsdp"), size)

    def at(offset):
        return ring_index(lax.rem(place + offset + size, size), size)

    return at, ({"fsdp": at(1)}, {"fsdp": at(-1)})


def greet():
    _, ends = ring_ends()
    partners = list(ends)
    for axis_name in ("ctx", "tensor"):
        partners += [other(axis_name, step) for step in range(1, lax.axis_size(axis_name))]
    barrier = pltpu.get_barrier_semaphore()
    for device in partners:
        pl.semaphore_signal(
            barrier, inc=1, device_id=device, device_id_type=pl.DeviceIdType.MESH
        )
    pl.semaphore_wait(barrier, len(partners))


def start_kernel(
    pack_ref,
    input_ref,
    upstream_ref,
    full_ref,
    all_input_ref,
    all_upstream_ref,
    ring_send,
    ring_recv,
    ctx_send,
    ctx_recv,
    tensor_send,
    tensor_recv,
    local_sem,
):
    size = lax.axis_size("fsdp")
    ctx = lax.axis_size("ctx")
    tensor = lax.axis_size("tensor")
    me_t = lax.axis_index("tensor")
    far = size // 2
    rows = pack_ref.shape[0]
    sub_rows = rows // 2
    quarter = all_input_ref.shape[2]
    at, ends = ring_ends()
    greet()
    pairs = ((input_ref, all_input_ref), (upstream_ref, all_upstream_ref))

    def block(owner, sub):
        start = pl.multiple_of(owner * rows + sub * sub_rows, sub_rows)
        return full_ref.at[pl.ds(start, sub_rows)]

    sends = []
    arrivals = {}

    def ring_step(step):
        for sub in range(2):
            for way in range(2):
                if step == far and sub != way:
                    continue
                if step > 1:
                    arrivals.pop((way, step - 1, sub)).wait_recv()
                owner = at((1 - step) if way == 0 else (step - 1))
                source = (
                    pack_ref.at[pl.ds(sub * sub_rows, sub_rows)] if step == 1 else block(owner, sub)
                )
                copy = send(
                    source,
                    block(owner, sub),
                    ring_send.at[way, step - 1, sub],
                    ring_recv.at[way, step - 1, sub],
                    ends[way],
                )
                sends.append(copy)
                arrivals[way, step, sub] = copy

    def own_rows(source, step):
        quarter_at = lax.rem(me_t - step + tensor, tensor)
        return source.at[0, pl.ds(pl.multiple_of(quarter_at * quarter, quarter), quarter)]

    ring_step(1)
    crossed = {}
    locals_ = []
    for which, (source, target) in enumerate(pairs):
        for step in range(1, ctx):
            copy = send(
                own_rows(source, 0),
                target.at[0, step],
                ctx_send.at[which, step - 1],
                ctx_recv.at[which, step - 1],
                other("ctx", step),
            )
            sends.append(copy)
            crossed[which, step] = copy
    for which, (source, target) in enumerate(pairs):
        for step in range(tensor):
            copy = pltpu.make_async_copy(
                own_rows(source, step), target.at[step, 0], local_sem.at[which, step]
            )
            copy.start()
            locals_.append(copy)
    own_copy = pltpu.make_async_copy(
        pack_ref,
        full_ref.at[pl.ds(pl.multiple_of(at(0) * rows, rows), rows)],
        local_sem.at[2, 0],
    )
    own_copy.start()
    locals_.append(own_copy)
    handed = []

    def hand_over(which):
        _, target = pairs[which]
        for step in range(1, ctx):
            crossed[which, step].wait_recv()
            for core in range(1, tensor):
                copy = send(
                    target.at[0, step],
                    target.at[core, step],
                    tensor_send.at[which, core - 1, step - 1],
                    tensor_recv.at[which, core - 1, step - 1],
                    other("tensor", core),
                )
                sends.append(copy)
                handed.append(copy)

    for step in range(2, far + 1):
        if step == far:
            hand_over(0)
        ring_step(step)
    if far < 2:
        hand_over(0)
    hand_over(1)
    for copy in arrivals.values():
        copy.wait_recv()
    for copy in handed:
        copy.wait_recv()
    for copy in sends:
        copy.wait_send()
    for copy in locals_:
        copy.wait()


def start_gather(pack, block_input, cotangent):
    size = lax.axis_size("fsdp")
    ctx = lax.axis_size("ctx")
    tensor = lax.axis_size("tensor")
    far = size // 2
    rows, columns = pack.shape
    _, tok_here, width = block_input.shape
    every = (tensor, ctx, tok_here // tensor, width)
    in_vmem = pl.BlockSpec(memory_space=pltpu.VMEM)
    dma = pltpu.SemaphoreType.DMA
    return pl.pallas_call(
        start_kernel,
        out_shape=(
            jax.ShapeDtypeStruct((rows * size, columns), pack.dtype),
            jax.ShapeDtypeStruct(every, block_input.dtype),
            jax.ShapeDtypeStruct(every, cotangent.dtype),
        ),
        in_specs=[in_vmem] * 3,
        out_specs=(in_vmem,) * 3,
        scratch_shapes=[
            dma((2, far, 2)),
            dma((2, far, 2)),
            dma((2, ctx)),
            dma((2, ctx)),
            dma((2, tensor, ctx)),
            dma((2, tensor, ctx)),
            dma((3, tensor)),
        ],
        compiler_params=pltpu.CompilerParams(
            collective_id=0, has_side_effects=True, vmem_limit_bytes=32 * 1024 * 1024
        ),
        name="start_gather",
    )(pack, block_input, cotangent)


def add_rows(count, block_rows, body):
    def step(index, carry):
        body(pl.ds(pl.multiple_of(index * block_rows, block_rows), block_rows))
        return carry

    lax.fori_loop(0, count // block_rows, step, 0)


def finish_kernel(
    grad_ref,
    part_ref,
    parts_ref,
    total_ref,
    going,
    coming,
    share,
    core_going,
    core_coming,
    ctx_going,
    ctx_coming,
    ring_send,
    ring_recv,
    core_send,
    core_recv,
    ctx_send,
    ctx_recv,
    share_send,
    share_recv,
    local_sem,
):
    f32 = jnp.float32
    bf16 = jnp.bfloat16
    size = lax.axis_size("fsdp")
    ctx = lax.axis_size("ctx")
    tensor = lax.axis_size("tensor")
    me_c = lax.axis_index("ctx")
    far = size // 2
    rows = share.shape[0]
    sub_rows = rows // 2
    quarter = part_ref.shape[2]
    at, ends = ring_ends()
    greet()
    sends = []
    arrivals = {}

    def own_block(owner, sub):
        return pl.ds(pl.multiple_of(owner * rows + sub * sub_rows, sub_rows), sub_rows)

    def ring_step(step):
        for sub in range(2):
            for way in range(2):
                if step == 1 and sub != way:
                    continue
                ahead = far + 1 - step
                owner = at(ahead if way == 0 else -ahead)
                mine = own_block(owner, sub)
                if step == 1:
                    source = grad_ref.at[mine]
                else:
                    source = going.at[way, step - 2, sub]
                    if (way, step - 1, sub) in arrivals:
                        arrivals.pop((way, step - 1, sub)).wait_recv()
                        source[...] = (
                            grad_ref[mine, :].astype(f32)
                            + coming[way, step - 2, sub].astype(f32)
                        ).astype(bf16)
                    else:
                        source = grad_ref.at[mine]
                copy = send(
                    source,
                    coming.at[way, step - 1, sub],
                    ring_send.at[way, step - 1, sub],
                    ring_recv.at[way, step - 1, sub],
                    ends[way],
                )
                sends.append(copy)
                arrivals[way, step, sub] = copy

    ring_step(1)
    by_core = []
    for core in range(1, tensor):
        for step in range(ctx):

            def narrow(block, core=core, step=step):
                core_going[core - 1, step, block] = part_ref[core, step, block].astype(bf16)

            add_rows(quarter, 32, narrow)
        copy = send(
            core_going.at[core - 1],
            core_coming.at[core - 1],
            core_send.at[core - 1],
            core_recv.at[core - 1],
            other("tensor", -core),
        )
        sends.append(copy)
        by_core.append(copy)
    if far > 1:
        ring_step(2)
    for copy in by_core:
        copy.wait_recv()
    by_ctx = []
    for step in list(range(1, ctx)) + [0]:

        def total(block, step=step):
            value = part_ref[0, step, block]
            for core in range(1, tensor):
                value = value + core_coming[core - 1, step, block].astype(f32)
            if step == 0:
                total_ref[block] = value
            else:
                ctx_going[step - 1, block] = value.astype(bf16)

        add_rows(quarter, 32, total)
        if step > 0:
            copy = send(
                ctx_going.at[step - 1],
                ctx_coming.at[step - 1],
                ctx_send.at[step - 1],
                ctx_recv.at[step - 1],
                other("ctx", -step),
            )
            sends.append(copy)
            by_ctx.append(copy)
    for step in range(3, far + 1):
        ring_step(step)
    mine = at(0)
    for sub in range(2):
        value = grad_ref[own_block(mine, sub), :].astype(f32)
        for way in range(2):
            if (way, far, sub) in arrivals:
                arrivals.pop((way, far, sub)).wait_recv()
                value = value + coming[way, far - 1, sub].astype(f32)
        share[sub * sub_rows : (sub + 1) * sub_rows, :] = value.astype(bf16)
    shared = []
    for step in range(1, ctx):
        copy = send(
            share,
            parts_ref.at[me_c],
            share_send.at[step - 1],
            share_recv.at[step - 1],
            other("ctx", step),
        )
        sends.append(copy)
        shared.append(copy)
    keep = pltpu.make_async_copy(share, parts_ref.at[me_c], local_sem)
    keep.start()
    for step in range(1, ctx):
        by_ctx[step - 1].wait_recv()

        def gather(block, step=step):
            total_ref[block] += ctx_coming[step - 1, block].astype(f32)

        add_rows(quarter, 32, gather)
    for step in range(1, ctx):
        shared[step - 1].wait_recv()
    for copy in sends:
        copy.wait_send()
    keep.wait()


def finish_sums(grad, part):
    size = lax.axis_size("fsdp")
    tensor, ctx, quarter, width = part.shape
    far = size // 2
    rows, columns = grad.shape[0] // size, grad.shape[1]
    in_vmem = pl.BlockSpec(memory_space=pltpu.VMEM)
    anywhere = pl.BlockSpec(memory_space=pl.ANY)
    dma = pltpu.SemaphoreType.DMA
    bf16 = jnp.bfloat16
    return pl.pallas_call(
        finish_kernel,
        out_shape=(
            jax.ShapeDtypeStruct((ctx, rows, columns), bf16),
            jax.ShapeDtypeStruct((quarter, width), jnp.float32),
        ),
        in_specs=[in_vmem] * 2,
        out_specs=(anywhere, in_vmem),
        scratch_shapes=[
            pltpu.VMEM((2, max(1, far - 1), 2, rows // 2, columns), bf16),
            pltpu.VMEM((2, far, 2, rows // 2, columns), bf16),
            pltpu.VMEM((rows, columns), bf16),
            pltpu.VMEM((max(1, tensor - 1), ctx, quarter, width), bf16),
            pltpu.VMEM((max(1, tensor - 1), ctx, quarter, width), bf16),
            pltpu.VMEM((max(1, ctx - 1), quarter, width), bf16),
            pltpu.VMEM((max(1, ctx - 1), quarter, width), bf16),
            dma((2, far, 2)),
            dma((2, far, 2)),
            dma((tensor,)),
            dma((tensor,)),
            dma((ctx,)),
            dma((ctx,)),
            dma((ctx,)),
            dma((ctx,)),
            dma(()),
        ],
        compiler_params=pltpu.CompilerParams(
            collective_id=1, has_side_effects=True, vmem_limit_bytes=48 * 1024 * 1024
        ),
        name="finish_sums",
    )(grad, part)


def gather_ring(shard_ref, full_ref, send_sem, recv_sem):
    size = lax.axis_size("fsdp")
    far = size // 2
    rows = shard_ref.shape[0]
    sub_rows = rows // 2
    at, ends = ring_ends()
    sends = []
    arrivals = {}
    queue = [(step, sub) for step in range(1, far + 1) for sub in range(2)]

    def block(owner, sub):
        start = pl.multiple_of(owner * rows + sub * sub_rows, sub_rows)
        return full_ref.at[pl.ds(start, sub_rows)]

    def go(count):
        for _ in range(min(count, len(queue))):
            step, sub = queue.pop(0)
            for way in range(2):
                if step > 1 and (step < far or sub == way):
                    arrivals.pop((way, step - 1, sub)).wait_recv()
                if step == far and sub != way:
                    continue
                owner = at((1 - step) if way == 0 else (step - 1))
                source = (
                    shard_ref.at[pl.ds(sub * sub_rows, sub_rows)] if step == 1 else block(owner, sub)
                )
                copy = send(
                    source,
                    block(owner, sub),
                    send_sem.at[way, step - 1, sub],
                    recv_sem.at[way, step - 1, sub],
                    ends[way],
                )
                sends.append(copy)
                arrivals[way, step, sub] = copy

    def finish():
        go(len(queue))
        for copy in arrivals.values():
            copy.wait_recv()
        for copy in sends:
            copy.wait_send()

    return go, finish


def scatter_ring(grad_ref, coming, send_sem, recv_sem):
    f32 = jnp.float32
    size = lax.axis_size("fsdp")
    far = size // 2
    rows = grad_ref.shape[0] // size
    sub_rows = rows // 2
    step_rows = 16
    at, ends = ring_ends()
    sends = []
    arrivals = {}
    queue = [(1, 0, 0), (1, 1, 1)]
    for step in range(2, far + 1):
        queue += [(step, 1, 0), (step, 0, 1), (step, 0, 0), (step, 1, 1)]

    def start_of(owner, sub):
        return pl.multiple_of(owner * rows + sub * sub_rows, sub_rows)

    def go(count):
        for _ in range(min(count, len(queue))):
            step, way, sub = queue.pop(0)
            ahead = far + 1 - step
            first = start_of(at(ahead if way == 0 else -ahead), sub)
            if (way, step - 1, sub) in arrivals:
                arrivals.pop((way, step - 1, sub)).wait_recv()

                def add(index, carry, way=way, step=step, sub=sub, first=first):
                    here = pl.ds(pl.multiple_of(index * step_rows, step_rows), step_rows)
                    there = pl.ds(
                        pl.multiple_of(first + index * step_rows, step_rows), step_rows
                    )
                    grad_ref[there] = (
                        grad_ref[there].astype(f32) + coming[way, step - 2, sub, here].astype(f32)
                    ).astype(grad_ref.dtype)
                    return carry

                lax.fori_loop(0, sub_rows // step_rows, add, 0)
            copy = send(
                grad_ref.at[pl.ds(first, sub_rows)],
                coming.at[way, step - 1, sub],
                send_sem.at[way, step - 1, sub],
                recv_sem.at[way, step - 1, sub],
                ends[way],
            )
            sends.append(copy)
            arrivals[way, step, sub] = copy

    def finish(share_ref):
        go(len(queue))
        for sub in range(2):
            landed = []
            for way in range(2):
                if (way, far, sub) in arrivals:
                    arrivals.pop((way, far, sub)).wait_recv()
                    landed.append(way)

            def add(index, carry, sub=sub, landed=landed):
                here = pl.ds(pl.multiple_of(index * step_rows, step_rows), step_rows)
                there = pl.ds(
                    pl.multiple_of(start_of(at(0), sub) + index * step_rows, step_rows), step_rows
                )
                out = pl.ds(
                    pl.multiple_of(sub * sub_rows + index * step_rows, step_rows), step_rows
                )
                value = grad_ref[there].astype(f32)
                for way in landed:
                    value = value + coming[way, far - 1, sub, here].astype(f32)
                share_ref[out] = value.astype(share_ref.dtype)
                return carry

            lax.fori_loop(0, sub_rows // step_rows, add, 0)
        for copy in sends:
            copy.wait_send()

    return go, finish


def slot_base(slot, quarter):
    ctx = lax.axis_size("ctx")
    tensor = lax.axis_size("tensor")
    of_core = lax.rem(lax.axis_index("tensor") - lax.div(slot, ctx) + tensor, tensor)
    of_ctx = lax.rem(lax.axis_index("ctx") - lax.rem(slot, ctx) + ctx, ctx)
    return of_core * quarter + of_ctx * (quarter * tensor)


def reachable(query_slot, key_slot, quarter):
    gap = slot_base(query_slot, quarter) - slot_base(key_slot, quarter)
    return gap, gap > -quarter


def masked_scores(keys, queries, gap):
    scores = lax.dot_general(
        keys, queries, (((1,), (1,)), ((), ())), preferred_element_type=jnp.float32
    ) * (1.0 / queries.shape[-1] ** 0.5)
    key_at = lax.broadcasted_iota(jnp.int32, scores.shape, 0)
    query_at = lax.broadcasted_iota(jnp.int32, scores.shape, 1)
    return jnp.where(key_at - query_at <= gap, scores, -1e30)


def attend_slot(slot, q_ref, k_ref, vt_ref, attended_ref, turned_ref, total_ref, work):
    scores_ref, peak_ref, sum_ref, out_ref = work
    slots, heads, quarter, head_width = q_ref.shape
    group = heads // k_ref.shape[1]

    def one_head(head, carry):
        kv_head = lax.div(head, group)
        peak_ref[...] = jnp.full(peak_ref.shape, -1e30, jnp.float32)
        sum_ref[...] = jnp.zeros(sum_ref.shape, jnp.float32)
        out_ref[...] = jnp.zeros(out_ref.shape, jnp.float32)

        def score(key_slot, carry):
            gap, seen = reachable(slot, key_slot, quarter)

            @pl.when(seen)
            def _():
                scores = masked_scores(k_ref[key_slot, kv_head], q_ref[slot, head], gap)
                scores_ref[key_slot] = scores
                peak_ref[...] = jnp.maximum(peak_ref[...], jnp.max(scores, axis=0, keepdims=True))

            return carry

        lax.fori_loop(0, slots, score, 0)

        def weigh(key_slot, carry):
            _, seen = reachable(slot, key_slot, quarter)

            @pl.when(seen)
            def _():
                raised = jnp.exp(scores_ref[key_slot] - peak_ref[...])
                sum_ref[...] += jnp.sum(raised, axis=0, keepdims=True)
                out_ref[...] += jnp.dot(
                    vt_ref[key_slot, kv_head],
                    raised.astype(jnp.bfloat16),
                    preferred_element_type=jnp.float32,
                )

            return carry

        lax.fori_loop(0, slots, weigh, 0)
        total_ref[slot, head] = peak_ref[...] + jnp.log(sum_ref[...])
        rows = pl.ds(pl.multiple_of(head * head_width, head_width), head_width)
        turned_ref[slot, rows] = (out_ref[...] / sum_ref[...]).astype(jnp.bfloat16)
        return carry

    lax.fori_loop(0, heads, one_head, 0)
    attended_ref[slot] = turned_ref[slot].astype(jnp.float32).T.astype(jnp.bfloat16)


def forward_kernel(
    shard_ref,
    q_ref,
    k_ref,
    vt_ref,
    weight_ref,
    own_ref,
    gain_ref,
    full_ref,
    attended_ref,
    turned_ref,
    total_ref,
    hidden_ref,
    normed_ref,
    scores_ref,
    peak_ref,
    sum_ref,
    out_ref,
    part_ref,
    core_going,
    core_coming,
    ctx_going,
    ctx_coming,
    ring_send,
    ring_recv,
    core_send,
    core_recv,
    ctx_send,
    ctx_recv,
    spread_send,
    spread_recv,
    local_sem,
):
    f32 = jnp.float32
    bf16 = jnp.bfloat16
    ctx = lax.axis_size("ctx")
    tensor = lax.axis_size("tensor")
    slots, _, quarter, _ = q_ref.shape
    rows = shard_ref.shape[0]
    greet()
    go, finish = gather_ring(shard_ref, full_ref, ring_send, ring_recv)
    go(2)
    keep = pltpu.make_async_copy(
        shard_ref,
        full_ref.at[pl.ds(pl.multiple_of(ring_ends()[0](0) * rows, rows), rows)],
        local_sem,
    )
    keep.start()
    work = (scores_ref, peak_ref, sum_ref, out_ref)

    def project(slot):
        attend_slot(slot, q_ref, k_ref, vt_ref, attended_ref, turned_ref, total_ref, work)
        return lax.dot_general(
            attended_ref[slot],
            weight_ref[...],
            (((1,), (1,)), ((), ())),
            preferred_element_type=f32,
        )

    sends = []
    by_core = {}
    by_ctx = {}
    for core in range(1, tensor):
        for step in list(range(1, ctx)) + [0]:
            core_going[core - 1, step] = project(core * ctx + step).astype(bf16)
            copy = send(
                core_going.at[core - 1, step],
                core_coming.at[core - 1, step],
                core_send.at[core - 1, step],
                core_recv.at[core - 1, step],
                other("tensor", -core),
            )
            sends.append(copy)
            by_core[core, step] = copy
    for step in list(range(1, ctx)) + [0]:
        part_ref[...] = project(step)
        for core in range(1, tensor):
            by_core[core, step].wait_recv()
            part_ref[...] += core_coming[core - 1, step].astype(f32)
        if step > 0:
            ctx_going[step - 1] = part_ref[...].astype(bf16)
            copy = send(
                ctx_going.at[step - 1],
                ctx_coming.at[step - 1],
                ctx_send.at[step - 1],
                ctx_recv.at[step - 1],
                other("ctx", -step),
            )
            sends.append(copy)
            by_ctx[step] = copy
        if step < 2:
            go(1)
    for step in range(1, ctx):
        by_ctx[step].wait_recv()
        part_ref[...] += ctx_coming[step - 1].astype(f32)

    def norm(block):
        hidden = own_ref[block].astype(f32) + part_ref[block]
        hidden_ref[block] = hidden
        scale = lax.rsqrt(jnp.mean(hidden * hidden, axis=-1, keepdims=True) + EPS)
        normed_ref[0, 0, block] = (hidden * scale * gain_ref[...]).astype(bf16)

    add_rows(quarter, 16, norm)
    spread = []
    for step in range(1, ctx):
        copy = send(
            normed_ref.at[0, 0],
            normed_ref.at[0, step],
            spread_send.at[0, step],
            spread_recv.at[0, step],
            other("ctx", step),
        )
        sends.append(copy)
        spread.append(copy)
    handed = []

    def hand_over(step):
        for core in range(1, tensor):
            copy = send(
                normed_ref.at[0, step],
                normed_ref.at[core, step],
                spread_send.at[core, step],
                spread_recv.at[core, step],
                other("tensor", core),
            )
            sends.append(copy)
            handed.append(copy)

    hand_over(0)
    go(1)
    for step in range(1, ctx):
        spread[step - 1].wait_recv()
        hand_over(step)
    finish()
    for copy in handed:
        copy.wait_recv()
    for copy in sends:
        copy.wait_send()
    keep.wait()


def forward_gather(shard, queries, keys, values_turned, weight, own, gain):
    size = lax.axis_size("fsdp")
    ctx = lax.axis_size("ctx")
    tensor = lax.axis_size("tensor")
    far = size // 2
    rows, columns = shard.shape
    slots, heads, quarter, head_width = queries.shape
    width = own.shape[-1]
    q_cols = heads * head_width
    in_vmem = pl.BlockSpec(memory_space=pltpu.VMEM)
    dma = pltpu.SemaphoreType.DMA
    bf16 = jnp.bfloat16
    f32 = jnp.float32
    cores = max(1, tensor - 1)
    return pl.pallas_call(
        forward_kernel,
        out_shape=(
            jax.ShapeDtypeStruct((rows * size, columns), bf16),
            jax.ShapeDtypeStruct((slots, quarter, q_cols), bf16),
            jax.ShapeDtypeStruct((slots, q_cols, quarter), bf16),
            jax.ShapeDtypeStruct((slots, heads, 1, quarter), f32),
            jax.ShapeDtypeStruct((quarter, width), f32),
            jax.ShapeDtypeStruct((tensor, ctx, quarter, width), bf16),
        ),
        in_specs=[in_vmem] * 7,
        out_specs=(in_vmem,) * 6,
        scratch_shapes=[
            pltpu.VMEM((slots, quarter, quarter), f32),
            pltpu.VMEM((1, quarter), f32),
            pltpu.VMEM((1, quarter), f32),
            pltpu.VMEM((head_width, quarter), f32),
            pltpu.VMEM((quarter, width), f32),
            pltpu.VMEM((cores, ctx, quarter, width), bf16),
            pltpu.VMEM((cores, ctx, quarter, width), bf16),
            pltpu.VMEM((max(1, ctx - 1), quarter, width), bf16),
            pltpu.VMEM((max(1, ctx - 1), quarter, width), bf16),
            dma((2, far, 2)),
            dma((2, far, 2)),
            dma((cores, ctx)),
            dma((cores, ctx)),
            dma((ctx,)),
            dma((ctx,)),
            dma((tensor, ctx)),
            dma((tensor, ctx)),
            dma(()),
        ],
        compiler_params=pltpu.CompilerParams(
            collective_id=2, has_side_effects=True, vmem_limit_bytes=48 * 1024 * 1024
        ),
        name="forward_gather",
    )(shard, queries, keys, values_turned, weight, own, gain)


def group_reduce(part_ref, core_coming, ctx_going, ctx_coming, sems, sends):
    f32 = jnp.float32
    ctx = lax.axis_size("ctx")
    tensor = lax.axis_size("tensor")
    quarter = part_ref.shape[1]
    core_send, core_recv, ctx_send, ctx_recv = sems
    by_core = []
    by_ctx = []

    def over_cores():
        for core in range(1, tensor):
            copy = send(
                part_ref.at[pl.ds(core * ctx, ctx)],
                core_coming.at[core - 1],
                core_send.at[core - 1],
                core_recv.at[core - 1],
                other("tensor", -core),
            )
            sends.append(copy)
            by_core.append(copy)

    def over_ctx(sum_ref):
        for copy in by_core:
            copy.wait_recv()
        for step in list(range(1, ctx)) + [0]:

            def add(block, step=step):
                value = part_ref[step, block].astype(f32)
                for core in range(1, tensor):
                    value = value + core_coming[core - 1, step, block].astype(f32)
                if step == 0:
                    sum_ref[block] = value
                else:
                    ctx_going[step - 1, block] = value.astype(jnp.bfloat16)

            add_rows(quarter, 16, add)
            if step > 0:
                copy = send(
                    ctx_going.at[step - 1],
                    ctx_coming.at[step - 1],
                    ctx_send.at[step - 1],
                    ctx_recv.at[step - 1],
                    other("ctx", -step),
                )
                sends.append(copy)
                by_ctx.append(copy)

    def finish():
        for copy in by_ctx:
            copy.wait_recv()

    return over_cores, over_ctx, finish


def attend_slot_grad(slot, refs, turned_grad, accumulators):
    q_ref, k_ref, kt_ref, v_ref, turned_ref, total_ref, dq_ref = refs
    dq_acc, dk_acc, dv_acc = accumulators
    f32 = jnp.float32
    bf16 = jnp.bfloat16
    slots, heads, quarter, head_width = q_ref.shape
    group = heads // k_ref.shape[1]
    scale = 1.0 / head_width**0.5

    def one_head(head, carry):
        kv_head = lax.div(head, group)
        rows = pl.ds(pl.multiple_of(head * head_width, head_width), head_width)
        grad = turned_grad[rows]
        delta = jnp.sum(
            grad.astype(f32) * turned_ref[slot, rows].astype(f32), axis=0, keepdims=True
        )
        dq_acc[...] = jnp.zeros(dq_acc.shape, f32)

        def one_key_slot(key_slot, carry):
            gap, seen = reachable(slot, key_slot, quarter)

            @pl.when(seen)
            def _():
                queries = q_ref[slot, head]
                scores = masked_scores(k_ref[key_slot, kv_head], queries, gap)
                probs = jnp.exp(scores - total_ref[slot, head])
                prob_grad = jnp.dot(v_ref[key_slot, kv_head], grad, preferred_element_type=f32)
                score_grad = (probs * (prob_grad - delta)).astype(bf16)
                dv_acc[key_slot, head] += lax.dot_general(
                    probs.astype(bf16), grad, (((1,), (1,)), ((), ())), preferred_element_type=f32
                )
                dk_acc[key_slot, head] += jnp.dot(score_grad, queries, preferred_element_type=f32)
                dq_acc[...] += jnp.dot(
                    kt_ref[key_slot, kv_head], score_grad, preferred_element_type=f32
                )

            return carry

        lax.fori_loop(0, slots, one_key_slot, 0)
        dq_ref[slot, head] = (dq_acc[...] * scale).astype(bf16)
        return carry

    lax.fori_loop(0, heads, one_head, 0)


def backward_kernel(
    hidden_part_ref,
    down_part_ref,
    normed_ref,
    upstream_ref,
    gate_up_ref,
    activation_ref,
    hidden_ref,
    own_upstream_ref,
    gain_ref,
    weight_ref,
    q_ref,
    k_ref,
    kt_ref,
    v_ref,
    turned_ref,
    total_ref,
    share_ref,
    hidden_grad_ref,
    all_grad_ref,
    output_ref,
    dq_ref,
    dk_ref,
    dv_ref,
    grad_ref,
    coming,
    core_coming,
    ctx_going,
    ctx_coming,
    sum_ref,
    out_sum_ref,
    turned_grad,
    own_output,
    dq_acc,
    dk_acc,
    dv_acc,
    ring_send,
    ring_recv,
    core_send,
    core_recv,
    ctx_send,
    ctx_recv,
    spread_send,
    spread_recv,
    output_send,
    output_recv,
    local_sem,
):
    f32 = jnp.float32
    bf16 = jnp.bfloat16
    size = lax.axis_size("fsdp")
    ctx = lax.axis_size("ctx")
    tensor = lax.axis_size("tensor")
    me_t = lax.axis_index("tensor")
    far = size // 2
    slots, heads, quarter, head_width = q_ref.shape
    rows = grad_ref.shape[0] // size
    gate_up_cols = gate_up_ref.shape[1]
    hidden_units = activation_ref.shape[1]
    at, _ = ring_ends()
    sends = []
    greet()
    reduce_hidden = group_reduce(
        hidden_part_ref,
        core_coming.at[0],
        ctx_going.at[0],
        ctx_coming.at[0],
        (core_send.at[0], core_recv.at[0], ctx_send.at[0], ctx_recv.at[0]),
        sends,
    )
    reduce_down = group_reduce(
        down_part_ref,
        core_coming.at[1],
        ctx_going.at[1],
        ctx_coming.at[1],
        (core_send.at[1], core_recv.at[1], ctx_send.at[1], ctx_recv.at[1]),
        sends,
    )
    go, finish_ring = scatter_ring(grad_ref, coming, ring_send, ring_recv)

    def piece(offset):
        here = pl.ds(pl.multiple_of(at(offset) * rows, rows), rows)
        for start in range(0, gate_up_cols, hidden_units):
            columns = slice(start, start + hidden_units)
            grad_ref[here, columns] = jnp.dot(
                normed_ref[here], gate_up_ref[:, columns], preferred_element_type=f32
            ).astype(bf16)
        grad_ref[here, gate_up_cols:] = jnp.dot(
            upstream_ref[here], activation_ref[...], preferred_element_type=f32
        ).astype(bf16)

    def pieces(offset):
        piece(offset)
        piece(-offset)

    reduce_hidden[0]()
    piece(far)
    go(2)
    reduce_hidden[1](sum_ref)
    reduce_down[0]()
    ready = 0
    if far > 1:
        pieces(far - 1)
        go(2)
        ready = 1
    dk_acc[...] = jnp.zeros(dk_acc.shape, f32)
    dv_acc[...] = jnp.zeros(dv_acc.shape, f32)
    if far > 2:
        pieces(far - 2)
        ready = 2
    go(2)
    reduce_hidden[2]()

    def norm_back(block):
        grad = sum_ref[block]
        for step in range(1, ctx):
            grad = grad + ctx_coming[0, step - 1, block].astype(f32)
        hidden = hidden_ref[block]
        scale = lax.rsqrt(jnp.mean(hidden * hidden, axis=-1, keepdims=True) + EPS)
        grad = grad * gain_ref[...]
        inner = jnp.mean(grad * hidden, axis=-1, keepdims=True) * (scale * scale)
        grad = own_upstream_ref[block].astype(f32) + scale * (grad - hidden * inner)
        hidden_grad_ref[block] = grad
        all_grad_ref[0, block] = grad.astype(bf16)

    add_rows(quarter, 16, norm_back)
    spread = []
    handed = {}
    for step in range(1, ctx):
        copy = send(
            all_grad_ref.at[0],
            all_grad_ref.at[step],
            spread_send.at[0, step],
            spread_recv.at[0, step],
            other("ctx", step),
        )
        sends.append(copy)
        spread.append(copy)

    def hand_over(step):
        for core in range(1, tensor):
            copy = send(
                all_grad_ref.at[step],
                all_grad_ref.at[core * ctx + step],
                spread_send.at[core, step],
                spread_recv.at[core, step],
                other("tensor", core),
            )
            sends.append(copy)
            handed[core, step] = copy

    hand_over(0)
    reduce_down[1](out_sum_ref)

    def attention_back(slot):
        grad = jnp.dot(all_grad_ref[slot], weight_ref[...], preferred_element_type=f32)
        turned_grad[...] = grad.T.astype(bf16)
        attend_slot_grad(
            slot,
            (q_ref, k_ref, kt_ref, v_ref, turned_ref, total_ref, dq_ref),
            turned_grad,
            (dq_acc, dk_acc, dv_acc),
        )

    if far > 2:
        go(2)
    attention_back(0)
    for core in range(1, tensor):
        handed[core, 0].wait_recv()
        attention_back(core * ctx)
    if far > 2:
        go(2)
    for step in range(1, ctx):
        spread[step - 1].wait_recv()
        hand_over(step)
        attention_back(step)
    for offset in range(far - ready - 1, 0, -1):
        pieces(offset)
    piece(0)
    go(2)
    for step in range(1, ctx):
        for core in range(1, tensor):
            handed[core, step].wait_recv()
            attention_back(core * ctx + step)
    go(2)
    scale = 1.0 / head_width**0.5
    for slot in range(slots):
        dk_ref[slot] = (dk_acc[slot] * scale).astype(bf16)
        dv_ref[slot] = dv_acc[slot].astype(bf16)
    reduce_down[2]()

    def output(block):
        value = hidden_ref[block] + out_sum_ref[block]
        for step in range(1, ctx):
            value = value + ctx_coming[1, step - 1, block].astype(f32)
        own_output[block] = value.astype(bf16)

    add_rows(quarter, 16, output)
    keep = pltpu.make_async_copy(own_output, output_ref.at[me_t], local_sem)
    keep.start()
    given = []
    for core in range(1, tensor):
        copy = send(
            own_output,
            output_ref.at[me_t],
            output_send.at[core],
            output_recv.at[core],
            other("tensor", core),
        )
        sends.append(copy)
        given.append(copy)
    finish_ring(share_ref)
    for copy in given:
        copy.wait_recv()
    for copy in sends:
        copy.wait_send()
    keep.wait()


def backward_scatter(
    hidden_part,
    down_part,
    normed_turned,
    upstream_turned,
    gate_up_grad,
    activation,
    hidden,
    own_upstream,
    gain,
    weight,
    queries,
    keys,
    keys_turned,
    values,
    attended_turned,
    totals,
):
    size = lax.axis_size("fsdp")
    ctx = lax.axis_size("ctx")
    tensor = lax.axis_size("tensor")
    far = size // 2
    slots, heads, quarter, head_width = queries.shape
    width = weight.shape[0]
    q_cols = weight.shape[1]
    rows = width // size
    columns = gate_up_grad.shape[1] + activation.shape[1]
    in_vmem = pl.BlockSpec(memory_space=pltpu.VMEM)
    dma = pltpu.SemaphoreType.DMA
    bf16 = jnp.bfloat16
    f32 = jnp.float32
    cores = max(1, tensor - 1)
    apart = max(1, ctx - 1)
    by_head = (slots, heads, quarter, head_width)
    return pl.pallas_call(
        backward_kernel,
        out_shape=(
            jax.ShapeDtypeStruct((rows, columns), bf16),
            jax.ShapeDtypeStruct((quarter, width), f32),
            jax.ShapeDtypeStruct((slots, quarter, width), bf16),
            jax.ShapeDtypeStruct((tensor, quarter, width), bf16),
            jax.ShapeDtypeStruct((slots, heads, head_width, quarter), bf16),
            jax.ShapeDtypeStruct(by_head, bf16),
            jax.ShapeDtypeStruct(by_head, bf16),
        ),
        in_specs=[in_vmem] * 16,
        out_specs=(in_vmem,) * 7,
        scratch_shapes=[
            pltpu.VMEM((width, columns), bf16),
            pltpu.VMEM((2, far, 2, rows // 2, columns), bf16),
            pltpu.VMEM((2, cores, ctx, quarter, width), bf16),
            pltpu.VMEM((2, apart, quarter, width), bf16),
            pltpu.VMEM((2, apart, quarter, width), bf16),
            pltpu.VMEM((quarter, width), f32),
            pltpu.VMEM((quarter, width), f32),
            pltpu.VMEM((q_cols, quarter), bf16),
            pltpu.VMEM((quarter, width), bf16),
            pltpu.VMEM((head_width, quarter), f32),
            pltpu.VMEM(by_head, f32),
            pltpu.VMEM(by_head, f32),
            dma((2, far, 2)),
            dma((2, far, 2)),
            dma((2, cores)),
            dma((2, cores)),
            dma((2, ctx)),
            dma((2, ctx)),
            dma((tensor, ctx)),
            dma((tensor, ctx)),
            dma((tensor,)),
            dma((tensor,)),
            dma(()),
        ],
        compiler_params=pltpu.CompilerParams(
            collective_id=3, has_side_effects=True, vmem_limit_bytes=60 * 1024 * 1024
        ),
        name="backward_scatter",
    )(
        hidden_part,
        down_part,
        normed_turned,
        upstream_turned,
        gate_up_grad,
        activation,
        hidden,
        own_upstream,
        gain,
        weight,
        queries,
        keys,
        keys_turned,
        values,
        attended_turned,
        totals,
    )


def part_of(array, dim, count, start):
    return lax.dynamic_slice_in_dim(array, start, count, dim)


def shards(
    block_input,
    operator_gain,
    query_weight,
    key_weight,
    value_weight,
    output_weight,
    feedforward_gain,
    gate_weight,
    up_weight,
    down_weight,
    query_gain,
    key_gain,
    cotangent,
):
    bf16 = jnp.bfloat16
    f32 = jnp.float32
    fsdp = lax.axis_size("fsdp")
    ctx = lax.axis_size("ctx")
    tensor = lax.axis_size("tensor")
    me_c = lax.axis_index("ctx")
    me_t = lax.axis_index("tensor")
    seqs, tok_here, width = block_input.shape
    quarter = tok_here // tensor
    tokens = tok_here * ctx
    rows = seqs * tokens
    gain_rows = query_gain.shape[0]
    head_width = gain_rows * fsdp
    heads_shard = query_weight.shape[1] // head_width
    kv_shard = key_weight.shape[1] // head_width
    spread = heads_shard // kv_shard
    heads = heads_shard // ctx
    kv = max(1, kv_shard // ctx)
    group = heads // kv
    copies = max(1, ctx // kv_shard)
    q_cols = heads * head_width
    kv_cols = kv * head_width
    kv_start = ((me_c * heads) // spread) * head_width
    hidden_units = gate_weight.shape[1] // ctx
    shard_rows = query_weight.shape[0]

    gains = jnp.stack(
        [
            operator_gain,
            feedforward_gain,
            jnp.pad(query_gain, (0, shard_rows - gain_rows)),
            jnp.pad(key_gain, (0, shard_rows - gain_rows)),
        ],
        axis=1,
    )
    attention_pack = jnp.concatenate(
        [
            part_of(query_weight, 1, q_cols, me_c * q_cols),
            part_of(key_weight, 1, kv_cols, kv_start),
            part_of(value_weight, 1, kv_cols, kv_start),
            part_of(output_weight, 0, q_cols, me_c * q_cols).T,
            jnp.pad(gains, ((0, 0), (0, 124))),
        ],
        axis=1,
    )
    feedforward_shard = jnp.concatenate(
        [
            part_of(gate_weight, 1, hidden_units, me_c * hidden_units),
            part_of(up_weight, 1, hidden_units, me_c * hidden_units),
            part_of(down_weight, 0, hidden_units, me_c * hidden_units).T,
        ],
        axis=1,
    )
    attention_full, all_input, upstream = start_gather(attention_pack, block_input, cotangent)
    all_input = all_input.reshape(rows, width)
    upstream = upstream.reshape(rows, width)
    qkv_cols = q_cols + 2 * kv_cols
    qkv_full = attention_full[:, :qkv_cols]
    output_full = attention_full[:, qkv_cols : qkv_cols + q_cols]
    gains_full = attention_full[:, qkv_cols + q_cols :].astype(f32)
    operator_scale = gains_full[:, 0]
    feedforward_scale = gains_full[:, 1]
    query_scale = gains_full[:, 2].reshape(fsdp, shard_rows)[:, :gain_rows].reshape(-1)
    key_scale = gains_full[:, 3].reshape(fsdp, shard_rows)[:, :gain_rows].reshape(-1)

    own_input = part_of(block_input, 1, quarter, me_t * quarter)
    upstream_own = part_of(cotangent, 1, quarter, me_t * quarter)

    ctx_order = lax.rem(me_c - jnp.arange(ctx) + ctx, ctx)
    tensor_order = lax.rem(me_t - jnp.arange(tensor) + tensor, tensor)
    positions = (
        tensor_order[:, None, None] * quarter
        + ctx_order[None, :, None] * tok_here
        + jnp.arange(quarter)[None, None, :]
    ).reshape(tokens)
    cosine, sine = rotary_tables(positions, head_width)

    def prepare(raw, gain):
        return head_prepare(raw, gain, cosine, sine)

    normed_input = rms_scale(all_input.astype(f32), operator_scale).astype(bf16)
    qkv_raw = jnp.dot(normed_input, qkv_full, preferred_element_type=f32).reshape(seqs, tokens, -1)
    query_f32, query_back = jax.vjp(prepare, qkv_raw[..., :q_cols], query_scale)
    key_f32, key_back = jax.vjp(prepare, qkv_raw[..., q_cols : q_cols + kv_cols], key_scale)
    slots = tensor * ctx

    def by_slot(array):
        return array.astype(bf16).reshape(slots, quarter, -1, head_width)

    queries = by_slot(query_f32).transpose(0, 2, 1, 3)
    keys = by_slot(key_f32).transpose(0, 2, 1, 3)
    values = by_slot(qkv_raw[..., q_cols + kv_cols :])
    own_f32 = own_input.astype(f32)
    feedforward_full, attended, attended_turned, totals, hidden, normed_hidden = forward_gather(
        feedforward_shard,
        queries,
        keys,
        values.transpose(0, 2, 3, 1),
        output_full,
        own_input.reshape(quarter, width),
        feedforward_scale.reshape(1, width),
    )
    attended_rows = attended.reshape(rows, q_cols)
    normed_hidden = normed_hidden.reshape(rows, width)
    gate_up_full = feedforward_full[:, : 2 * hidden_units]
    down_full = feedforward_full[:, 2 * hidden_units :]
    gate_up = jnp.dot(normed_hidden, gate_up_full, preferred_element_type=f32)
    act_f32, act_back = jax.vjp(swiglu, gate_up[:, :hidden_units], gate_up[:, hidden_units:])
    activation = act_f32.astype(bf16)
    act_grad = jnp.dot(upstream, down_full, preferred_element_type=f32)
    gate_grad, up_grad = act_back(act_grad)
    gate_up_grad = jnp.concatenate([gate_grad.astype(bf16), up_grad.astype(bf16)], axis=1)
    hidden_part = contract(gate_up_grad, gate_up_full, 1, 1).astype(bf16)
    down_part = contract(activation, down_full, 1, 1).astype(bf16)
    (
        feedforward_share,
        hidden_grad,
        all_hidden_grad,
        block_output,
        query_hgrad,
        key_hgrad,
        value_hgrad,
    ) = backward_scatter(
        hidden_part.reshape(slots, quarter, width),
        down_part.reshape(slots, quarter, width),
        normed_hidden.T,
        upstream.T,
        gate_up_grad,
        activation,
        hidden,
        upstream_own.reshape(quarter, width),
        feedforward_scale.reshape(1, width),
        output_full,
        queries,
        keys,
        keys.transpose(0, 1, 3, 2),
        values.transpose(0, 2, 1, 3),
        attended_turned,
        totals,
    )
    hidden_grad = hidden_grad[None]
    block_output = block_output.reshape(seqs, tok_here, width)
    output_weight_grad = contract(all_hidden_grad.reshape(rows, width), attended_rows, 0, 0)
    query_hgrad = query_hgrad.transpose(0, 3, 1, 2).reshape(seqs, tokens, heads, head_width)
    key_hgrad = key_hgrad.transpose(0, 2, 1, 3).reshape(seqs, tokens, heads, head_width)
    value_hgrad = value_hgrad.transpose(0, 2, 1, 3).reshape(seqs, tokens, heads, head_width)

    def head_sum(grad):
        return grad.astype(f32).reshape(seqs, tokens, kv, group, head_width).sum(axis=3)

    query_pre, query_gain_grad = query_back(query_hgrad.astype(f32))
    key_pre, key_gain_grad = key_back(head_sum(key_hgrad))
    qkv_raw_grad = jnp.concatenate(
        [
            query_pre.astype(bf16).reshape(rows, q_cols),
            key_pre.astype(bf16).reshape(rows, kv_cols),
            head_sum(value_hgrad).astype(bf16).reshape(rows, kv_cols),
        ],
        axis=1,
    )
    input_part = contract(qkv_raw_grad, qkv_full, 1, 1).reshape(tensor, ctx, quarter, width)
    qkv_weight_grad = contract(normed_input, qkv_raw_grad, 0, 0)
    gain_grads = jnp.stack([query_gain_grad, key_gain_grad], axis=1).reshape(fsdp, gain_rows, 2)
    gain_grads = jnp.pad(
        gain_grads, ((0, 0), (0, shard_rows - gain_rows), (0, 126))
    ).reshape(width, 128)
    attention_grad = jnp.concatenate(
        [qkv_weight_grad, output_weight_grad, gain_grads], axis=1
    ).astype(bf16)
    feedforward_parts = in_order(feedforward_share[None], "ctx", 0)
    attention_grad, feedforward_parts = lax.optimization_barrier(
        (attention_grad, feedforward_parts)
    )
    attention_parts, normed_input_grad = finish_sums(attention_grad, input_part)
    attention_parts = attention_parts.astype(f32)
    normed_input_grad = normed_input_grad[None]
    _, norm_one_back = jax.vjp(lambda v: rms_scale(v, operator_scale), own_f32)
    (input_norm_grad,) = norm_one_back(normed_input_grad)
    input_grad = in_order(hidden_grad + input_norm_grad, "tensor", 1)

    def columns(parts):
        return jnp.concatenate([parts[step] for step in range(ctx)], axis=1)

    def head_columns(parts):
        every = columns(parts)
        if copies == 1:
            return every
        return every.reshape(shard_rows, kv_shard, copies, head_width).sum(axis=2).reshape(
            shard_rows, -1
        )

    query_weight_grad = columns(attention_parts[:, :, :q_cols])
    key_weight_grad = head_columns(attention_parts[:, :, q_cols : q_cols + kv_cols])
    value_weight_grad = head_columns(attention_parts[:, :, q_cols + kv_cols : qkv_cols])
    gate_weight_grad = columns(feedforward_parts[:, :, :hidden_units].astype(f32))
    up_weight_grad = columns(
        feedforward_parts[:, :, hidden_units : 2 * hidden_units].astype(f32)
    )
    down_weight_grad = jnp.swapaxes(feedforward_parts[:, :, 2 * hidden_units :], 1, 2)
    down_weight_grad = down_weight_grad.astype(f32).reshape(-1, shard_rows)
    gain_parts = attention_parts[:, :, qkv_cols + q_cols : qkv_cols + q_cols + 2].sum(axis=0)

    def gain_part(pairs, gain):
        total = 0.0
        for weight, grad in pairs:
            total = total + jnp.sum(weight.astype(f32) * grad, axis=1)
        return total / gain.astype(f32)

    gain_columns = jnp.concatenate(
        [
            gain_part(
                [
                    (query_weight, query_weight_grad),
                    (key_weight, key_weight_grad),
                    (value_weight, value_weight_grad),
                ],
                operator_gain,
            )[:, None],
            gain_part(
                [(gate_weight, gate_weight_grad), (up_weight, up_weight_grad)], feedforward_gain
            )[:, None],
            gain_parts,
        ],
        axis=1,
    )
    gain_totals = gain_columns
    for step in range(1, tensor):
        gain_totals = gain_totals + shift(gain_columns, "tensor", step)

    return (
        block_output,
        input_grad,
        gain_totals[:, 0],
        query_weight_grad,
        key_weight_grad,
        value_weight_grad,
        jnp.swapaxes(attention_parts[:, :, qkv_cols : qkv_cols + q_cols], 1, 2).reshape(
            -1, shard_rows
        ),
        gain_totals[:, 1],
        gate_weight_grad,
        up_weight_grad,
        down_weight_grad,
        gain_totals[:gain_rows, 2],
        gain_totals[:gain_rows, 3],
    )


def solution(mesh):
    in_specs = (
        P("fsdp", "ctx", None),
        P("fsdp"),
        P("fsdp", "tensor"),
        P("fsdp", "tensor"),
        P("fsdp", "tensor"),
        P("tensor", "fsdp"),
        P("fsdp"),
        P("fsdp", "tensor"),
        P("fsdp", "tensor"),
        P("tensor", "fsdp"),
        P("fsdp"),
        P("fsdp"),
        P("fsdp", "ctx", None),
    )
    out_specs = (
        P("fsdp", "ctx", None),
        P("fsdp", "ctx", None),
        P("fsdp"),
        P("fsdp", "tensor"),
        P("fsdp", "tensor"),
        P("fsdp", "tensor"),
        P("tensor", "fsdp"),
        P("fsdp"),
        P("fsdp", "tensor"),
        P("fsdp", "tensor"),
        P("tensor", "fsdp"),
        P("fsdp"),
        P("fsdp"),
    )
    return jax.shard_map(shards, mesh=mesh, in_specs=in_specs, out_specs=out_specs, check_vma=False)
```

```python
import jax
import jax.numpy as jnp
from jax import lax
from jax.experimental import pallas as pl
from jax.experimental.pallas import tpu as pltpu
from jax.sharding import PartitionSpec as P

EPS = 1e-05
THETA = 1000000.0


def rms_scale(values_in, gain):
    return (
        values_in * lax.rsqrt(jnp.mean(values_in * values_in, axis=-1, keepdims=True) + EPS) * gain
    )


def rotary_tables(positions, head_width):
    half_width = head_width // 2
    freqs = THETA ** (-jnp.arange(half_width).astype(jnp.float32) * 2.0 / head_width)
    angles = positions.astype(jnp.float32)[:, None] * freqs[None, :]
    return (jnp.cos(angles), jnp.sin(angles))


def rotate_halves(heads_in, cosine, sine):
    half_width = heads_in.shape[-1] // 2
    front_half = heads_in[..., :half_width]
    back_half = heads_in[..., half_width:]
    cos_rows = cosine[:, None, :]
    sin_rows = sine[:, None, :]
    return jnp.concatenate(
        [
            front_half * cos_rows - back_half * sin_rows,
            back_half * cos_rows + front_half * sin_rows,
        ],
        axis=-1,
    )


def head_prepare(raw, gain, cosine, sine):
    head_width = gain.shape[0]
    shaped = raw.reshape(raw.shape[:-1] + (raw.shape[-1] // head_width, head_width))
    return rotate_halves(rms_scale(shaped, gain), cosine, sine)


def swiglu(gate, upper):
    return jax.nn.silu(gate) * upper


def contract(left, right, left_dim, right_dim):
    return lax.dot_general(
        left, right, (((left_dim,), (right_dim,)), ((), ())), preferred_element_type=jnp.float32
    )


def block_scores(query_block, keys, query_pos, key_pos):
    scale = 1.0 / query_block.shape[-1] ** 0.5
    scores = (
        jnp.einsum("qhd,khd->hqk", query_block, keys, preferred_element_type=jnp.float32) * scale
    )
    allowed = key_pos[None, :] <= query_pos[:, None]
    return jnp.where(allowed[None, :, :], scores, -1e30)


def attend(queries, keys, values, positions):
    length = queries.shape[0]
    block_rows = min(512, length)
    outputs = []
    totals = []
    for start in range(0, length, block_rows):
        rows = slice(start, start + block_rows)
        scores = block_scores(queries[rows], keys, positions[rows], positions)
        peak = jnp.max(scores, axis=-1, keepdims=True)
        log_total = peak + jnp.log(jnp.sum(jnp.exp(scores - peak), axis=-1, keepdims=True))
        probs = jnp.exp(scores - log_total).astype(jnp.bfloat16)
        block_out = jnp.einsum("hqk,khd->qhd", probs, values, preferred_element_type=jnp.float32)
        outputs.append(block_out.astype(jnp.bfloat16))
        totals.append(log_total[..., 0])
    return (jnp.concatenate(outputs, axis=0), jnp.concatenate(totals, axis=1))


def attend_grad(queries, keys, values, outputs, totals, out_grad, positions):
    length = queries.shape[0]
    block_rows = min(512, length)
    scale = 1.0 / queries.shape[-1] ** 0.5
    key_acc = jnp.zeros(keys.shape, jnp.float32)
    value_acc = jnp.zeros(values.shape, jnp.float32)
    query_parts = []
    for start in range(0, length, block_rows):
        rows = slice(start, start + block_rows)
        query_block = queries[rows]
        scores = block_scores(query_block, keys, positions[rows], positions)
        probs = jnp.exp(scores - totals[:, rows][..., None])
        grad_block = out_grad[rows]
        value_acc = value_acc + jnp.einsum(
            "hqk,qhd->khd",
            probs.astype(jnp.bfloat16),
            grad_block,
            preferred_element_type=jnp.float32,
        )
        prob_grad = jnp.einsum(
            "qhd,khd->hqk", grad_block, values, preferred_element_type=jnp.float32
        )
        delta = jnp.sum(
            grad_block.astype(jnp.float32) * outputs[rows].astype(jnp.float32),
            axis=-1,
        ).T
        score_grad = (probs * (prob_grad - delta[..., None])).astype(jnp.bfloat16)
        query_parts.append(
            (
                jnp.einsum("hqk,khd->qhd", score_grad, keys, preferred_element_type=jnp.float32)
                * scale
            ).astype(jnp.bfloat16)
        )
        key_acc = (
            key_acc
            + jnp.einsum(
                "hqk,qhd->khd", score_grad, query_block, preferred_element_type=jnp.float32
            )
            * scale
        )
    return (
        jnp.concatenate(query_parts, axis=0),
        key_acc.astype(jnp.bfloat16),
        value_acc.astype(jnp.bfloat16),
    )


def shift(array, axis_name, step):
    size = lax.axis_size(axis_name)
    return lax.ppermute(array, axis_name, [(i, (i + step) % size) for i in range(size)])


def around(array, axis_name, dim):
    size = lax.axis_size(axis_name)
    return jnp.concatenate(
        [array] + [shift(array, axis_name, step) for step in range(1, size)], axis=dim
    )


def group_rows(array):
    return around(around(array, "ctx", 1), "tensor", 1)


def sum_around(array, axis_name):
    size = lax.axis_size(axis_name)
    part = array.shape[1] // size
    total = array[:, :part].astype(jnp.float32)
    for step in range(1, size):
        piece = array[:, step * part : (step + 1) * part].astype(jnp.bfloat16)
        total = total + shift(piece, axis_name, -step).astype(jnp.float32)
    return total


def group_sum(array):
    return sum_around(sum_around(array, "tensor"), "ctx")


def in_order(array, axis_name, dim):
    size = lax.axis_size(axis_name)
    me = lax.axis_index(axis_name)
    width = array.shape[dim]
    shape = list(array.shape)
    shape[dim] = width * size
    out = jnp.zeros(shape, array.dtype)
    for step in range(size):
        piece = array if step == 0 else shift(array, axis_name, step)
        owner = lax.rem(me - step + size, size)
        out = lax.dynamic_update_slice_in_dim(out, piece, owner * width, dim)
    return out


def ring_index(place, size):
    if size % 2:
        return place
    turn = size // 2
    return jnp.where(place < turn, 2 * place, 2 * (size - 1 - place) + 1)


def ring_place(index, size):
    if size % 2:
        return index
    return jnp.where(lax.rem(index, 2) == 0, lax.div(index, 2), size - 1 - lax.div(index, 2))


def ring_order(size):
    if size % 2:
        return list(range(size))
    return [2 * i for i in range(size // 2)] + [2 * i + 1 for i in reversed(range(size // 2))]


def ring_shift(array, axis_name, step):
    size = lax.axis_size(axis_name)
    order = ring_order(size)
    pairs = [(order[i], order[(i + step) % size]) for i in range(size)]
    return lax.ppermute(array, axis_name, pairs)


def ring_gather(shard, axis_name, dim=0):
    size = lax.axis_size(axis_name)
    place = ring_place(lax.axis_index(axis_name), size)
    shape = list(shard.shape)
    shape[dim] *= size
    half = shard.shape[0] // 2
    out = jnp.zeros(shape, shard.dtype)

    def put(out, piece, at, offset):
        owner = ring_index(lax.rem(at + size, size), size)
        starts = [offset, 0]
        starts[dim] += owner * shard.shape[dim]
        return lax.dynamic_update_slice(out, piece, starts)

    out = put(out, shard, place, 0)
    rightward = leftward = shard
    for step in range(1, (size + 1) // 2):
        rightward = ring_shift(rightward, axis_name, 1)
        leftward = ring_shift(leftward, axis_name, -1)
        out = put(out, rightward, place - step, 0)
        out = put(out, leftward, place + step, 0)
    if size % 2 == 0:
        rightward = ring_shift(rightward[:half], axis_name, 1)
        leftward = ring_shift(leftward[half:], axis_name, -1)
        out = put(out, rightward, place + size // 2, 0)
        out = put(out, leftward, place + size // 2, half)
    return out, rightward


def ring_scatter(piece_for, axis_name):
    size = lax.axis_size(axis_name)
    place = ring_place(lax.axis_index(axis_name), size)

    def piece(offset):
        return piece_for(ring_index(lax.rem(place + offset + size, size), size))

    mine = piece(0).astype(jnp.float32)
    if size == 1:
        return mine
    half = mine.shape[0] // 2
    far = size // 2
    bf16 = jnp.bfloat16
    f32 = jnp.float32
    if size % 2 == 0:
        across = piece(far)
        rightward = ring_shift(across[:half].astype(bf16), axis_name, 1).astype(f32)
        leftward = ring_shift(across[half:].astype(bf16), axis_name, -1).astype(f32)
        zero = jnp.zeros_like(mine[:half])
        rightward = jnp.concatenate([rightward, zero], axis=0)
        leftward = jnp.concatenate([zero, leftward], axis=0)
        steps = far - 1
    else:
        rightward = leftward = jnp.zeros_like(mine)
        steps = far
    for step in range(steps, 0, -1):
        rightward = ring_shift((rightward + piece(step)).astype(bf16), axis_name, 1).astype(f32)
        leftward = ring_shift((leftward + piece(-step)).astype(bf16), axis_name, -1).astype(f32)
    return mine + rightward + leftward


def other(axis_name, step):
    size = lax.axis_size(axis_name)
    return {axis_name: lax.rem(lax.axis_index(axis_name) + step + size, size)}


def send(source, target, send_sem, recv_sem, device):
    copy = pltpu.make_async_remote_copy(
        src_ref=source,
        dst_ref=target,
        send_sem=send_sem,
        recv_sem=recv_sem,
        device_id=device,
        device_id_type=pl.DeviceIdType.MESH,
    )
    copy.start()
    return copy


def ring_ends():
    size = lax.axis_size("fsdp")
    place = ring_place(lax.axis_index("fsdp"), size)

    def at(offset):
        return ring_index(lax.rem(place + offset + size, size), size)

    return at, ({"fsdp": at(1)}, {"fsdp": at(-1)})


def greet():
    _, ends = ring_ends()
    partners = list(ends)
    for axis_name in ("ctx", "tensor"):
        partners += [other(axis_name, step) for step in range(1, lax.axis_size(axis_name))]
    barrier = pltpu.get_barrier_semaphore()
    for device in partners:
        pl.semaphore_signal(
            barrier, inc=1, device_id=device, device_id_type=pl.DeviceIdType.MESH
        )
    pl.semaphore_wait(barrier, len(partners))


def start_kernel(
    pack_ref,
    input_ref,
    upstream_ref,
    full_ref,
    all_input_ref,
    all_upstream_ref,
    ring_send,
    ring_recv,
    ctx_send,
    ctx_recv,
    tensor_send,
    tensor_recv,
    local_sem,
):
    size = lax.axis_size("fsdp")
    ctx = lax.axis_size("ctx")
    tensor = lax.axis_size("tensor")
    me_t = lax.axis_index("tensor")
    far = size // 2
    rows = pack_ref.shape[0]
    sub_rows = rows // 2
    quarter = all_input_ref.shape[2]
    at, ends = ring_ends()
    greet()
    pairs = ((input_ref, all_input_ref), (upstream_ref, all_upstream_ref))

    def block(owner, sub):
        start = pl.multiple_of(owner * rows + sub * sub_rows, sub_rows)
        return full_ref.at[pl.ds(start, sub_rows)]

    sends = []
    arrivals = {}

    def ring_step(step):
        for sub in range(2):
            for way in range(2):
                if step == far and sub != way:
                    continue
                if step > 1:
                    arrivals.pop((way, step - 1, sub)).wait_recv()
                owner = at((1 - step) if way == 0 else (step - 1))
                source = (
                    pack_ref.at[pl.ds(sub * sub_rows, sub_rows)] if step == 1 else block(owner, sub)
                )
                copy = send(
                    source,
                    block(owner, sub),
                    ring_send.at[way, step - 1, sub],
                    ring_recv.at[way, step - 1, sub],
                    ends[way],
                )
                sends.append(copy)
                arrivals[way, step, sub] = copy

    def own_rows(source, step):
        quarter_at = lax.rem(me_t - step + tensor, tensor)
        return source.at[0, pl.ds(pl.multiple_of(quarter_at * quarter, quarter), quarter)]

    ring_step(1)
    crossed = {}
    locals_ = []
    for which, (source, target) in enumerate(pairs):
        for step in range(1, ctx):
            copy = send(
                own_rows(source, 0),
                target.at[0, step],
                ctx_send.at[which, step - 1],
                ctx_recv.at[which, step - 1],
                other("ctx", step),
            )
            sends.append(copy)
            crossed[which, step] = copy
    for which, (source, target) in enumerate(pairs):
        for step in range(tensor):
            copy = pltpu.make_async_copy(
                own_rows(source, step), target.at[step, 0], local_sem.at[which, step]
            )
            copy.start()
            locals_.append(copy)
    own_copy = pltpu.make_async_copy(
        pack_ref,
        full_ref.at[pl.ds(pl.multiple_of(at(0) * rows, rows), rows)],
        local_sem.at[2, 0],
    )
    own_copy.start()
    locals_.append(own_copy)
    handed = []

    def hand_over(which):
        _, target = pairs[which]
        for step in range(1, ctx):
            crossed[which, step].wait_recv()
            for core in range(1, tensor):
                copy = send(
                    target.at[0, step],
                    target.at[core, step],
                    tensor_send.at[which, core - 1, step - 1],
                    tensor_recv.at[which, core - 1, step - 1],
                    other("tensor", core),
                )
                sends.append(copy)
                handed.append(copy)

    for step in range(2, far + 1):
        if step == far:
            hand_over(0)
        ring_step(step)
    if far < 2:
        hand_over(0)
    hand_over(1)
    for copy in arrivals.values():
        copy.wait_recv()
    for copy in handed:
        copy.wait_recv()
    for copy in sends:
        copy.wait_send()
    for copy in locals_:
        copy.wait()


def start_gather(pack, block_input, cotangent):
    size = lax.axis_size("fsdp")
    ctx = lax.axis_size("ctx")
    tensor = lax.axis_size("tensor")
    far = size // 2
    rows, columns = pack.shape
    _, tok_here, width = block_input.shape
    every = (tensor, ctx, tok_here // tensor, width)
    in_vmem = pl.BlockSpec(memory_space=pltpu.VMEM)
    dma = pltpu.SemaphoreType.DMA
    return pl.pallas_call(
        start_kernel,
        out_shape=(
            jax.ShapeDtypeStruct((rows * size, columns), pack.dtype),
            jax.ShapeDtypeStruct(every, block_input.dtype),
            jax.ShapeDtypeStruct(every, cotangent.dtype),
        ),
        in_specs=[in_vmem] * 3,
        out_specs=(in_vmem,) * 3,
        scratch_shapes=[
            dma((2, far, 2)),
            dma((2, far, 2)),
            dma((2, ctx)),
            dma((2, ctx)),
            dma((2, tensor, ctx)),
            dma((2, tensor, ctx)),
            dma((3, tensor)),
        ],
        compiler_params=pltpu.CompilerParams(
            collective_id=0, has_side_effects=True, vmem_limit_bytes=32 * 1024 * 1024
        ),
        name="start_gather",
    )(pack, block_input, cotangent)


def add_rows(count, block_rows, body):
    def step(index, carry):
        body(pl.ds(pl.multiple_of(index * block_rows, block_rows), block_rows))
        return carry

    lax.fori_loop(0, count // block_rows, step, 0)


def finish_kernel(
    grad_ref,
    part_ref,
    parts_ref,
    total_ref,
    going,
    coming,
    share,
    core_going,
    core_coming,
    ctx_going,
    ctx_coming,
    ring_send,
    ring_recv,
    core_send,
    core_recv,
    ctx_send,
    ctx_recv,
    share_send,
    share_recv,
    local_sem,
):
    f32 = jnp.float32
    bf16 = jnp.bfloat16
    size = lax.axis_size("fsdp")
    ctx = lax.axis_size("ctx")
    tensor = lax.axis_size("tensor")
    me_c = lax.axis_index("ctx")
    far = size // 2
    rows = share.shape[0]
    sub_rows = rows // 2
    quarter = part_ref.shape[2]
    at, ends = ring_ends()
    greet()
    sends = []
    arrivals = {}

    def own_block(owner, sub):
        return pl.ds(pl.multiple_of(owner * rows + sub * sub_rows, sub_rows), sub_rows)

    def ring_step(step):
        for sub in range(2):
            for way in range(2):
                if step == 1 and sub != way:
                    continue
                ahead = far + 1 - step
                owner = at(ahead if way == 0 else -ahead)
                mine = own_block(owner, sub)
                if step == 1:
                    source = grad_ref.at[mine]
                else:
                    source = going.at[way, step - 2, sub]
                    if (way, step - 1, sub) in arrivals:
                        arrivals.pop((way, step - 1, sub)).wait_recv()
                        source[...] = (
                            grad_ref[mine, :].astype(f32)
                            + coming[way, step - 2, sub].astype(f32)
                        ).astype(bf16)
                    else:
                        source = grad_ref.at[mine]
                copy = send(
                    source,
                    coming.at[way, step - 1, sub],
                    ring_send.at[way, step - 1, sub],
                    ring_recv.at[way, step - 1, sub],
                    ends[way],
                )
                sends.append(copy)
                arrivals[way, step, sub] = copy

    ring_step(1)
    by_core = []
    for core in range(1, tensor):
        for step in range(ctx):

            def narrow(block, core=core, step=step):
                core_going[core - 1, step, block] = part_ref[core, step, block].astype(bf16)

            add_rows(quarter, 32, narrow)
        copy = send(
            core_going.at[core - 1],
            core_coming.at[core - 1],
            core_send.at[core - 1],
            core_recv.at[core - 1],
            other("tensor", -core),
        )
        sends.append(copy)
        by_core.append(copy)
    if far > 1:
        ring_step(2)
    for copy in by_core:
        copy.wait_recv()
    by_ctx = []
    for step in list(range(1, ctx)) + [0]:

        def total(block, step=step):
            value = part_ref[0, step, block]
            for core in range(1, tensor):
                value = value + core_coming[core - 1, step, block].astype(f32)
            if step == 0:
                total_ref[block] = value
            else:
                ctx_going[step - 1, block] = value.astype(bf16)

        add_rows(quarter, 32, total)
        if step > 0:
            copy = send(
                ctx_going.at[step - 1],
                ctx_coming.at[step - 1],
                ctx_send.at[step - 1],
                ctx_recv.at[step - 1],
                other("ctx", -step),
            )
            sends.append(copy)
            by_ctx.append(copy)
    for step in range(3, far + 1):
        ring_step(step)
    mine = at(0)
    for sub in range(2):
        value = grad_ref[own_block(mine, sub), :].astype(f32)
        for way in range(2):
            if (way, far, sub) in arrivals:
                arrivals.pop((way, far, sub)).wait_recv()
                value = value + coming[way, far - 1, sub].astype(f32)
        share[sub * sub_rows : (sub + 1) * sub_rows, :] = value.astype(bf16)
    shared = []
    for step in range(1, ctx):
        copy = send(
            share,
            parts_ref.at[me_c],
            share_send.at[step - 1],
            share_recv.at[step - 1],
            other("ctx", step),
        )
        sends.append(copy)
        shared.append(copy)
    keep = pltpu.make_async_copy(share, parts_ref.at[me_c], local_sem)
    keep.start()
    for step in range(1, ctx):
        by_ctx[step - 1].wait_recv()

        def gather(block, step=step):
            total_ref[block] += ctx_coming[step - 1, block].astype(f32)

        add_rows(quarter, 32, gather)
    for step in range(1, ctx):
        shared[step - 1].wait_recv()
    for copy in sends:
        copy.wait_send()
    keep.wait()


def finish_sums(grad, part):
    size = lax.axis_size("fsdp")
    tensor, ctx, quarter, width = part.shape
    far = size // 2
    rows, columns = grad.shape[0] // size, grad.shape[1]
    in_vmem = pl.BlockSpec(memory_space=pltpu.VMEM)
    anywhere = pl.BlockSpec(memory_space=pl.ANY)
    dma = pltpu.SemaphoreType.DMA
    bf16 = jnp.bfloat16
    return pl.pallas_call(
        finish_kernel,
        out_shape=(
            jax.ShapeDtypeStruct((ctx, rows, columns), bf16),
            jax.ShapeDtypeStruct((quarter, width), jnp.float32),
        ),
        in_specs=[in_vmem] * 2,
        out_specs=(anywhere, in_vmem),
        scratch_shapes=[
            pltpu.VMEM((2, max(1, far - 1), 2, rows // 2, columns), bf16),
            pltpu.VMEM((2, far, 2, rows // 2, columns), bf16),
            pltpu.VMEM((rows, columns), bf16),
            pltpu.VMEM((max(1, tensor - 1), ctx, quarter, width), bf16),
            pltpu.VMEM((max(1, tensor - 1), ctx, quarter, width), bf16),
            pltpu.VMEM((max(1, ctx - 1), quarter, width), bf16),
            pltpu.VMEM((max(1, ctx - 1), quarter, width), bf16),
            dma((2, far, 2)),
            dma((2, far, 2)),
            dma((tensor,)),
            dma((tensor,)),
            dma((ctx,)),
            dma((ctx,)),
            dma((ctx,)),
            dma((ctx,)),
            dma(()),
        ],
        compiler_params=pltpu.CompilerParams(
            collective_id=1, has_side_effects=True, vmem_limit_bytes=48 * 1024 * 1024
        ),
        name="finish_sums",
    )(grad, part)


def gather_ring(shard_ref, full_ref, send_sem, recv_sem):
    size = lax.axis_size("fsdp")
    far = size // 2
    rows = shard_ref.shape[0]
    sub_rows = rows // 2
    at, ends = ring_ends()
    sends = []
    arrivals = {}
    queue = [(step, sub) for step in range(1, far + 1) for sub in range(2)]

    def block(owner, sub):
        start = pl.multiple_of(owner * rows + sub * sub_rows, sub_rows)
        return full_ref.at[pl.ds(start, sub_rows)]

    def go(count):
        for _ in range(min(count, len(queue))):
            step, sub = queue.pop(0)
            for way in range(2):
                if (way, step - 1, sub) in arrivals and (step < far or sub == way):
                    arrivals.pop((way, step - 1, sub)).wait_recv()
                if step == far and sub != way:
                    continue
                owner = at((1 - step) if way == 0 else (step - 1))
                source = (
                    shard_ref.at[pl.ds(sub * sub_rows, sub_rows)] if step == 1 else block(owner, sub)
                )
                copy = send(
                    source,
                    block(owner, sub),
                    send_sem.at[way, step - 1, sub],
                    recv_sem.at[way, step - 1, sub],
                    ends[way],
                )
                sends.append(copy)
                arrivals[way, step, sub] = copy

    def land(step):
        while len(queue) > 0 and queue[0][0] <= step:
            go(1)
        for key in [key for key in arrivals if key[1] <= step]:
            arrivals.pop(key).wait_recv()

    def finish():
        go(len(queue))
        land(far)
        for copy in sends:
            copy.wait_send()

    return go, land, finish


def scatter_ring(grad_ref, coming, send_sem, recv_sem):
    f32 = jnp.float32
    size = lax.axis_size("fsdp")
    far = size // 2
    rows = grad_ref.shape[0] // size
    sub_rows = rows // 2
    step_rows = 16
    at, ends = ring_ends()
    sends = []
    arrivals = {}
    queue = [(1, 0, 0), (1, 1, 1)]
    for step in range(2, far + 1):
        queue += [(step, 1, 0), (step, 0, 1), (step, 0, 0), (step, 1, 1)]

    def start_of(owner, sub):
        return pl.multiple_of(owner * rows + sub * sub_rows, sub_rows)

    def go(count):
        for _ in range(min(count, len(queue))):
            step, way, sub = queue.pop(0)
            ahead = far + 1 - step
            first = start_of(at(ahead if way == 0 else -ahead), sub)
            if (way, step - 1, sub) in arrivals:
                arrivals.pop((way, step - 1, sub)).wait_recv()

                def add(index, carry, way=way, step=step, sub=sub, first=first):
                    here = pl.ds(pl.multiple_of(index * step_rows, step_rows), step_rows)
                    there = pl.ds(
                        pl.multiple_of(first + index * step_rows, step_rows), step_rows
                    )
                    grad_ref[there] = (
                        grad_ref[there].astype(f32) + coming[way, step - 2, sub, here].astype(f32)
                    ).astype(grad_ref.dtype)
                    return carry

                lax.fori_loop(0, sub_rows // step_rows, add, 0)
            copy = send(
                grad_ref.at[pl.ds(first, sub_rows)],
                coming.at[way, step - 1, sub],
                send_sem.at[way, step - 1, sub],
                recv_sem.at[way, step - 1, sub],
                ends[way],
            )
            sends.append(copy)
            arrivals[way, step, sub] = copy

    def finish(share_ref):
        go(len(queue))
        for sub in range(2):
            landed = []
            for way in range(2):
                if (way, far, sub) in arrivals:
                    arrivals.pop((way, far, sub)).wait_recv()
                    landed.append(way)

            def add(index, carry, sub=sub, landed=landed):
                here = pl.ds(pl.multiple_of(index * step_rows, step_rows), step_rows)
                there = pl.ds(
                    pl.multiple_of(start_of(at(0), sub) + index * step_rows, step_rows), step_rows
                )
                out = pl.ds(
                    pl.multiple_of(sub * sub_rows + index * step_rows, step_rows), step_rows
                )
                value = grad_ref[there].astype(f32)
                for way in landed:
                    value = value + coming[way, far - 1, sub, here].astype(f32)
                share_ref[out] = value.astype(share_ref.dtype)
                return carry

            lax.fori_loop(0, sub_rows // step_rows, add, 0)
        for copy in sends:
            copy.wait_send()

    return go, finish


def slot_base(slot, quarter):
    ctx = lax.axis_size("ctx")
    tensor = lax.axis_size("tensor")
    of_core = lax.rem(lax.axis_index("tensor") - lax.div(slot, ctx) + tensor, tensor)
    of_ctx = lax.rem(lax.axis_index("ctx") - lax.rem(slot, ctx) + ctx, ctx)
    return of_core * quarter + of_ctx * (quarter * tensor)


def reachable(query_slot, key_slot, quarter):
    gap = slot_base(query_slot, quarter) - slot_base(key_slot, quarter)
    return gap, gap > -quarter


def masked_scores(keys, queries, gap):
    scores = lax.dot_general(
        keys, queries, (((1,), (1,)), ((), ())), preferred_element_type=jnp.float32
    ) * (1.0 / queries.shape[-1] ** 0.5)
    key_at = lax.broadcasted_iota(jnp.int32, scores.shape, 0)
    query_at = lax.broadcasted_iota(jnp.int32, scores.shape, 1)
    return jnp.where(key_at - query_at <= gap, scores, -1e30)


def attend_slot(slot, q_ref, k_ref, vt_ref, attended_ref, turned_ref, total_ref, work):
    scores_ref, peak_ref, sum_ref, out_ref = work
    slots, heads, quarter, head_width = q_ref.shape
    group = heads // k_ref.shape[1]

    def one_head(head, carry):
        kv_head = lax.div(head, group)
        peak_ref[...] = jnp.full(peak_ref.shape, -1e30, jnp.float32)
        sum_ref[...] = jnp.zeros(sum_ref.shape, jnp.float32)
        out_ref[...] = jnp.zeros(out_ref.shape, jnp.float32)

        def score(key_slot, carry):
            gap, seen = reachable(slot, key_slot, quarter)

            @pl.when(seen)
            def _():
                scores = masked_scores(k_ref[key_slot, kv_head], q_ref[slot, head], gap)
                scores_ref[key_slot] = scores
                peak_ref[...] = jnp.maximum(peak_ref[...], jnp.max(scores, axis=0, keepdims=True))

            return carry

        lax.fori_loop(0, slots, score, 0)

        def weigh(key_slot, carry):
            _, seen = reachable(slot, key_slot, quarter)

            @pl.when(seen)
            def _():
                raised = jnp.exp(scores_ref[key_slot] - peak_ref[...])
                sum_ref[...] += jnp.sum(raised, axis=0, keepdims=True)
                out_ref[...] += jnp.dot(
                    vt_ref[key_slot, kv_head],
                    raised.astype(jnp.bfloat16),
                    preferred_element_type=jnp.float32,
                )

            return carry

        lax.fori_loop(0, slots, weigh, 0)
        total_ref[slot, head] = peak_ref[...] + jnp.log(sum_ref[...])
        rows = pl.ds(pl.multiple_of(head * head_width, head_width), head_width)
        turned_ref[slot, rows] = (out_ref[...] / sum_ref[...]).astype(jnp.bfloat16)
        return carry

    lax.fori_loop(0, heads, one_head, 0)
    attended_ref[slot] = turned_ref[slot].astype(jnp.float32).T.astype(jnp.bfloat16)


def rotated(raw, gain, cosine, sine):
    half = raw.shape[-1] // 2
    scale = lax.rsqrt(jnp.mean(raw * raw, axis=-1, keepdims=True) + EPS)
    scaled = raw * scale * gain
    front, back = scaled[:, :half], scaled[:, half:]
    return jnp.concatenate(
        [front * cosine - back * sine, back * cosine + front * sine], axis=1
    )


def forward_kernel(
    shard_ref,
    input_ref,
    upstream_ref,
    qkv_ref,
    weight_ref,
    operator_gain_ref,
    gain_ref,
    query_gain_ref,
    key_gain_ref,
    cosine_ref,
    sine_ref,
    full_ref,
    attended_ref,
    turned_ref,
    total_ref,
    hidden_ref,
    normed_blocks,
    upstream_blocks,
    normed_input_ref,
    raw_ref,
    q_ref,
    k_ref,
    kt_ref,
    v_ref,
    gate_up_grad_ref,
    activation_ref,
    vt_ref,
    normed_ref,
    total_acc,
    scores_ref,
    peak_ref,
    sum_ref,
    out_ref,
    part_ref,
    core_going,
    core_coming,
    ctx_going,
    ctx_coming,
    ring_send,
    ring_recv,
    core_send,
    core_recv,
    ctx_send,
    ctx_recv,
    spread_send,
    spread_recv,
    local_sem,
):
    f32 = jnp.float32
    bf16 = jnp.bfloat16
    size = lax.axis_size("fsdp")
    ctx = lax.axis_size("ctx")
    tensor = lax.axis_size("tensor")
    far = size // 2
    slots, heads, quarter, head_width = q_ref.shape
    kv = k_ref.shape[1]
    rows = shard_ref.shape[0]
    tokens = slots * quarter
    hidden_units = activation_ref.shape[1]
    at, _ = ring_ends()
    greet()
    go, land, finish = gather_ring(shard_ref, full_ref, ring_send, ring_recv)
    go(2)
    keep = pltpu.make_async_copy(
        shard_ref,
        full_ref.at[pl.ds(pl.multiple_of(at(0) * rows, rows), rows)],
        local_sem,
    )
    keep.start()
    work = (scores_ref, peak_ref, sum_ref, out_ref)

    def prepare(slot, carry):
        def norm(block):
            value = input_ref[slot, block].astype(f32)
            scale = lax.rsqrt(jnp.mean(value * value, axis=-1, keepdims=True) + EPS)
            normed_input_ref[slot, block] = (value * scale * operator_gain_ref[...]).astype(bf16)

        add_rows(quarter, 32, norm)
        raw_ref[slot] = jnp.dot(
            normed_input_ref[slot], qkv_ref[...], preferred_element_type=f32
        )
        cosine = cosine_ref[slot]
        sine = sine_ref[slot]
        for head in range(heads):
            raw = raw_ref[slot, :, head * head_width : (head + 1) * head_width]
            q_ref[slot, head] = rotated(raw, query_gain_ref[...], cosine, sine).astype(bf16)
        for head in range(kv):
            start = (heads + head) * head_width
            raw = raw_ref[slot, :, start : start + head_width]
            turned = rotated(raw, key_gain_ref[...], cosine, sine)
            k_ref[slot, head] = turned.astype(bf16)
            kt_ref[slot, head] = turned.T.astype(bf16)
            start = (heads + kv + head) * head_width
            raw = raw_ref[slot, :, start : start + head_width]
            v_ref[slot, head] = raw.astype(bf16)
            vt_ref[slot, head] = raw.T.astype(bf16)
        here = pl.ds(pl.multiple_of(slot * quarter, quarter), quarter)
        for owner in range(size):
            upstream_blocks[owner, here] = upstream_ref[
                slot, :, owner * rows : (owner + 1) * rows
            ]
        return carry

    lax.fori_loop(0, slots, prepare, 0)
    go(1)

    def accumulate(offset, lhs, start, stop, first=False):
        owner = at(offset)
        there = pl.ds(pl.multiple_of(owner * rows, rows), rows)
        for column in range(start, stop):
            columns = slice(column * hidden_units, (column + 1) * hidden_units)

            def add(here, columns=columns):
                value = jnp.dot(
                    lhs[owner, here], full_ref[there, columns], preferred_element_type=f32
                )
                if first:
                    total_acc[here, columns] = value
                else:
                    total_acc[here, columns] += value

            add_rows(tokens, quarter, add)

    def project(slot):
        attend_slot(slot, q_ref, k_ref, vt_ref, attended_ref, turned_ref, total_ref, work)
        return lax.dot_general(
            attended_ref[slot],
            weight_ref[...],
            (((1,), (1,)), ((), ())),
            preferred_element_type=f32,
        )

    sends = []
    by_core = {}
    by_ctx = {}
    for core in range(1, tensor):
        for step in list(range(1, ctx)) + [0]:
            core_going[core - 1, step] = project(core * ctx + step).astype(bf16)
            copy = send(
                core_going.at[core - 1, step],
                core_coming.at[core - 1, step],
                core_send.at[core - 1, step],
                core_recv.at[core - 1, step],
                other("tensor", -core),
            )
            sends.append(copy)
            by_core[core, step] = copy
    for step in list(range(1, ctx)) + [0]:
        part_ref[...] = project(step)
        for core in range(1, tensor):
            by_core[core, step].wait_recv()
            part_ref[...] += core_coming[core - 1, step].astype(f32)
        if step > 0:
            ctx_going[step - 1] = part_ref[...].astype(bf16)
            copy = send(
                ctx_going.at[step - 1],
                ctx_coming.at[step - 1],
                ctx_send.at[step - 1],
                ctx_recv.at[step - 1],
                other("ctx", -step),
            )
            sends.append(copy)
            by_ctx[step] = copy
        if step < 2:
            go(1)
    keep.wait()
    accumulate(0, upstream_blocks, 2, 3, True)
    for step in range(1, ctx):
        by_ctx[step].wait_recv()
        part_ref[...] += ctx_coming[step - 1].astype(f32)

    def norm(block):
        hidden = input_ref[0, block].astype(f32) + part_ref[block]
        hidden_ref[block] = hidden
        scale = lax.rsqrt(jnp.mean(hidden * hidden, axis=-1, keepdims=True) + EPS)
        normed_ref[0, 0, block] = (hidden * scale * gain_ref[...]).astype(bf16)

    add_rows(quarter, 16, norm)
    spread = []
    for step in range(1, ctx):
        copy = send(
            normed_ref.at[0, 0],
            normed_ref.at[0, step],
            spread_send.at[0, step],
            spread_recv.at[0, step],
            other("ctx", step),
        )
        sends.append(copy)
        spread.append(copy)
    handed = []

    def hand_over(step):
        for core in range(1, tensor):
            copy = send(
                normed_ref.at[0, step],
                normed_ref.at[core, step],
                spread_send.at[core, step],
                spread_recv.at[core, step],
                other("tensor", core),
            )
            sends.append(copy)
            handed.append(copy)

    hand_over(0)
    go(1)

    def keep_blocks(slot):
        here = slice(slot * quarter, (slot + 1) * quarter)
        for owner in range(size):
            normed_blocks[owner, here] = normed_ref[
                slot // ctx, slot % ctx, :, owner * rows : (owner + 1) * rows
            ]

    near = max(0, far - 2)
    if far > 3:
        land(near)
        for offset in range(1, near + 1):
            accumulate(offset, upstream_blocks, 2, 3)
            accumulate(-offset, upstream_blocks, 2, 3)
    keep_blocks(0)
    go(1)
    for step in range(1, ctx):
        spread[step - 1].wait_recv()
        hand_over(step)
        keep_blocks(step)
    for core in range(1, tensor):
        for step in range(ctx):
            handed[(core - 1) + step * (tensor - 1)].wait_recv()
            keep_blocks(core * ctx + step)
    accumulate(0, normed_blocks, 0, 2, True)
    if far > 3:
        accumulate(1, normed_blocks, 0, 2)
        accumulate(-1, normed_blocks, 0, 2)
        go(2)
        for offset in range(2, near + 1):
            accumulate(offset, normed_blocks, 0, 2)
            accumulate(-offset, normed_blocks, 0, 2)
    else:
        near = 0
    go(2 * far)
    for offset in range(near + 1, far):
        land(offset)
        accumulate(offset, upstream_blocks, 2, 3)
        accumulate(-offset, upstream_blocks, 2, 3)
        accumulate(offset, normed_blocks, 0, 2)
        accumulate(-offset, normed_blocks, 0, 2)
    land(far)
    accumulate(far, upstream_blocks, 2, 3)
    accumulate(far, normed_blocks, 0, 2)

    def activate(here):
        gate = total_acc[here, :hidden_units]
        upper = total_acc[here, hidden_units : 2 * hidden_units]
        grad = total_acc[here, 2 * hidden_units :]
        sigmoid = 1.0 / (1.0 + jnp.exp(-gate))
        silu = gate * sigmoid
        activation_ref[here] = (silu * upper).astype(bf16)
        slope = sigmoid * (1.0 + gate * (1.0 - sigmoid))
        gate_up_grad_ref[here, :hidden_units] = (grad * upper * slope).astype(bf16)
        gate_up_grad_ref[here, hidden_units:] = (grad * silu).astype(bf16)

    add_rows(tokens, 16, activate)
    finish()
    for copy in sends:
        copy.wait_send()


def forward_gather(shard, inputs, upstream, qkv, weight, gains, cosine, sine):
    size = lax.axis_size("fsdp")
    ctx = lax.axis_size("ctx")
    tensor = lax.axis_size("tensor")
    far = size // 2
    rows, columns = shard.shape
    slots, quarter, width = inputs.shape
    q_cols = weight.shape[1]
    head_width = gains[2].shape[1]
    heads = q_cols // head_width
    kv = (qkv.shape[1] // head_width - heads) // 2
    tokens = slots * quarter
    hidden_units = columns // 3
    in_vmem = pl.BlockSpec(memory_space=pltpu.VMEM)
    dma = pltpu.SemaphoreType.DMA
    bf16 = jnp.bfloat16
    f32 = jnp.float32
    cores = max(1, tensor - 1)
    shape = jax.ShapeDtypeStruct
    return pl.pallas_call(
        forward_kernel,
        out_shape=(
            shape((rows * size, columns), bf16),
            shape((slots, quarter, q_cols), bf16),
            shape((slots, q_cols, quarter), bf16),
            shape((slots, heads, 1, quarter), f32),
            shape((quarter, width), f32),
            shape((size, tokens, rows), bf16),
            shape((size, tokens, rows), bf16),
            shape((slots, quarter, width), bf16),
            shape((slots, quarter, qkv.shape[1]), f32),
            shape((slots, heads, quarter, head_width), bf16),
            shape((slots, kv, quarter, head_width), bf16),
            shape((slots, kv, head_width, quarter), bf16),
            shape((slots, kv, quarter, head_width), bf16),
            shape((tokens, 2 * hidden_units), bf16),
            shape((tokens, hidden_units), bf16),
        ),
        in_specs=[in_vmem] * 11,
        out_specs=(in_vmem,) * 15,
        scratch_shapes=[
            pltpu.VMEM((slots, kv, head_width, quarter), bf16),
            pltpu.VMEM((tensor, ctx, quarter, width), bf16),
            pltpu.VMEM((tokens, columns), f32),
            pltpu.VMEM((slots, quarter, quarter), f32),
            pltpu.VMEM((1, quarter), f32),
            pltpu.VMEM((1, quarter), f32),
            pltpu.VMEM((head_width, quarter), f32),
            pltpu.VMEM((quarter, width), f32),
            pltpu.VMEM((cores, ctx, quarter, width), bf16),
            pltpu.VMEM((cores, ctx, quarter, width), bf16),
            pltpu.VMEM((max(1, ctx - 1), quarter, width), bf16),
            pltpu.VMEM((max(1, ctx - 1), quarter, width), bf16),
            dma((2, far, 2)),
            dma((2, far, 2)),
            dma((cores, ctx)),
            dma((cores, ctx)),
            dma((ctx,)),
            dma((ctx,)),
            dma((tensor, ctx)),
            dma((tensor, ctx)),
            dma(()),
        ],
        compiler_params=pltpu.CompilerParams(
            collective_id=2, has_side_effects=True, vmem_limit_bytes=62 * 1024 * 1024
        ),
        name="forward_gather",
    )(shard, inputs, upstream, qkv, weight, *gains, cosine, sine)


def group_reduce(part_ref, core_coming, ctx_going, ctx_coming, sems, sends):
    f32 = jnp.float32
    ctx = lax.axis_size("ctx")
    tensor = lax.axis_size("tensor")
    quarter = part_ref.shape[1]
    core_send, core_recv, ctx_send, ctx_recv = sems
    by_core = []
    by_ctx = []

    def over_cores():
        for core in range(1, tensor):
            copy = send(
                part_ref.at[pl.ds(core * ctx, ctx)],
                core_coming.at[core - 1],
                core_send.at[core - 1],
                core_recv.at[core - 1],
                other("tensor", -core),
            )
            sends.append(copy)
            by_core.append(copy)

    def over_ctx(sum_ref):
        for copy in by_core:
            copy.wait_recv()
        for step in list(range(1, ctx)) + [0]:

            def add(block, step=step):
                value = part_ref[step, block].astype(f32)
                for core in range(1, tensor):
                    value = value + core_coming[core - 1, step, block].astype(f32)
                if step == 0:
                    sum_ref[block] = value
                else:
                    ctx_going[step - 1, block] = value.astype(jnp.bfloat16)

            add_rows(quarter, 16, add)
            if step > 0:
                copy = send(
                    ctx_going.at[step - 1],
                    ctx_coming.at[step - 1],
                    ctx_send.at[step - 1],
                    ctx_recv.at[step - 1],
                    other("ctx", -step),
                )
                sends.append(copy)
                by_ctx.append(copy)

    def finish():
        for copy in by_ctx:
            copy.wait_recv()

    return over_cores, over_ctx, finish


def attend_slot_grad(slot, refs, turned_grad, accumulators):
    q_ref, k_ref, kt_ref, v_ref, turned_ref, total_ref, dq_ref = refs
    dq_acc, dk_acc, dv_acc = accumulators
    f32 = jnp.float32
    bf16 = jnp.bfloat16
    slots, heads, quarter, head_width = q_ref.shape
    group = heads // k_ref.shape[1]
    scale = 1.0 / head_width**0.5

    def one_head(head, carry):
        kv_head = lax.div(head, group)
        rows = pl.ds(pl.multiple_of(head * head_width, head_width), head_width)
        grad = turned_grad[rows]
        delta = jnp.sum(
            grad.astype(f32) * turned_ref[slot, rows].astype(f32), axis=0, keepdims=True
        )
        dq_acc[...] = jnp.zeros(dq_acc.shape, f32)

        def one_key_slot(key_slot, carry):
            gap, seen = reachable(slot, key_slot, quarter)

            @pl.when(seen)
            def _():
                queries = q_ref[slot, head]
                scores = masked_scores(k_ref[key_slot, kv_head], queries, gap)
                probs = jnp.exp(scores - total_ref[slot, head])
                prob_grad = jnp.dot(v_ref[key_slot, kv_head], grad, preferred_element_type=f32)
                score_grad = (probs * (prob_grad - delta)).astype(bf16)
                dv_acc[key_slot, head] += lax.dot_general(
                    probs.astype(bf16), grad, (((1,), (1,)), ((), ())), preferred_element_type=f32
                )
                dk_acc[key_slot, head] += jnp.dot(score_grad, queries, preferred_element_type=f32)
                dq_acc[...] += jnp.dot(
                    kt_ref[key_slot, kv_head], score_grad, preferred_element_type=f32
                )

            return carry

        lax.fori_loop(0, slots, one_key_slot, 0)
        dq_ref[slot, head] = (dq_acc[...] * scale).astype(bf16)
        return carry

    lax.fori_loop(0, heads, one_head, 0)


def backward_kernel(
    hidden_part_ref,
    down_part_ref,
    normed_ref,
    upstream_ref,
    gate_up_ref,
    activation_ref,
    hidden_ref,
    own_upstream_ref,
    gain_ref,
    weight_ref,
    q_ref,
    k_ref,
    kt_ref,
    v_ref,
    turned_ref,
    total_ref,
    share_ref,
    hidden_grad_ref,
    all_grad_ref,
    output_ref,
    dq_ref,
    dk_ref,
    dv_ref,
    grad_ref,
    coming,
    core_coming,
    ctx_going,
    ctx_coming,
    sum_ref,
    out_sum_ref,
    turned_grad,
    own_output,
    dq_acc,
    dk_acc,
    dv_acc,
    ring_send,
    ring_recv,
    core_send,
    core_recv,
    ctx_send,
    ctx_recv,
    spread_send,
    spread_recv,
    output_send,
    output_recv,
    local_sem,
):
    f32 = jnp.float32
    bf16 = jnp.bfloat16
    size = lax.axis_size("fsdp")
    ctx = lax.axis_size("ctx")
    tensor = lax.axis_size("tensor")
    me_t = lax.axis_index("tensor")
    far = size // 2
    slots, heads, quarter, head_width = q_ref.shape
    rows = grad_ref.shape[0] // size
    gate_up_cols = gate_up_ref.shape[1]
    hidden_units = activation_ref.shape[1]
    at, _ = ring_ends()
    sends = []
    greet()
    reduce_hidden = group_reduce(
        hidden_part_ref,
        core_coming.at[0],
        ctx_going.at[0],
        ctx_coming.at[0],
        (core_send.at[0], core_recv.at[0], ctx_send.at[0], ctx_recv.at[0]),
        sends,
    )
    reduce_down = group_reduce(
        down_part_ref,
        core_coming.at[1],
        ctx_going.at[1],
        ctx_coming.at[1],
        (core_send.at[1], core_recv.at[1], ctx_send.at[1], ctx_recv.at[1]),
        sends,
    )
    go, finish_ring = scatter_ring(grad_ref, coming, ring_send, ring_recv)

    def piece(offset):
        here = pl.ds(pl.multiple_of(at(offset) * rows, rows), rows)
        for start in range(0, gate_up_cols, hidden_units):
            columns = slice(start, start + hidden_units)
            grad_ref[here, columns] = lax.dot_general(
                normed_ref[at(offset)],
                gate_up_ref[:, columns],
                (((0,), (0,)), ((), ())),
                preferred_element_type=f32,
            ).astype(bf16)
        grad_ref[here, gate_up_cols:] = lax.dot_general(
            upstream_ref[at(offset)],
            activation_ref[...],
            (((0,), (0,)), ((), ())),
            preferred_element_type=f32,
        ).astype(bf16)

    def pieces(offset):
        piece(offset)
        piece(-offset)

    reduce_hidden[0]()
    piece(far)
    go(2)
    reduce_hidden[1](sum_ref)
    reduce_down[0]()
    ready = 0
    if far > 1:
        pieces(far - 1)
        go(2)
        ready = 1
    dk_acc[...] = jnp.zeros(dk_acc.shape, f32)
    dv_acc[...] = jnp.zeros(dv_acc.shape, f32)
    if far > 2:
        pieces(far - 2)
        ready = 2
    go(2)
    reduce_hidden[2]()

    def norm_back(block):
        grad = sum_ref[block]
        for step in range(1, ctx):
            grad = grad + ctx_coming[0, step - 1, block].astype(f32)
        hidden = hidden_ref[block]
        scale = lax.rsqrt(jnp.mean(hidden * hidden, axis=-1, keepdims=True) + EPS)
        grad = grad * gain_ref[...]
        inner = jnp.mean(grad * hidden, axis=-1, keepdims=True) * (scale * scale)
        grad = own_upstream_ref[block].astype(f32) + scale * (grad - hidden * inner)
        hidden_grad_ref[block] = grad
        all_grad_ref[0, block] = grad.astype(bf16)

    add_rows(quarter, 16, norm_back)
    spread = []
    handed = {}
    for step in range(1, ctx):
        copy = send(
            all_grad_ref.at[0],
            all_grad_ref.at[step],
            spread_send.at[0, step],
            spread_recv.at[0, step],
            other("ctx", step),
        )
        sends.append(copy)
        spread.append(copy)

    def hand_over(step):
        for core in range(1, tensor):
            copy = send(
                all_grad_ref.at[step],
                all_grad_ref.at[core * ctx + step],
                spread_send.at[core, step],
                spread_recv.at[core, step],
                other("tensor", core),
            )
            sends.append(copy)
            handed[core, step] = copy

    hand_over(0)
    reduce_down[1](out_sum_ref)

    def attention_back(slot):
        grad = jnp.dot(all_grad_ref[slot], weight_ref[...], preferred_element_type=f32)
        turned_grad[...] = grad.T.astype(bf16)
        attend_slot_grad(
            slot,
            (q_ref, k_ref, kt_ref, v_ref, turned_ref, total_ref, dq_ref),
            turned_grad,
            (dq_acc, dk_acc, dv_acc),
        )

    if far > 2:
        go(2)
    attention_back(0)
    for core in range(1, tensor):
        handed[core, 0].wait_recv()
        attention_back(core * ctx)
    if far > 2:
        go(2)
    for step in range(1, ctx):
        spread[step - 1].wait_recv()
        hand_over(step)
        attention_back(step)
    for offset in range(far - ready - 1, 0, -1):
        pieces(offset)
    piece(0)
    go(2)
    for step in range(1, ctx):
        for core in range(1, tensor):
            handed[core, step].wait_recv()
            attention_back(core * ctx + step)
    go(2)
    scale = 1.0 / head_width**0.5
    for slot in range(slots):
        dk_ref[slot] = (dk_acc[slot] * scale).astype(bf16)
        dv_ref[slot] = dv_acc[slot].astype(bf16)
    reduce_down[2]()

    def output(block):
        value = hidden_ref[block] + out_sum_ref[block]
        for step in range(1, ctx):
            value = value + ctx_coming[1, step - 1, block].astype(f32)
        own_output[block] = value.astype(bf16)

    add_rows(quarter, 16, output)
    keep = pltpu.make_async_copy(own_output, output_ref.at[me_t], local_sem)
    keep.start()
    given = []
    for core in range(1, tensor):
        copy = send(
            own_output,
            output_ref.at[me_t],
            output_send.at[core],
            output_recv.at[core],
            other("tensor", core),
        )
        sends.append(copy)
        given.append(copy)
    finish_ring(share_ref)
    for copy in given:
        copy.wait_recv()
    for copy in sends:
        copy.wait_send()
    keep.wait()


def backward_scatter(
    hidden_part,
    down_part,
    normed_turned,
    upstream_turned,
    gate_up_grad,
    activation,
    hidden,
    own_upstream,
    gain,
    weight,
    queries,
    keys,
    keys_turned,
    values,
    attended_turned,
    totals,
):
    size = lax.axis_size("fsdp")
    ctx = lax.axis_size("ctx")
    tensor = lax.axis_size("tensor")
    far = size // 2
    slots, heads, quarter, head_width = queries.shape
    width = weight.shape[0]
    q_cols = weight.shape[1]
    rows = width // size
    columns = gate_up_grad.shape[1] + activation.shape[1]
    in_vmem = pl.BlockSpec(memory_space=pltpu.VMEM)
    dma = pltpu.SemaphoreType.DMA
    bf16 = jnp.bfloat16
    f32 = jnp.float32
    cores = max(1, tensor - 1)
    apart = max(1, ctx - 1)
    by_head = (slots, heads, quarter, head_width)
    return pl.pallas_call(
        backward_kernel,
        out_shape=(
            jax.ShapeDtypeStruct((rows, columns), bf16),
            jax.ShapeDtypeStruct((quarter, width), f32),
            jax.ShapeDtypeStruct((slots, quarter, width), bf16),
            jax.ShapeDtypeStruct((tensor, quarter, width), bf16),
            jax.ShapeDtypeStruct((slots, heads, head_width, quarter), bf16),
            jax.ShapeDtypeStruct(by_head, bf16),
            jax.ShapeDtypeStruct(by_head, bf16),
        ),
        in_specs=[in_vmem] * 16,
        out_specs=(in_vmem,) * 7,
        scratch_shapes=[
            pltpu.VMEM((width, columns), bf16),
            pltpu.VMEM((2, far, 2, rows // 2, columns), bf16),
            pltpu.VMEM((2, cores, ctx, quarter, width), bf16),
            pltpu.VMEM((2, apart, quarter, width), bf16),
            pltpu.VMEM((2, apart, quarter, width), bf16),
            pltpu.VMEM((quarter, width), f32),
            pltpu.VMEM((quarter, width), f32),
            pltpu.VMEM((q_cols, quarter), bf16),
            pltpu.VMEM((quarter, width), bf16),
            pltpu.VMEM((head_width, quarter), f32),
            pltpu.VMEM(by_head, f32),
            pltpu.VMEM(by_head, f32),
            dma((2, far, 2)),
            dma((2, far, 2)),
            dma((2, cores)),
            dma((2, cores)),
            dma((2, ctx)),
            dma((2, ctx)),
            dma((tensor, ctx)),
            dma((tensor, ctx)),
            dma((tensor,)),
            dma((tensor,)),
            dma(()),
        ],
        compiler_params=pltpu.CompilerParams(
            collective_id=3, has_side_effects=True, vmem_limit_bytes=60 * 1024 * 1024
        ),
        name="backward_scatter",
    )(
        hidden_part,
        down_part,
        normed_turned,
        upstream_turned,
        gate_up_grad,
        activation,
        hidden,
        own_upstream,
        gain,
        weight,
        queries,
        keys,
        keys_turned,
        values,
        attended_turned,
        totals,
    )


def part_of(array, dim, count, start):
    return lax.dynamic_slice_in_dim(array, start, count, dim)


def shards(
    block_input,
    operator_gain,
    query_weight,
    key_weight,
    value_weight,
    output_weight,
    feedforward_gain,
    gate_weight,
    up_weight,
    down_weight,
    query_gain,
    key_gain,
    cotangent,
):
    bf16 = jnp.bfloat16
    f32 = jnp.float32
    fsdp = lax.axis_size("fsdp")
    ctx = lax.axis_size("ctx")
    tensor = lax.axis_size("tensor")
    me_c = lax.axis_index("ctx")
    me_t = lax.axis_index("tensor")
    seqs, tok_here, width = block_input.shape
    quarter = tok_here // tensor
    tokens = tok_here * ctx
    rows = seqs * tokens
    gain_rows = query_gain.shape[0]
    head_width = gain_rows * fsdp
    heads_shard = query_weight.shape[1] // head_width
    kv_shard = key_weight.shape[1] // head_width
    spread = heads_shard // kv_shard
    heads = heads_shard // ctx
    kv = max(1, kv_shard // ctx)
    group = heads // kv
    copies = max(1, ctx // kv_shard)
    q_cols = heads * head_width
    kv_cols = kv * head_width
    kv_start = ((me_c * heads) // spread) * head_width
    hidden_units = gate_weight.shape[1] // ctx
    shard_rows = query_weight.shape[0]

    gains = jnp.stack(
        [
            operator_gain,
            feedforward_gain,
            jnp.pad(query_gain, (0, shard_rows - gain_rows)),
            jnp.pad(key_gain, (0, shard_rows - gain_rows)),
        ],
        axis=1,
    )
    attention_pack = jnp.concatenate(
        [
            part_of(query_weight, 1, q_cols, me_c * q_cols),
            part_of(key_weight, 1, kv_cols, kv_start),
            part_of(value_weight, 1, kv_cols, kv_start),
            part_of(output_weight, 0, q_cols, me_c * q_cols).T,
            jnp.pad(gains, ((0, 0), (0, 124))),
        ],
        axis=1,
    )
    feedforward_shard = jnp.concatenate(
        [
            part_of(gate_weight, 1, hidden_units, me_c * hidden_units),
            part_of(up_weight, 1, hidden_units, me_c * hidden_units),
            part_of(down_weight, 0, hidden_units, me_c * hidden_units).T,
        ],
        axis=1,
    )
    attention_full, all_input, upstream = start_gather(attention_pack, block_input, cotangent)
    all_input = all_input.reshape(rows, width)
    upstream = upstream.reshape(rows, width)
    qkv_cols = q_cols + 2 * kv_cols
    qkv_full = attention_full[:, :qkv_cols]
    output_full = attention_full[:, qkv_cols : qkv_cols + q_cols]
    gains_full = attention_full[:, qkv_cols + q_cols :].astype(f32)
    operator_scale = gains_full[:, 0]
    feedforward_scale = gains_full[:, 1]
    query_scale = gains_full[:, 2].reshape(fsdp, shard_rows)[:, :gain_rows].reshape(-1)
    key_scale = gains_full[:, 3].reshape(fsdp, shard_rows)[:, :gain_rows].reshape(-1)

    own_input = part_of(block_input, 1, quarter, me_t * quarter)
    upstream_own = part_of(cotangent, 1, quarter, me_t * quarter)

    ctx_order = lax.rem(me_c - jnp.arange(ctx) + ctx, ctx)
    tensor_order = lax.rem(me_t - jnp.arange(tensor) + tensor, tensor)
    positions = (
        tensor_order[:, None, None] * quarter
        + ctx_order[None, :, None] * tok_here
        + jnp.arange(quarter)[None, None, :]
    ).reshape(tokens)
    cosine, sine = rotary_tables(positions, head_width)

    def prepare(raw, gain):
        return head_prepare(raw, gain, cosine, sine)

    slots = tensor * ctx
    own_f32 = own_input.astype(f32)
    (
        feedforward_full,
        attended,
        attended_turned,
        totals,
        hidden,
        normed_blocks,
        upstream_blocks,
        normed_input,
        qkv_raw,
        queries,
        keys,
        keys_turned,
        values,
        gate_up_grad,
        activation,
    ) = forward_gather(
        feedforward_shard,
        all_input.reshape(slots, quarter, width),
        upstream.reshape(slots, quarter, width),
        qkv_full,
        output_full,
        (
            operator_scale[None],
            feedforward_scale[None],
            query_scale[None],
            key_scale[None],
        ),
        cosine.reshape(slots, quarter, -1),
        sine.reshape(slots, quarter, -1),
    )
    attended_rows = attended.reshape(rows, q_cols)
    normed_input = normed_input.reshape(rows, width)
    qkv_raw = qkv_raw.reshape(seqs, tokens, -1)
    _, query_back = jax.vjp(prepare, qkv_raw[..., :q_cols], query_scale)
    _, key_back = jax.vjp(prepare, qkv_raw[..., q_cols : q_cols + kv_cols], key_scale)
    gate_up_full = feedforward_full[:, : 2 * hidden_units]
    down_full = feedforward_full[:, 2 * hidden_units :]
    hidden_part = contract(gate_up_grad, gate_up_full, 1, 1).astype(bf16)
    down_part = contract(activation, down_full, 1, 1).astype(bf16)
    (
        feedforward_share,
        hidden_grad,
        all_hidden_grad,
        block_output,
        query_hgrad,
        key_hgrad,
        value_hgrad,
    ) = backward_scatter(
        hidden_part.reshape(slots, quarter, width),
        down_part.reshape(slots, quarter, width),
        normed_blocks,
        upstream_blocks,
        gate_up_grad,
        activation,
        hidden,
        upstream_own.reshape(quarter, width),
        feedforward_scale.reshape(1, width),
        output_full,
        queries,
        keys,
        keys_turned,
        values,
        attended_turned,
        totals,
    )
    hidden_grad = hidden_grad[None]
    block_output = block_output.reshape(seqs, tok_here, width)
    output_weight_grad = contract(all_hidden_grad.reshape(rows, width), attended_rows, 0, 0)
    query_hgrad = query_hgrad.transpose(0, 3, 1, 2).reshape(seqs, tokens, heads, head_width)
    key_hgrad = key_hgrad.transpose(0, 2, 1, 3).reshape(seqs, tokens, heads, head_width)
    value_hgrad = value_hgrad.transpose(0, 2, 1, 3).reshape(seqs, tokens, heads, head_width)

    def head_sum(grad):
        return grad.astype(f32).reshape(seqs, tokens, kv, group, head_width).sum(axis=3)

    query_pre, query_gain_grad = query_back(query_hgrad.astype(f32))
    key_pre, key_gain_grad = key_back(head_sum(key_hgrad))
    qkv_raw_grad = jnp.concatenate(
        [
            query_pre.astype(bf16).reshape(rows, q_cols),
            key_pre.astype(bf16).reshape(rows, kv_cols),
            head_sum(value_hgrad).astype(bf16).reshape(rows, kv_cols),
        ],
        axis=1,
    )
    input_part = contract(qkv_raw_grad, qkv_full, 1, 1).reshape(tensor, ctx, quarter, width)
    qkv_weight_grad = contract(normed_input, qkv_raw_grad, 0, 0)
    gain_grads = jnp.stack([query_gain_grad, key_gain_grad], axis=1).reshape(fsdp, gain_rows, 2)
    gain_grads = jnp.pad(
        gain_grads, ((0, 0), (0, shard_rows - gain_rows), (0, 126))
    ).reshape(width, 128)
    attention_grad = jnp.concatenate(
        [qkv_weight_grad, output_weight_grad, gain_grads], axis=1
    ).astype(bf16)
    feedforward_parts = in_order(feedforward_share[None], "ctx", 0)
    attention_grad, feedforward_parts = lax.optimization_barrier(
        (attention_grad, feedforward_parts)
    )
    attention_parts, normed_input_grad = finish_sums(attention_grad, input_part)
    attention_parts = attention_parts.astype(f32)
    normed_input_grad = normed_input_grad[None]
    _, norm_one_back = jax.vjp(lambda v: rms_scale(v, operator_scale), own_f32)
    (input_norm_grad,) = norm_one_back(normed_input_grad)
    input_grad = in_order(hidden_grad + input_norm_grad, "tensor", 1)

    def columns(parts):
        return jnp.concatenate([parts[step] for step in range(ctx)], axis=1)

    def head_columns(parts):
        every = columns(parts)
        if copies == 1:
            return every
        return every.reshape(shard_rows, kv_shard, copies, head_width).sum(axis=2).reshape(
            shard_rows, -1
        )

    query_weight_grad = columns(attention_parts[:, :, :q_cols])
    key_weight_grad = head_columns(attention_parts[:, :, q_cols : q_cols + kv_cols])
    value_weight_grad = head_columns(attention_parts[:, :, q_cols + kv_cols : qkv_cols])
    gate_weight_grad = columns(feedforward_parts[:, :, :hidden_units].astype(f32))
    up_weight_grad = columns(
        feedforward_parts[:, :, hidden_units : 2 * hidden_units].astype(f32)
    )
    down_weight_grad = jnp.swapaxes(feedforward_parts[:, :, 2 * hidden_units :], 1, 2)
    down_weight_grad = down_weight_grad.astype(f32).reshape(-1, shard_rows)
    gain_parts = attention_parts[:, :, qkv_cols + q_cols : qkv_cols + q_cols + 2].sum(axis=0)

    def gain_part(pairs, gain):
        total = 0.0
        for weight, grad in pairs:
            total = total + jnp.sum(weight.astype(f32) * grad, axis=1)
        return total / gain.astype(f32)

    gain_columns = jnp.concatenate(
        [
            gain_part(
                [
                    (query_weight, query_weight_grad),
                    (key_weight, key_weight_grad),
                    (value_weight, value_weight_grad),
                ],
                operator_gain,
            )[:, None],
            gain_part(
                [(gate_weight, gate_weight_grad), (up_weight, up_weight_grad)], feedforward_gain
            )[:, None],
            gain_parts,
        ],
        axis=1,
    )
    gain_totals = gain_columns
    for step in range(1, tensor):
        gain_totals = gain_totals + shift(gain_columns, "tensor", step)

    return (
        block_output,
        input_grad,
        gain_totals[:, 0],
        query_weight_grad,
        key_weight_grad,
        value_weight_grad,
        jnp.swapaxes(attention_parts[:, :, qkv_cols : qkv_cols + q_cols], 1, 2).reshape(
            -1, shard_rows
        ),
        gain_totals[:, 1],
        gate_weight_grad,
        up_weight_grad,
        down_weight_grad,
        gain_totals[:gain_rows, 2],
        gain_totals[:gain_rows, 3],
    )


def solution(mesh):
    in_specs = (
        P("fsdp", "ctx", None),
        P("fsdp"),
        P("fsdp", "tensor"),
        P("fsdp", "tensor"),
        P("fsdp", "tensor"),
        P("tensor", "fsdp"),
        P("fsdp"),
        P("fsdp", "tensor"),
        P("fsdp", "tensor"),
        P("tensor", "fsdp"),
        P("fsdp"),
        P("fsdp"),
        P("fsdp", "ctx", None),
    )
    out_specs = (
        P("fsdp", "ctx", None),
        P("fsdp", "ctx", None),
        P("fsdp"),
        P("fsdp", "tensor"),
        P("fsdp", "tensor"),
        P("fsdp", "tensor"),
        P("tensor", "fsdp"),
        P("fsdp"),
        P("fsdp", "tensor"),
        P("fsdp", "tensor"),
        P("tensor", "fsdp"),
        P("fsdp"),
        P("fsdp"),
    )
    return jax.shard_map(shards, mesh=mesh, in_specs=in_specs, out_specs=out_specs, check_vma=False)
```

```python
import jax
import jax.numpy as jnp
from jax import lax
from jax.experimental import pallas as pl
from jax.experimental.pallas import tpu as pltpu
from jax.sharding import PartitionSpec as P

EPS = 1e-05
THETA = 1000000.0


def rms_scale(values_in, gain):
    return (
        values_in * lax.rsqrt(jnp.mean(values_in * values_in, axis=-1, keepdims=True) + EPS) * gain
    )


def rotary_tables(positions, head_width):
    half_width = head_width // 2
    freqs = THETA ** (-jnp.arange(half_width).astype(jnp.float32) * 2.0 / head_width)
    angles = positions.astype(jnp.float32)[:, None] * freqs[None, :]
    return (jnp.cos(angles), jnp.sin(angles))


def rotate_halves(heads_in, cosine, sine):
    half_width = heads_in.shape[-1] // 2
    front_half = heads_in[..., :half_width]
    back_half = heads_in[..., half_width:]
    cos_rows = cosine[:, None, :]
    sin_rows = sine[:, None, :]
    return jnp.concatenate(
        [
            front_half * cos_rows - back_half * sin_rows,
            back_half * cos_rows + front_half * sin_rows,
        ],
        axis=-1,
    )


def head_prepare(raw, gain, cosine, sine):
    head_width = gain.shape[0]
    shaped = raw.reshape(raw.shape[:-1] + (raw.shape[-1] // head_width, head_width))
    return rotate_halves(rms_scale(shaped, gain), cosine, sine)


def swiglu(gate, upper):
    return jax.nn.silu(gate) * upper


def contract(left, right, left_dim, right_dim):
    return lax.dot_general(
        left, right, (((left_dim,), (right_dim,)), ((), ())), preferred_element_type=jnp.float32
    )


def block_scores(query_block, keys, query_pos, key_pos):
    scale = 1.0 / query_block.shape[-1] ** 0.5
    scores = (
        jnp.einsum("qhd,khd->hqk", query_block, keys, preferred_element_type=jnp.float32) * scale
    )
    allowed = key_pos[None, :] <= query_pos[:, None]
    return jnp.where(allowed[None, :, :], scores, -1e30)


def attend(queries, keys, values, positions):
    length = queries.shape[0]
    block_rows = min(512, length)
    outputs = []
    totals = []
    for start in range(0, length, block_rows):
        rows = slice(start, start + block_rows)
        scores = block_scores(queries[rows], keys, positions[rows], positions)
        peak = jnp.max(scores, axis=-1, keepdims=True)
        log_total = peak + jnp.log(jnp.sum(jnp.exp(scores - peak), axis=-1, keepdims=True))
        probs = jnp.exp(scores - log_total).astype(jnp.bfloat16)
        block_out = jnp.einsum("hqk,khd->qhd", probs, values, preferred_element_type=jnp.float32)
        outputs.append(block_out.astype(jnp.bfloat16))
        totals.append(log_total[..., 0])
    return (jnp.concatenate(outputs, axis=0), jnp.concatenate(totals, axis=1))


def attend_grad(queries, keys, values, outputs, totals, out_grad, positions):
    length = queries.shape[0]
    block_rows = min(512, length)
    scale = 1.0 / queries.shape[-1] ** 0.5
    key_acc = jnp.zeros(keys.shape, jnp.float32)
    value_acc = jnp.zeros(values.shape, jnp.float32)
    query_parts = []
    for start in range(0, length, block_rows):
        rows = slice(start, start + block_rows)
        query_block = queries[rows]
        scores = block_scores(query_block, keys, positions[rows], positions)
        probs = jnp.exp(scores - totals[:, rows][..., None])
        grad_block = out_grad[rows]
        value_acc = value_acc + jnp.einsum(
            "hqk,qhd->khd",
            probs.astype(jnp.bfloat16),
            grad_block,
            preferred_element_type=jnp.float32,
        )
        prob_grad = jnp.einsum(
            "qhd,khd->hqk", grad_block, values, preferred_element_type=jnp.float32
        )
        delta = jnp.sum(
            grad_block.astype(jnp.float32) * outputs[rows].astype(jnp.float32),
            axis=-1,
        ).T
        score_grad = (probs * (prob_grad - delta[..., None])).astype(jnp.bfloat16)
        query_parts.append(
            (
                jnp.einsum("hqk,khd->qhd", score_grad, keys, preferred_element_type=jnp.float32)
                * scale
            ).astype(jnp.bfloat16)
        )
        key_acc = (
            key_acc
            + jnp.einsum(
                "hqk,qhd->khd", score_grad, query_block, preferred_element_type=jnp.float32
            )
            * scale
        )
    return (
        jnp.concatenate(query_parts, axis=0),
        key_acc.astype(jnp.bfloat16),
        value_acc.astype(jnp.bfloat16),
    )


def shift(array, axis_name, step):
    size = lax.axis_size(axis_name)
    return lax.ppermute(array, axis_name, [(i, (i + step) % size) for i in range(size)])


def around(array, axis_name, dim):
    size = lax.axis_size(axis_name)
    return jnp.concatenate(
        [array] + [shift(array, axis_name, step) for step in range(1, size)], axis=dim
    )


def group_rows(array):
    return around(around(array, "ctx", 1), "tensor", 1)


def sum_around(array, axis_name):
    size = lax.axis_size(axis_name)
    part = array.shape[1] // size
    total = array[:, :part].astype(jnp.float32)
    for step in range(1, size):
        piece = array[:, step * part : (step + 1) * part].astype(jnp.bfloat16)
        total = total + shift(piece, axis_name, -step).astype(jnp.float32)
    return total


def group_sum(array):
    return sum_around(sum_around(array, "tensor"), "ctx")


def in_order(array, axis_name, dim):
    size = lax.axis_size(axis_name)
    me = lax.axis_index(axis_name)
    width = array.shape[dim]
    shape = list(array.shape)
    shape[dim] = width * size
    out = jnp.zeros(shape, array.dtype)
    for step in range(size):
        piece = array if step == 0 else shift(array, axis_name, step)
        owner = lax.rem(me - step + size, size)
        out = lax.dynamic_update_slice_in_dim(out, piece, owner * width, dim)
    return out


def ring_index(place, size):
    if size % 2:
        return place
    turn = size // 2
    return jnp.where(place < turn, 2 * place, 2 * (size - 1 - place) + 1)


def ring_place(index, size):
    if size % 2:
        return index
    return jnp.where(lax.rem(index, 2) == 0, lax.div(index, 2), size - 1 - lax.div(index, 2))


def ring_order(size):
    if size % 2:
        return list(range(size))
    return [2 * i for i in range(size // 2)] + [2 * i + 1 for i in reversed(range(size // 2))]


def ring_shift(array, axis_name, step):
    size = lax.axis_size(axis_name)
    order = ring_order(size)
    pairs = [(order[i], order[(i + step) % size]) for i in range(size)]
    return lax.ppermute(array, axis_name, pairs)


def ring_gather(shard, axis_name, dim=0):
    size = lax.axis_size(axis_name)
    place = ring_place(lax.axis_index(axis_name), size)
    shape = list(shard.shape)
    shape[dim] *= size
    half = shard.shape[0] // 2
    out = jnp.zeros(shape, shard.dtype)

    def put(out, piece, at, offset):
        owner = ring_index(lax.rem(at + size, size), size)
        starts = [offset, 0]
        starts[dim] += owner * shard.shape[dim]
        return lax.dynamic_update_slice(out, piece, starts)

    out = put(out, shard, place, 0)
    rightward = leftward = shard
    for step in range(1, (size + 1) // 2):
        rightward = ring_shift(rightward, axis_name, 1)
        leftward = ring_shift(leftward, axis_name, -1)
        out = put(out, rightward, place - step, 0)
        out = put(out, leftward, place + step, 0)
    if size % 2 == 0:
        rightward = ring_shift(rightward[:half], axis_name, 1)
        leftward = ring_shift(leftward[half:], axis_name, -1)
        out = put(out, rightward, place + size // 2, 0)
        out = put(out, leftward, place + size // 2, half)
    return out, rightward


def ring_scatter(piece_for, axis_name):
    size = lax.axis_size(axis_name)
    place = ring_place(lax.axis_index(axis_name), size)

    def piece(offset):
        return piece_for(ring_index(lax.rem(place + offset + size, size), size))

    mine = piece(0).astype(jnp.float32)
    if size == 1:
        return mine
    half = mine.shape[0] // 2
    far = size // 2
    bf16 = jnp.bfloat16
    f32 = jnp.float32
    if size % 2 == 0:
        across = piece(far)
        rightward = ring_shift(across[:half].astype(bf16), axis_name, 1).astype(f32)
        leftward = ring_shift(across[half:].astype(bf16), axis_name, -1).astype(f32)
        zero = jnp.zeros_like(mine[:half])
        rightward = jnp.concatenate([rightward, zero], axis=0)
        leftward = jnp.concatenate([zero, leftward], axis=0)
        steps = far - 1
    else:
        rightward = leftward = jnp.zeros_like(mine)
        steps = far
    for step in range(steps, 0, -1):
        rightward = ring_shift((rightward + piece(step)).astype(bf16), axis_name, 1).astype(f32)
        leftward = ring_shift((leftward + piece(-step)).astype(bf16), axis_name, -1).astype(f32)
    return mine + rightward + leftward


def other(axis_name, step):
    size = lax.axis_size(axis_name)
    return {axis_name: lax.rem(lax.axis_index(axis_name) + step + size, size)}


def send(source, target, send_sem, recv_sem, device):
    copy = pltpu.make_async_remote_copy(
        src_ref=source,
        dst_ref=target,
        send_sem=send_sem,
        recv_sem=recv_sem,
        device_id=device,
        device_id_type=pl.DeviceIdType.MESH,
    )
    copy.start()
    return copy


def ring_ends():
    size = lax.axis_size("fsdp")
    place = ring_place(lax.axis_index("fsdp"), size)

    def at(offset):
        return ring_index(lax.rem(place + offset + size, size), size)

    return at, ({"fsdp": at(1)}, {"fsdp": at(-1)})


def greet():
    _, ends = ring_ends()
    partners = list(ends)
    for axis_name in ("ctx", "tensor"):
        partners += [other(axis_name, step) for step in range(1, lax.axis_size(axis_name))]
    barrier = pltpu.get_barrier_semaphore()
    for device in partners:
        pl.semaphore_signal(
            barrier, inc=1, device_id=device, device_id_type=pl.DeviceIdType.MESH
        )
    pl.semaphore_wait(barrier, len(partners))


def start_kernel(
    pack_ref,
    input_ref,
    upstream_ref,
    full_ref,
    all_input_ref,
    all_upstream_ref,
    ring_send,
    ring_recv,
    ctx_send,
    ctx_recv,
    tensor_send,
    tensor_recv,
    local_sem,
):
    size = lax.axis_size("fsdp")
    ctx = lax.axis_size("ctx")
    tensor = lax.axis_size("tensor")
    me_t = lax.axis_index("tensor")
    far = size // 2
    rows = pack_ref.shape[0]
    sub_rows = rows // 2
    quarter = all_input_ref.shape[2]
    at, ends = ring_ends()
    greet()
    pairs = ((input_ref, all_input_ref), (upstream_ref, all_upstream_ref))

    def block(owner, sub):
        start = pl.multiple_of(owner * rows + sub * sub_rows, sub_rows)
        return full_ref.at[pl.ds(start, sub_rows)]

    sends = []
    arrivals = {}

    def ring_step(step):
        for sub in range(2):
            for way in range(2):
                if step == far and sub != way:
                    continue
                if step > 1:
                    arrivals.pop((way, step - 1, sub)).wait_recv()
                owner = at((1 - step) if way == 0 else (step - 1))
                source = (
                    pack_ref.at[pl.ds(sub * sub_rows, sub_rows)] if step == 1 else block(owner, sub)
                )
                copy = send(
                    source,
                    block(owner, sub),
                    ring_send.at[way, step - 1, sub],
                    ring_recv.at[way, step - 1, sub],
                    ends[way],
                )
                sends.append(copy)
                arrivals[way, step, sub] = copy

    def own_rows(source, step):
        quarter_at = lax.rem(me_t - step + tensor, tensor)
        return source.at[0, pl.ds(pl.multiple_of(quarter_at * quarter, quarter), quarter)]

    ring_step(1)
    crossed = {}
    locals_ = []
    for which, (source, target) in enumerate(pairs):
        for step in range(1, ctx):
            copy = send(
                own_rows(source, 0),
                target.at[0, step],
                ctx_send.at[which, step - 1],
                ctx_recv.at[which, step - 1],
                other("ctx", step),
            )
            sends.append(copy)
            crossed[which, step] = copy
    for which, (source, target) in enumerate(pairs):
        for step in range(tensor):
            copy = pltpu.make_async_copy(
                own_rows(source, step), target.at[step, 0], local_sem.at[which, step]
            )
            copy.start()
            locals_.append(copy)
    own_copy = pltpu.make_async_copy(
        pack_ref,
        full_ref.at[pl.ds(pl.multiple_of(at(0) * rows, rows), rows)],
        local_sem.at[2, 0],
    )
    own_copy.start()
    locals_.append(own_copy)
    handed = []

    def hand_over(which):
        _, target = pairs[which]
        for step in range(1, ctx):
            crossed[which, step].wait_recv()
            for core in range(1, tensor):
                copy = send(
                    target.at[0, step],
                    target.at[core, step],
                    tensor_send.at[which, core - 1, step - 1],
                    tensor_recv.at[which, core - 1, step - 1],
                    other("tensor", core),
                )
                sends.append(copy)
                handed.append(copy)

    for step in range(2, far + 1):
        if step == far:
            hand_over(0)
        ring_step(step)
    if far < 2:
        hand_over(0)
    hand_over(1)
    for copy in arrivals.values():
        copy.wait_recv()
    for copy in handed:
        copy.wait_recv()
    for copy in sends:
        copy.wait_send()
    for copy in locals_:
        copy.wait()


def start_gather(pack, block_input, cotangent):
    size = lax.axis_size("fsdp")
    ctx = lax.axis_size("ctx")
    tensor = lax.axis_size("tensor")
    far = size // 2
    rows, columns = pack.shape
    _, tok_here, width = block_input.shape
    every = (tensor, ctx, tok_here // tensor, width)
    in_vmem = pl.BlockSpec(memory_space=pltpu.VMEM)
    dma = pltpu.SemaphoreType.DMA
    return pl.pallas_call(
        start_kernel,
        out_shape=(
            jax.ShapeDtypeStruct((rows * size, columns), pack.dtype),
            jax.ShapeDtypeStruct(every, block_input.dtype),
            jax.ShapeDtypeStruct(every, cotangent.dtype),
        ),
        in_specs=[in_vmem] * 3,
        out_specs=(in_vmem,) * 3,
        scratch_shapes=[
            dma((2, far, 2)),
            dma((2, far, 2)),
            dma((2, ctx)),
            dma((2, ctx)),
            dma((2, tensor, ctx)),
            dma((2, tensor, ctx)),
            dma((3, tensor)),
        ],
        compiler_params=pltpu.CompilerParams(
            collective_id=0, has_side_effects=True, vmem_limit_bytes=32 * 1024 * 1024
        ),
        name="start_gather",
    )(pack, block_input, cotangent)


def add_rows(count, block_rows, body):
    def step(index, carry):
        body(pl.ds(pl.multiple_of(index * block_rows, block_rows), block_rows))
        return carry

    lax.fori_loop(0, count // block_rows, step, 0)


def finish_kernel(
    grad_ref,
    part_ref,
    parts_ref,
    total_ref,
    going,
    coming,
    share,
    core_going,
    core_coming,
    ctx_going,
    ctx_coming,
    ring_send,
    ring_recv,
    core_send,
    core_recv,
    ctx_send,
    ctx_recv,
    share_send,
    share_recv,
    local_sem,
):
    f32 = jnp.float32
    bf16 = jnp.bfloat16
    size = lax.axis_size("fsdp")
    ctx = lax.axis_size("ctx")
    tensor = lax.axis_size("tensor")
    me_c = lax.axis_index("ctx")
    far = size // 2
    rows = share.shape[0]
    sub_rows = rows // 2
    quarter = part_ref.shape[2]
    at, ends = ring_ends()
    greet()
    sends = []
    arrivals = {}

    def own_block(owner, sub):
        return pl.ds(pl.multiple_of(owner * rows + sub * sub_rows, sub_rows), sub_rows)

    def ring_step(step):
        for sub in range(2):
            for way in range(2):
                if step == 1 and sub != way:
                    continue
                ahead = far + 1 - step
                owner = at(ahead if way == 0 else -ahead)
                mine = own_block(owner, sub)
                if step == 1:
                    source = grad_ref.at[mine]
                else:
                    source = going.at[way, step - 2, sub]
                    if (way, step - 1, sub) in arrivals:
                        arrivals.pop((way, step - 1, sub)).wait_recv()
                        source[...] = (
                            grad_ref[mine, :].astype(f32)
                            + coming[way, step - 2, sub].astype(f32)
                        ).astype(bf16)
                    else:
                        source = grad_ref.at[mine]
                copy = send(
                    source,
                    coming.at[way, step - 1, sub],
                    ring_send.at[way, step - 1, sub],
                    ring_recv.at[way, step - 1, sub],
                    ends[way],
                )
                sends.append(copy)
                arrivals[way, step, sub] = copy

    ring_step(1)
    by_core = []
    for core in range(1, tensor):
        for step in range(ctx):

            def narrow(block, core=core, step=step):
                core_going[core - 1, step, block] = part_ref[core, step, block].astype(bf16)

            add_rows(quarter, 32, narrow)
        copy = send(
            core_going.at[core - 1],
            core_coming.at[core - 1],
            core_send.at[core - 1],
            core_recv.at[core - 1],
            other("tensor", -core),
        )
        sends.append(copy)
        by_core.append(copy)
    if far > 1:
        ring_step(2)
    for copy in by_core:
        copy.wait_recv()
    by_ctx = []
    for step in list(range(1, ctx)) + [0]:

        def total(block, step=step):
            value = part_ref[0, step, block].astype(f32)
            for core in range(1, tensor):
                value = value + core_coming[core - 1, step, block].astype(f32)
            if step == 0:
                total_ref[block] = value
            else:
                ctx_going[step - 1, block] = value.astype(bf16)

        add_rows(quarter, 32, total)
        if step > 0:
            copy = send(
                ctx_going.at[step - 1],
                ctx_coming.at[step - 1],
                ctx_send.at[step - 1],
                ctx_recv.at[step - 1],
                other("ctx", -step),
            )
            sends.append(copy)
            by_ctx.append(copy)
    for step in range(3, far + 1):
        ring_step(step)
    mine = at(0)
    for sub in range(2):
        value = grad_ref[own_block(mine, sub), :].astype(f32)
        for way in range(2):
            if (way, far, sub) in arrivals:
                arrivals.pop((way, far, sub)).wait_recv()
                value = value + coming[way, far - 1, sub].astype(f32)
        share[sub * sub_rows : (sub + 1) * sub_rows, :] = value.astype(bf16)
    shared = []
    for step in range(1, ctx):
        copy = send(
            share,
            parts_ref.at[me_c],
            share_send.at[step - 1],
            share_recv.at[step - 1],
            other("ctx", step),
        )
        sends.append(copy)
        shared.append(copy)
    keep = pltpu.make_async_copy(share, parts_ref.at[me_c], local_sem)
    keep.start()
    for step in range(1, ctx):
        by_ctx[step - 1].wait_recv()

        def gather(block, step=step):
            total_ref[block] += ctx_coming[step - 1, block].astype(f32)

        add_rows(quarter, 32, gather)
    for step in range(1, ctx):
        shared[step - 1].wait_recv()
    for copy in sends:
        copy.wait_send()
    keep.wait()


def finish_sums(grad, part):
    size = lax.axis_size("fsdp")
    tensor, ctx, quarter, width = part.shape
    far = size // 2
    rows, columns = grad.shape[0] // size, grad.shape[1]
    in_vmem = pl.BlockSpec(memory_space=pltpu.VMEM)
    anywhere = pl.BlockSpec(memory_space=pl.ANY)
    dma = pltpu.SemaphoreType.DMA
    bf16 = jnp.bfloat16
    return pl.pallas_call(
        finish_kernel,
        out_shape=(
            jax.ShapeDtypeStruct((ctx, rows, columns), bf16),
            jax.ShapeDtypeStruct((quarter, width), jnp.float32),
        ),
        in_specs=[in_vmem] * 2,
        out_specs=(anywhere, in_vmem),
        scratch_shapes=[
            pltpu.VMEM((2, max(1, far - 1), 2, rows // 2, columns), bf16),
            pltpu.VMEM((2, far, 2, rows // 2, columns), bf16),
            pltpu.VMEM((rows, columns), bf16),
            pltpu.VMEM((max(1, tensor - 1), ctx, quarter, width), bf16),
            pltpu.VMEM((max(1, tensor - 1), ctx, quarter, width), bf16),
            pltpu.VMEM((max(1, ctx - 1), quarter, width), bf16),
            pltpu.VMEM((max(1, ctx - 1), quarter, width), bf16),
            dma((2, far, 2)),
            dma((2, far, 2)),
            dma((tensor,)),
            dma((tensor,)),
            dma((ctx,)),
            dma((ctx,)),
            dma((ctx,)),
            dma((ctx,)),
            dma(()),
        ],
        compiler_params=pltpu.CompilerParams(
            collective_id=1, has_side_effects=True, vmem_limit_bytes=48 * 1024 * 1024
        ),
        name="finish_sums",
    )(grad, part)


def gather_ring(shard_ref, full_ref, send_sem, recv_sem):
    size = lax.axis_size("fsdp")
    far = size // 2
    rows = shard_ref.shape[0]
    sub_rows = rows // 2
    at, ends = ring_ends()
    sends = []
    arrivals = {}
    queue = [(step, sub) for step in range(1, far + 1) for sub in range(2)]

    def block(owner, sub):
        start = pl.multiple_of(owner * rows + sub * sub_rows, sub_rows)
        return full_ref.at[pl.ds(start, sub_rows)]

    def go(count):
        for _ in range(min(count, len(queue))):
            step, sub = queue.pop(0)
            for way in range(2):
                if (way, step - 1, sub) in arrivals and (step < far or sub == way):
                    arrivals.pop((way, step - 1, sub)).wait_recv()
                if step == far and sub != way:
                    continue
                owner = at((1 - step) if way == 0 else (step - 1))
                source = (
                    shard_ref.at[pl.ds(sub * sub_rows, sub_rows)] if step == 1 else block(owner, sub)
                )
                copy = send(
                    source,
                    block(owner, sub),
                    send_sem.at[way, step - 1, sub],
                    recv_sem.at[way, step - 1, sub],
                    ends[way],
                )
                sends.append(copy)
                arrivals[way, step, sub] = copy

    def land(step):
        while len(queue) > 0 and queue[0][0] <= step:
            go(1)
        for key in [key for key in arrivals if key[1] <= step]:
            arrivals.pop(key).wait_recv()

    def finish():
        go(len(queue))
        land(far)
        for copy in sends:
            copy.wait_send()

    return go, land, finish


def scatter_ring(grad_ref, first_ref, coming, send_sem, recv_sem):
    f32 = jnp.float32
    size = lax.axis_size("fsdp")
    far = size // 2
    rows = grad_ref.shape[0] // size
    sub_rows = rows // 2
    step_rows = 16
    at, ends = ring_ends()
    sends = []
    arrivals = {}
    queue = [(1, 0, 0), (1, 1, 1)]
    for step in range(2, far + 1):
        queue += [(step, 1, 0), (step, 0, 1), (step, 0, 0), (step, 1, 1)]

    def start_of(owner, sub):
        return pl.multiple_of(owner * rows + sub * sub_rows, sub_rows)

    def go(count):
        for _ in range(min(count, len(queue))):
            step, way, sub = queue.pop(0)
            ahead = far + 1 - step
            first = start_of(at(ahead if way == 0 else -ahead), sub)
            if (way, step - 1, sub) in arrivals:
                arrivals.pop((way, step - 1, sub)).wait_recv()

                def add(index, carry, way=way, step=step, sub=sub, first=first):
                    here = pl.ds(pl.multiple_of(index * step_rows, step_rows), step_rows)
                    there = pl.ds(
                        pl.multiple_of(first + index * step_rows, step_rows), step_rows
                    )
                    grad_ref[there] = (
                        grad_ref[there].astype(f32) + coming[way, step - 2, sub, here].astype(f32)
                    ).astype(grad_ref.dtype)
                    return carry

                lax.fori_loop(0, sub_rows // step_rows, add, 0)
            source = (
                first_ref.at[pl.ds(sub * sub_rows, sub_rows)]
                if step == 1
                else grad_ref.at[pl.ds(first, sub_rows)]
            )
            copy = send(
                source,
                coming.at[way, step - 1, sub],
                send_sem.at[way, step - 1, sub],
                recv_sem.at[way, step - 1, sub],
                ends[way],
            )
            sends.append(copy)
            arrivals[way, step, sub] = copy

    def finish(share_ref):
        go(len(queue))
        for copy in sends:
            copy.wait_send()
        for sub in range(2):
            landed = []
            for way in range(2):
                if (way, far, sub) in arrivals:
                    arrivals.pop((way, far, sub)).wait_recv()
                    landed.append(way)

            def add(index, carry, sub=sub, landed=landed):
                here = pl.ds(pl.multiple_of(index * step_rows, step_rows), step_rows)
                there = pl.ds(
                    pl.multiple_of(start_of(at(0), sub) + index * step_rows, step_rows), step_rows
                )
                out = pl.ds(
                    pl.multiple_of(sub * sub_rows + index * step_rows, step_rows), step_rows
                )
                value = grad_ref[there].astype(f32)
                for way in landed:
                    value = value + coming[way, far - 1, sub, here].astype(f32)
                share_ref[out] = value.astype(share_ref.dtype)
                return carry

            lax.fori_loop(0, sub_rows // step_rows, add, 0)

    return go, finish


def slot_base(slot, quarter):
    ctx = lax.axis_size("ctx")
    tensor = lax.axis_size("tensor")
    of_core = lax.rem(lax.axis_index("tensor") - lax.div(slot, ctx) + tensor, tensor)
    of_ctx = lax.rem(lax.axis_index("ctx") - lax.rem(slot, ctx) + ctx, ctx)
    return of_core * quarter + of_ctx * (quarter * tensor)


def reachable(query_slot, key_slot, quarter):
    gap = slot_base(query_slot, quarter) - slot_base(key_slot, quarter)
    return gap, gap > -quarter


def masked_scores(keys, queries, gap):
    scores = lax.dot_general(
        keys, queries, (((1,), (1,)), ((), ())), preferred_element_type=jnp.float32
    ) * (1.0 / queries.shape[-1] ** 0.5)
    key_at = lax.broadcasted_iota(jnp.int32, scores.shape, 0)
    query_at = lax.broadcasted_iota(jnp.int32, scores.shape, 1)
    return jnp.where(key_at - query_at <= gap, scores, -1e30)


def attend_slot(slot, q_ref, k_ref, vt_ref, attended_ref, turned_ref, total_ref, work):
    scores_ref, peak_ref, sum_ref, out_ref = work
    slots, heads, quarter, head_width = q_ref.shape
    group = heads // k_ref.shape[1]

    def one_head(head, carry):
        kv_head = lax.div(head, group)
        peak_ref[...] = jnp.full(peak_ref.shape, -1e30, jnp.float32)
        sum_ref[...] = jnp.zeros(sum_ref.shape, jnp.float32)
        out_ref[...] = jnp.zeros(out_ref.shape, jnp.float32)

        def score(key_slot, carry):
            gap, seen = reachable(slot, key_slot, quarter)

            @pl.when(seen)
            def _():
                scores = masked_scores(k_ref[key_slot, kv_head], q_ref[slot, head], gap)
                scores_ref[key_slot] = scores
                peak_ref[...] = jnp.maximum(peak_ref[...], jnp.max(scores, axis=0, keepdims=True))

            return carry

        lax.fori_loop(0, slots, score, 0)

        def weigh(key_slot, carry):
            _, seen = reachable(slot, key_slot, quarter)

            @pl.when(seen)
            def _():
                raised = jnp.exp(scores_ref[key_slot] - peak_ref[...])
                sum_ref[...] += jnp.sum(raised, axis=0, keepdims=True)
                out_ref[...] += jnp.dot(
                    vt_ref[key_slot, kv_head],
                    raised.astype(jnp.bfloat16),
                    preferred_element_type=jnp.float32,
                )

            return carry

        lax.fori_loop(0, slots, weigh, 0)
        total_ref[slot, head] = peak_ref[...] + jnp.log(sum_ref[...])
        rows = pl.ds(pl.multiple_of(head * head_width, head_width), head_width)
        turned_ref[slot, rows] = (out_ref[...] / sum_ref[...]).astype(jnp.bfloat16)
        return carry

    lax.fori_loop(0, heads, one_head, 0)
    attended_ref[slot] = turned_ref[slot].astype(jnp.float32).T.astype(jnp.bfloat16)


def rotated(raw, gain, cosine, sine):
    half = raw.shape[-1] // 2
    scale = lax.rsqrt(jnp.mean(raw * raw, axis=-1, keepdims=True) + EPS)
    scaled = raw * scale * gain
    front, back = scaled[:, :half], scaled[:, half:]
    return jnp.concatenate(
        [front * cosine - back * sine, back * cosine + front * sine], axis=1
    )


def rotated_back(grad, raw, gain, cosine, sine):
    half = raw.shape[-1] // 2
    scale = lax.rsqrt(jnp.mean(raw * raw, axis=-1, keepdims=True) + EPS)
    normed = raw * scale
    front, back = grad[:, :half], grad[:, half:]
    grad = jnp.concatenate(
        [front * cosine + back * sine, back * cosine - front * sine], axis=1
    )
    gain_grad = jnp.sum(grad * normed, axis=0, keepdims=True)
    grad = grad * gain
    inner = jnp.mean(grad * normed, axis=-1, keepdims=True)
    return scale * (grad - normed * inner), gain_grad


def forward_kernel(
    shard_ref,
    input_ref,
    upstream_ref,
    qkv_ref,
    weight_ref,
    operator_gain_ref,
    gain_ref,
    query_gain_ref,
    key_gain_ref,
    cosine_ref,
    sine_ref,
    full_ref,
    attended_ref,
    turned_ref,
    total_ref,
    hidden_ref,
    normed_blocks,
    upstream_blocks,
    normed_input_ref,
    raw_ref,
    q_ref,
    k_ref,
    kt_ref,
    v_ref,
    gate_up_grad_ref,
    activation_ref,
    vt_ref,
    normed_ref,
    total_acc,
    scores_ref,
    peak_ref,
    sum_ref,
    out_ref,
    part_ref,
    core_going,
    core_coming,
    ctx_going,
    ctx_coming,
    ring_send,
    ring_recv,
    core_send,
    core_recv,
    ctx_send,
    ctx_recv,
    spread_send,
    spread_recv,
    local_sem,
):
    f32 = jnp.float32
    bf16 = jnp.bfloat16
    size = lax.axis_size("fsdp")
    ctx = lax.axis_size("ctx")
    tensor = lax.axis_size("tensor")
    far = size // 2
    slots, heads, quarter, head_width = q_ref.shape
    kv = k_ref.shape[1]
    rows = shard_ref.shape[0]
    tokens = slots * quarter
    hidden_units = activation_ref.shape[1]
    at, _ = ring_ends()
    greet()
    go, land, finish = gather_ring(shard_ref, full_ref, ring_send, ring_recv)
    go(2)
    keep = pltpu.make_async_copy(
        shard_ref,
        full_ref.at[pl.ds(pl.multiple_of(at(0) * rows, rows), rows)],
        local_sem,
    )
    keep.start()
    work = (scores_ref, peak_ref, sum_ref, out_ref)

    def prepare(slot, carry):
        def norm(block):
            value = input_ref[slot, block].astype(f32)
            scale = lax.rsqrt(jnp.mean(value * value, axis=-1, keepdims=True) + EPS)
            normed_input_ref[slot, block] = (value * scale * operator_gain_ref[...]).astype(bf16)

        add_rows(quarter, 32, norm)
        raw_ref[slot] = jnp.dot(
            normed_input_ref[slot], qkv_ref[...], preferred_element_type=f32
        )
        cosine = cosine_ref[slot]
        sine = sine_ref[slot]
        for head in range(heads):
            raw = raw_ref[slot, :, head * head_width : (head + 1) * head_width]
            q_ref[slot, head] = rotated(raw, query_gain_ref[...], cosine, sine).astype(bf16)
        for head in range(kv):
            start = (heads + head) * head_width
            raw = raw_ref[slot, :, start : start + head_width]
            turned = rotated(raw, key_gain_ref[...], cosine, sine)
            k_ref[slot, head] = turned.astype(bf16)
            kt_ref[slot, head] = turned.T.astype(bf16)
            start = (heads + kv + head) * head_width
            raw = raw_ref[slot, :, start : start + head_width]
            v_ref[slot, head] = raw.astype(bf16)
            vt_ref[slot, head] = raw.T.astype(bf16)
        here = pl.ds(pl.multiple_of(slot * quarter, quarter), quarter)
        for owner in range(size):
            upstream_blocks[owner, here] = upstream_ref[
                slot, :, owner * rows : (owner + 1) * rows
            ]
        return carry

    lax.fori_loop(0, slots, prepare, 0)
    go(1)

    def accumulate(offset, lhs, start, stop, first=False):
        owner = at(offset)
        there = pl.ds(pl.multiple_of(owner * rows, rows), rows)
        for column in range(start, stop):
            columns = slice(column * hidden_units, (column + 1) * hidden_units)

            def add(here, columns=columns):
                value = jnp.dot(
                    lhs[owner, here], full_ref[there, columns], preferred_element_type=f32
                )
                if first:
                    total_acc[here, columns] = value
                else:
                    total_acc[here, columns] += value

            add_rows(tokens, quarter, add)

    def project(slot):
        attend_slot(slot, q_ref, k_ref, vt_ref, attended_ref, turned_ref, total_ref, work)
        return lax.dot_general(
            attended_ref[slot],
            weight_ref[...],
            (((1,), (1,)), ((), ())),
            preferred_element_type=f32,
        )

    sends = []
    by_core = {}
    by_ctx = {}
    for core in range(1, tensor):
        for step in list(range(1, ctx)) + [0]:
            core_going[core - 1, step] = project(core * ctx + step).astype(bf16)
            copy = send(
                core_going.at[core - 1, step],
                core_coming.at[core - 1, step],
                core_send.at[core - 1, step],
                core_recv.at[core - 1, step],
                other("tensor", -core),
            )
            sends.append(copy)
            by_core[core, step] = copy
    for step in list(range(1, ctx)) + [0]:
        part_ref[...] = project(step)
        for core in range(1, tensor):
            by_core[core, step].wait_recv()
            part_ref[...] += core_coming[core - 1, step].astype(f32)
        if step > 0:
            ctx_going[step - 1] = part_ref[...].astype(bf16)
            copy = send(
                ctx_going.at[step - 1],
                ctx_coming.at[step - 1],
                ctx_send.at[step - 1],
                ctx_recv.at[step - 1],
                other("ctx", -step),
            )
            sends.append(copy)
            by_ctx[step] = copy
        if step < 2:
            go(1)
    keep.wait()
    accumulate(0, upstream_blocks, 2, 3, True)
    for step in range(1, ctx):
        by_ctx[step].wait_recv()
        part_ref[...] += ctx_coming[step - 1].astype(f32)

    def norm(block):
        hidden = input_ref[0, block].astype(f32) + part_ref[block]
        hidden_ref[block] = hidden
        scale = lax.rsqrt(jnp.mean(hidden * hidden, axis=-1, keepdims=True) + EPS)
        normed_ref[0, 0, block] = (hidden * scale * gain_ref[...]).astype(bf16)

    add_rows(quarter, 16, norm)
    spread = []
    for step in range(1, ctx):
        copy = send(
            normed_ref.at[0, 0],
            normed_ref.at[0, step],
            spread_send.at[0, step],
            spread_recv.at[0, step],
            other("ctx", step),
        )
        sends.append(copy)
        spread.append(copy)
    handed = []

    def hand_over(step):
        for core in range(1, tensor):
            copy = send(
                normed_ref.at[0, step],
                normed_ref.at[core, step],
                spread_send.at[core, step],
                spread_recv.at[core, step],
                other("tensor", core),
            )
            sends.append(copy)
            handed.append(copy)

    hand_over(0)
    go(1)

    def keep_blocks(slot):
        here = slice(slot * quarter, (slot + 1) * quarter)
        for owner in range(size):
            normed_blocks[owner, here] = normed_ref[
                slot // ctx, slot % ctx, :, owner * rows : (owner + 1) * rows
            ]

    near = max(0, far - 2)
    if far > 3:
        land(near)
        for offset in range(1, near + 1):
            accumulate(offset, upstream_blocks, 2, 3)
            accumulate(-offset, upstream_blocks, 2, 3)
    keep_blocks(0)
    go(1)
    for step in range(1, ctx):
        spread[step - 1].wait_recv()
        hand_over(step)
        keep_blocks(step)
    for core in range(1, tensor):
        for step in range(ctx):
            handed[(core - 1) + step * (tensor - 1)].wait_recv()
            keep_blocks(core * ctx + step)
    accumulate(0, normed_blocks, 0, 2, True)
    if far > 3:
        accumulate(1, normed_blocks, 0, 2)
        accumulate(-1, normed_blocks, 0, 2)
        go(2)
        for offset in range(2, near + 1):
            accumulate(offset, normed_blocks, 0, 2)
            accumulate(-offset, normed_blocks, 0, 2)
    else:
        near = 0
    go(2 * far)
    for offset in range(near + 1, far):
        land(offset)
        accumulate(offset, upstream_blocks, 2, 3)
        accumulate(-offset, upstream_blocks, 2, 3)
        accumulate(offset, normed_blocks, 0, 2)
        accumulate(-offset, normed_blocks, 0, 2)
    land(far)
    accumulate(far, upstream_blocks, 2, 3)
    accumulate(far, normed_blocks, 0, 2)

    def activate(here):
        gate = total_acc[here, :hidden_units]
        upper = total_acc[here, hidden_units : 2 * hidden_units]
        grad = total_acc[here, 2 * hidden_units :]
        sigmoid = 1.0 / (1.0 + jnp.exp(-gate))
        silu = gate * sigmoid
        activation_ref[here] = (silu * upper).astype(bf16)
        slope = sigmoid * (1.0 + gate * (1.0 - sigmoid))
        gate_up_grad_ref[here, :hidden_units] = (grad * upper * slope).astype(bf16)
        gate_up_grad_ref[here, hidden_units:] = (grad * silu).astype(bf16)

    add_rows(tokens, 16, activate)
    finish()
    for copy in sends:
        copy.wait_send()


def forward_gather(shard, inputs, upstream, qkv, weight, gains, cosine, sine):
    size = lax.axis_size("fsdp")
    ctx = lax.axis_size("ctx")
    tensor = lax.axis_size("tensor")
    far = size // 2
    rows, columns = shard.shape
    slots, quarter, width = inputs.shape
    q_cols = weight.shape[1]
    head_width = gains[2].shape[1]
    heads = q_cols // head_width
    kv = (qkv.shape[1] // head_width - heads) // 2
    tokens = slots * quarter
    hidden_units = columns // 3
    in_vmem = pl.BlockSpec(memory_space=pltpu.VMEM)
    dma = pltpu.SemaphoreType.DMA
    bf16 = jnp.bfloat16
    f32 = jnp.float32
    cores = max(1, tensor - 1)
    shape = jax.ShapeDtypeStruct
    return pl.pallas_call(
        forward_kernel,
        out_shape=(
            shape((rows * size, columns), bf16),
            shape((slots, quarter, q_cols), bf16),
            shape((slots, q_cols, quarter), bf16),
            shape((slots, heads, 1, quarter), f32),
            shape((quarter, width), f32),
            shape((size, tokens, rows), bf16),
            shape((size, tokens, rows), bf16),
            shape((slots, quarter, width), bf16),
            shape((slots, quarter, qkv.shape[1]), f32),
            shape((slots, heads, quarter, head_width), bf16),
            shape((slots, kv, quarter, head_width), bf16),
            shape((slots, kv, head_width, quarter), bf16),
            shape((slots, kv, quarter, head_width), bf16),
            shape((tokens, 2 * hidden_units), bf16),
            shape((tokens, hidden_units), bf16),
        ),
        in_specs=[in_vmem] * 11,
        out_specs=(in_vmem,) * 15,
        scratch_shapes=[
            pltpu.VMEM((slots, kv, head_width, quarter), bf16),
            pltpu.VMEM((tensor, ctx, quarter, width), bf16),
            pltpu.VMEM((tokens, columns), f32),
            pltpu.VMEM((slots, quarter, quarter), f32),
            pltpu.VMEM((1, quarter), f32),
            pltpu.VMEM((1, quarter), f32),
            pltpu.VMEM((head_width, quarter), f32),
            pltpu.VMEM((quarter, width), f32),
            pltpu.VMEM((cores, ctx, quarter, width), bf16),
            pltpu.VMEM((cores, ctx, quarter, width), bf16),
            pltpu.VMEM((max(1, ctx - 1), quarter, width), bf16),
            pltpu.VMEM((max(1, ctx - 1), quarter, width), bf16),
            dma((2, far, 2)),
            dma((2, far, 2)),
            dma((cores, ctx)),
            dma((cores, ctx)),
            dma((ctx,)),
            dma((ctx,)),
            dma((tensor, ctx)),
            dma((tensor, ctx)),
            dma(()),
        ],
        compiler_params=pltpu.CompilerParams(
            collective_id=2, has_side_effects=True, vmem_limit_bytes=62 * 1024 * 1024
        ),
        name="forward_gather",
    )(shard, inputs, upstream, qkv, weight, *gains, cosine, sine)


def group_reduce(part_ref, core_coming, ctx_going, ctx_coming, sems, sends):
    f32 = jnp.float32
    ctx = lax.axis_size("ctx")
    tensor = lax.axis_size("tensor")
    quarter = part_ref.shape[1]
    core_send, core_recv, ctx_send, ctx_recv = sems
    by_core = []
    by_ctx = []

    def over_cores():
        for core in range(1, tensor):
            copy = send(
                part_ref.at[pl.ds(core * ctx, ctx)],
                core_coming.at[core - 1],
                core_send.at[core - 1],
                core_recv.at[core - 1],
                other("tensor", -core),
            )
            sends.append(copy)
            by_core.append(copy)

    def over_ctx(sum_ref):
        for copy in by_core:
            copy.wait_recv()
        for step in list(range(1, ctx)) + [0]:

            def add(block, step=step):
                value = part_ref[step, block].astype(f32)
                for core in range(1, tensor):
                    value = value + core_coming[core - 1, step, block].astype(f32)
                if step == 0:
                    sum_ref[block] = value
                else:
                    ctx_going[step - 1, block] = value.astype(jnp.bfloat16)

            add_rows(quarter, 16, add)
            if step > 0:
                copy = send(
                    ctx_going.at[step - 1],
                    ctx_coming.at[step - 1],
                    ctx_send.at[step - 1],
                    ctx_recv.at[step - 1],
                    other("ctx", -step),
                )
                sends.append(copy)
                by_ctx.append(copy)

    def finish():
        for copy in by_ctx:
            copy.wait_recv()

    return over_cores, over_ctx, finish


def attend_slot_grad(slot, refs, turned_grad, accumulators):
    q_ref, k_ref, kt_ref, v_ref, turned_ref, total_ref, dq_ref = refs
    dq_acc, dk_acc, dv_acc = accumulators
    f32 = jnp.float32
    bf16 = jnp.bfloat16
    slots, heads, quarter, head_width = q_ref.shape
    group = heads // k_ref.shape[1]
    scale = 1.0 / head_width**0.5

    def one_head(head, carry):
        kv_head = lax.div(head, group)
        rows = pl.ds(pl.multiple_of(head * head_width, head_width), head_width)
        grad = turned_grad[rows]
        delta = jnp.sum(
            grad.astype(f32) * turned_ref[slot, rows].astype(f32), axis=0, keepdims=True
        )
        dq_acc[...] = jnp.zeros(dq_acc.shape, f32)

        def one_key_slot(key_slot, carry):
            gap, seen = reachable(slot, key_slot, quarter)

            @pl.when(seen)
            def _():
                queries = q_ref[slot, head]
                scores = masked_scores(k_ref[key_slot, kv_head], queries, gap)
                probs = jnp.exp(scores - total_ref[slot, head])
                prob_grad = jnp.dot(v_ref[key_slot, kv_head], grad, preferred_element_type=f32)
                score_grad = (probs * (prob_grad - delta)).astype(bf16)
                dv_acc[key_slot, head] += lax.dot_general(
                    probs.astype(bf16), grad, (((1,), (1,)), ((), ())), preferred_element_type=f32
                )
                dk_acc[key_slot, head] += jnp.dot(score_grad, queries, preferred_element_type=f32)
                dq_acc[...] += jnp.dot(
                    kt_ref[key_slot, kv_head], score_grad, preferred_element_type=f32
                )

            return carry

        lax.fori_loop(0, slots, one_key_slot, 0)
        dq_ref[slot, head] = (dq_acc[...] * scale).astype(bf16)
        return carry

    lax.fori_loop(0, heads, one_head, 0)


def backward_kernel(
    full_ref,
    normed_ref,
    upstream_ref,
    gate_up_ref,
    activation_ref,
    hidden_ref,
    own_upstream_ref,
    gain_ref,
    weight_ref,
    q_ref,
    k_ref,
    kt_ref,
    v_ref,
    turned_ref,
    total_ref,
    attended_ref,
    normed_input_ref,
    raw_ref,
    qkv_ref,
    query_gain_ref,
    key_gain_ref,
    cosine_ref,
    sine_ref,
    share_ref,
    hidden_grad_ref,
    output_ref,
    input_part_ref,
    qkv_grad_ref,
    weight_grad_ref,
    gain_grad_ref,
    all_grad_ref,
    dq_ref,
    raw_grad_ref,
    hidden_part_ref,
    down_part_ref,
    grad_ref,
    coming,
    core_coming,
    ctx_going,
    ctx_coming,
    sum_ref,
    out_sum_ref,
    turned_grad,
    own_output,
    dq_acc,
    dk_acc,
    dv_acc,
    ring_send,
    ring_recv,
    core_send,
    core_recv,
    ctx_send,
    ctx_recv,
    spread_send,
    spread_recv,
    output_send,
    output_recv,
    local_sem,
    full_sem,
):
    f32 = jnp.float32
    bf16 = jnp.bfloat16
    size = lax.axis_size("fsdp")
    ctx = lax.axis_size("ctx")
    tensor = lax.axis_size("tensor")
    me_t = lax.axis_index("tensor")
    far = size // 2
    slots, heads, quarter, head_width = q_ref.shape
    rows = grad_ref.shape[0] // size
    gate_up_cols = gate_up_ref.shape[1]
    hidden_units = activation_ref.shape[1]
    at, _ = ring_ends()
    sends = []
    load = pltpu.make_async_copy(full_ref, grad_ref, full_sem)
    load.start()
    greet()
    reduce_hidden = group_reduce(
        hidden_part_ref,
        core_coming.at[0],
        ctx_going.at[0],
        ctx_coming.at[0],
        (core_send.at[0], core_recv.at[0], ctx_send.at[0], ctx_recv.at[0]),
        sends,
    )
    reduce_down = group_reduce(
        down_part_ref,
        core_coming.at[1],
        ctx_going.at[1],
        ctx_coming.at[1],
        (core_send.at[1], core_recv.at[1], ctx_send.at[1], ctx_recv.at[1]),
        sends,
    )
    go, finish_ring = scatter_ring(grad_ref, share_ref, coming, ring_send, ring_recv)

    def piece(offset):
        here = pl.ds(pl.multiple_of(at(offset) * rows, rows), rows)
        target_ref = grad_ref
        if offset == far:
            here = slice(0, rows)
            target_ref = share_ref
        for start in range(0, gate_up_cols, hidden_units):
            columns = slice(start, start + hidden_units)
            target_ref[here, columns] = lax.dot_general(
                normed_ref[at(offset)],
                gate_up_ref[:, columns],
                (((0,), (0,)), ((), ())),
                preferred_element_type=f32,
            ).astype(bf16)
        target_ref[here, gate_up_cols:] = lax.dot_general(
            upstream_ref[at(offset)],
            activation_ref[...],
            (((0,), (0,)), ((), ())),
            preferred_element_type=f32,
        ).astype(bf16)

    def pieces(offset):
        piece(offset)
        piece(-offset)

    piece(far)
    go(2)
    load.wait()

    def part_of_slot(target_ref, lhs_ref, columns):
        def one(slot, carry):
            here = pl.ds(pl.multiple_of(slot * quarter, quarter), quarter)
            target_ref[slot] = lax.dot_general(
                lhs_ref[here],
                grad_ref[:, columns],
                (((1,), (1,)), ((), ())),
                preferred_element_type=f32,
            ).astype(bf16)
            return carry

        lax.fori_loop(0, slots, one, 0)

    part_of_slot(hidden_part_ref, gate_up_ref, slice(0, gate_up_cols))
    reduce_hidden[0]()
    part_of_slot(down_part_ref, activation_ref, slice(gate_up_cols, None))
    reduce_hidden[1](sum_ref)
    reduce_down[0]()
    ready = 0
    if far > 1:
        pieces(far - 1)
        go(2)
        ready = 1
    dk_acc[...] = jnp.zeros(dk_acc.shape, f32)
    dv_acc[...] = jnp.zeros(dv_acc.shape, f32)
    if far > 2:
        pieces(far - 2)
        ready = 2
    go(2)
    reduce_hidden[2]()

    def norm_back(block):
        grad = sum_ref[block]
        for step in range(1, ctx):
            grad = grad + ctx_coming[0, step - 1, block].astype(f32)
        hidden = hidden_ref[block]
        scale = lax.rsqrt(jnp.mean(hidden * hidden, axis=-1, keepdims=True) + EPS)
        grad = grad * gain_ref[...]
        inner = jnp.mean(grad * hidden, axis=-1, keepdims=True) * (scale * scale)
        grad = own_upstream_ref[block].astype(f32) + scale * (grad - hidden * inner)
        hidden_grad_ref[block] = grad
        all_grad_ref[0, block] = grad.astype(bf16)

    add_rows(quarter, 16, norm_back)
    spread = []
    handed = {}
    for step in range(1, ctx):
        copy = send(
            all_grad_ref.at[0],
            all_grad_ref.at[step],
            spread_send.at[0, step],
            spread_recv.at[0, step],
            other("ctx", step),
        )
        sends.append(copy)
        spread.append(copy)

    def hand_over(step):
        for core in range(1, tensor):
            copy = send(
                all_grad_ref.at[step],
                all_grad_ref.at[core * ctx + step],
                spread_send.at[core, step],
                spread_recv.at[core, step],
                other("tensor", core),
            )
            sends.append(copy)
            handed[core, step] = copy

    hand_over(0)
    reduce_down[1](out_sum_ref)

    def attention_back(slot):
        grad = jnp.dot(all_grad_ref[slot], weight_ref[...], preferred_element_type=f32)
        turned_grad[...] = grad.T.astype(bf16)
        attend_slot_grad(
            slot,
            (q_ref, k_ref, kt_ref, v_ref, turned_ref, total_ref, dq_ref),
            turned_grad,
            (dq_acc, dk_acc, dv_acc),
        )

    if far > 2:
        go(2)
    attention_back(0)
    for core in range(1, tensor):
        handed[core, 0].wait_recv()
        attention_back(core * ctx)
    if far > 2:
        go(2)
    for step in range(1, ctx):
        spread[step - 1].wait_recv()
        hand_over(step)
        attention_back(step)
    for offset in range(far - ready - 1, 0, -1):
        pieces(offset)
    piece(0)
    go(2)
    for step in range(1, ctx):
        for core in range(1, tensor):
            handed[core, step].wait_recv()
            attention_back(core * ctx + step)
    go(2)
    reduce_down[2]()

    def output(block):
        value = hidden_ref[block] + out_sum_ref[block]
        for step in range(1, ctx):
            value = value + ctx_coming[1, step - 1, block].astype(f32)
        own_output[block] = value.astype(bf16)

    add_rows(quarter, 16, output)
    keep = pltpu.make_async_copy(own_output, output_ref.at[me_t], local_sem)
    keep.start()
    given = []
    for core in range(1, tensor):
        copy = send(
            own_output,
            output_ref.at[me_t],
            output_send.at[core],
            output_recv.at[core],
            other("tensor", core),
        )
        sends.append(copy)
        given.append(copy)
    kv = k_ref.shape[1]
    group = heads // kv
    scale = 1.0 / head_width**0.5
    gain_grad_ref[...] = jnp.zeros(gain_grad_ref.shape, f32)

    def rounded(value):
        return value.astype(bf16).astype(f32)

    def heads_back(slot, carry):
        cosine = cosine_ref[slot]
        sine = sine_ref[slot]
        columns = []
        for head in range(heads + kv):
            raw = raw_ref[slot, :, head * head_width : (head + 1) * head_width]
            if head < heads:
                grad = dq_ref[slot, head].astype(f32).T
                gain_ref_here, row = query_gain_ref, 0
            else:
                first = (head - heads) * group
                grad = rounded(dk_acc[slot, first] * scale)
                for member in range(first + 1, first + group):
                    grad = grad + rounded(dk_acc[slot, member] * scale)
                gain_ref_here, row = key_gain_ref, 1
            grad, gain_grad = rotated_back(grad, raw, gain_ref_here[...], cosine, sine)
            gain_grad_ref[row : row + 1] += gain_grad
            columns.append(grad.astype(bf16))
        for head in range(kv):
            grad = rounded(dv_acc[slot, head * group])
            for member in range(head * group + 1, (head + 1) * group):
                grad = grad + rounded(dv_acc[slot, member])
            columns.append(grad.astype(bf16))
        raw_grad_ref[slot] = jnp.concatenate(columns, axis=1)
        input_part_ref[slot] = lax.dot_general(
            raw_grad_ref[slot],
            qkv_ref[...],
            (((1,), (1,)), ((), ())),
            preferred_element_type=f32,
        ).astype(bf16)
        return carry

    lax.fori_loop(0, slots, heads_back, 0)
    wide = rows * max(1, 256 // rows)

    def over_tokens(left_ref, right_ref, columns):
        total = 0.0
        for slot in range(slots):
            total = total + lax.dot_general(
                left_ref[slot, :, columns],
                right_ref[slot],
                (((0,), (0,)), ((), ())),
                preferred_element_type=f32,
            )
        return total.astype(bf16)

    def weights_back(index, carry):
        columns = pl.ds(pl.multiple_of(index * wide, wide), wide)
        qkv_grad_ref[columns] = over_tokens(normed_input_ref, raw_grad_ref, columns)
        weight_grad_ref[columns] = over_tokens(all_grad_ref, attended_ref, columns)
        return carry

    lax.fori_loop(0, grad_ref.shape[0] // wide, weights_back, 0)
    finish_ring(share_ref)
    for copy in given:
        copy.wait_recv()
    for copy in sends:
        copy.wait_send()
    keep.wait()


def backward_scatter(
    full,
    normed_blocks,
    upstream_blocks,
    gate_up_grad,
    activation,
    hidden,
    own_upstream,
    gain,
    weight,
    queries,
    keys,
    keys_turned,
    values,
    attended_turned,
    totals,
    attended,
    normed_input,
    raw,
    qkv,
    query_gain,
    key_gain,
    cosine,
    sine,
):
    size = lax.axis_size("fsdp")
    ctx = lax.axis_size("ctx")
    tensor = lax.axis_size("tensor")
    far = size // 2
    slots, heads, quarter, head_width = queries.shape
    width = weight.shape[0]
    q_cols = weight.shape[1]
    rows = width // size
    columns = gate_up_grad.shape[1] + activation.shape[1]
    in_vmem = pl.BlockSpec(memory_space=pltpu.VMEM)
    dma = pltpu.SemaphoreType.DMA
    bf16 = jnp.bfloat16
    f32 = jnp.float32
    cores = max(1, tensor - 1)
    apart = max(1, ctx - 1)
    by_head = (slots, heads, quarter, head_width)
    return pl.pallas_call(
        backward_kernel,
        out_shape=(
            jax.ShapeDtypeStruct((rows, columns), bf16),
            jax.ShapeDtypeStruct((quarter, width), f32),
            jax.ShapeDtypeStruct((tensor, quarter, width), bf16),
            jax.ShapeDtypeStruct((slots, quarter, width), bf16),
            jax.ShapeDtypeStruct(qkv.shape, bf16),
            jax.ShapeDtypeStruct(weight.shape, bf16),
            jax.ShapeDtypeStruct((2, head_width), f32),
        ),
        in_specs=[pl.BlockSpec(memory_space=pl.ANY)] + [in_vmem] * 22,
        out_specs=(in_vmem,) * 7,
        scratch_shapes=[
            pltpu.VMEM((slots, quarter, width), bf16),
            pltpu.VMEM((slots, heads, head_width, quarter), bf16),
            pltpu.VMEM((slots, quarter, qkv.shape[1]), bf16),
            pltpu.VMEM((slots, quarter, width), bf16),
            pltpu.VMEM((slots, quarter, width), bf16),
            pltpu.VMEM((width, columns), bf16),
            pltpu.VMEM((2, far, 2, rows // 2, columns), bf16),
            pltpu.VMEM((2, cores, ctx, quarter, width), bf16),
            pltpu.VMEM((2, apart, quarter, width), bf16),
            pltpu.VMEM((2, apart, quarter, width), bf16),
            pltpu.VMEM((quarter, width), f32),
            pltpu.VMEM((quarter, width), f32),
            pltpu.VMEM((q_cols, quarter), bf16),
            pltpu.VMEM((quarter, width), bf16),
            pltpu.VMEM((head_width, quarter), f32),
            pltpu.VMEM(by_head, f32),
            pltpu.VMEM(by_head, f32),
            dma((2, far, 2)),
            dma((2, far, 2)),
            dma((2, cores)),
            dma((2, cores)),
            dma((2, ctx)),
            dma((2, ctx)),
            dma((tensor, ctx)),
            dma((tensor, ctx)),
            dma((tensor,)),
            dma((tensor,)),
            dma(()),
            dma(()),
        ],
        compiler_params=pltpu.CompilerParams(
            collective_id=3, has_side_effects=True, vmem_limit_bytes=63 * 1024 * 1024
        ),
        name="backward_scatter",
    )(
        full,
        normed_blocks,
        upstream_blocks,
        gate_up_grad,
        activation,
        hidden,
        own_upstream,
        gain,
        weight,
        queries,
        keys,
        keys_turned,
        values,
        attended_turned,
        totals,
        attended,
        normed_input,
        raw,
        qkv,
        query_gain,
        key_gain,
        cosine,
        sine,
    )


def part_of(array, dim, count, start):
    return lax.dynamic_slice_in_dim(array, start, count, dim)


def shards(
    block_input,
    operator_gain,
    query_weight,
    key_weight,
    value_weight,
    output_weight,
    feedforward_gain,
    gate_weight,
    up_weight,
    down_weight,
    query_gain,
    key_gain,
    cotangent,
):
    bf16 = jnp.bfloat16
    f32 = jnp.float32
    fsdp = lax.axis_size("fsdp")
    ctx = lax.axis_size("ctx")
    tensor = lax.axis_size("tensor")
    me_c = lax.axis_index("ctx")
    me_t = lax.axis_index("tensor")
    seqs, tok_here, width = block_input.shape
    quarter = tok_here // tensor
    tokens = tok_here * ctx
    rows = seqs * tokens
    gain_rows = query_gain.shape[0]
    head_width = gain_rows * fsdp
    heads_shard = query_weight.shape[1] // head_width
    kv_shard = key_weight.shape[1] // head_width
    spread = heads_shard // kv_shard
    heads = heads_shard // ctx
    kv = max(1, kv_shard // ctx)
    group = heads // kv
    copies = max(1, ctx // kv_shard)
    q_cols = heads * head_width
    kv_cols = kv * head_width
    kv_start = ((me_c * heads) // spread) * head_width
    hidden_units = gate_weight.shape[1] // ctx
    shard_rows = query_weight.shape[0]

    gains = jnp.stack(
        [
            operator_gain,
            feedforward_gain,
            jnp.pad(query_gain, (0, shard_rows - gain_rows)),
            jnp.pad(key_gain, (0, shard_rows - gain_rows)),
        ],
        axis=1,
    )
    attention_pack = jnp.concatenate(
        [
            part_of(query_weight, 1, q_cols, me_c * q_cols),
            part_of(key_weight, 1, kv_cols, kv_start),
            part_of(value_weight, 1, kv_cols, kv_start),
            part_of(output_weight, 0, q_cols, me_c * q_cols).T,
            jnp.pad(gains, ((0, 0), (0, 124))),
        ],
        axis=1,
    )
    feedforward_shard = jnp.concatenate(
        [
            part_of(gate_weight, 1, hidden_units, me_c * hidden_units),
            part_of(up_weight, 1, hidden_units, me_c * hidden_units),
            part_of(down_weight, 0, hidden_units, me_c * hidden_units).T,
        ],
        axis=1,
    )
    attention_full, all_input, upstream = start_gather(attention_pack, block_input, cotangent)
    all_input = all_input.reshape(rows, width)
    upstream = upstream.reshape(rows, width)
    qkv_cols = q_cols + 2 * kv_cols
    qkv_full = attention_full[:, :qkv_cols]
    output_full = attention_full[:, qkv_cols : qkv_cols + q_cols]
    gains_full = attention_full[:, qkv_cols + q_cols :].astype(f32)
    operator_scale = gains_full[:, 0]
    feedforward_scale = gains_full[:, 1]
    query_scale = gains_full[:, 2].reshape(fsdp, shard_rows)[:, :gain_rows].reshape(-1)
    key_scale = gains_full[:, 3].reshape(fsdp, shard_rows)[:, :gain_rows].reshape(-1)

    own_input = part_of(block_input, 1, quarter, me_t * quarter)
    upstream_own = part_of(cotangent, 1, quarter, me_t * quarter)

    ctx_order = lax.rem(me_c - jnp.arange(ctx) + ctx, ctx)
    tensor_order = lax.rem(me_t - jnp.arange(tensor) + tensor, tensor)
    positions = (
        tensor_order[:, None, None] * quarter
        + ctx_order[None, :, None] * tok_here
        + jnp.arange(quarter)[None, None, :]
    ).reshape(tokens)
    cosine, sine = rotary_tables(positions, head_width)

    slots = tensor * ctx
    own_f32 = own_input.astype(f32)
    (
        feedforward_full,
        attended,
        attended_turned,
        totals,
        hidden,
        normed_blocks,
        upstream_blocks,
        normed_input,
        qkv_raw,
        queries,
        keys,
        keys_turned,
        values,
        gate_up_grad,
        activation,
    ) = forward_gather(
        feedforward_shard,
        all_input.reshape(slots, quarter, width),
        upstream.reshape(slots, quarter, width),
        qkv_full,
        output_full,
        (
            operator_scale[None],
            feedforward_scale[None],
            query_scale[None],
            key_scale[None],
        ),
        cosine.reshape(slots, quarter, -1),
        sine.reshape(slots, quarter, -1),
    )
    (
        feedforward_share,
        hidden_grad,
        block_output,
        input_part,
        qkv_weight_grad,
        output_weight_grad,
        head_gain_grads,
    ) = backward_scatter(
        feedforward_full,
        normed_blocks,
        upstream_blocks,
        gate_up_grad,
        activation,
        hidden,
        upstream_own.reshape(quarter, width),
        feedforward_scale.reshape(1, width),
        output_full,
        queries,
        keys,
        keys_turned,
        values,
        attended_turned,
        totals,
        attended,
        normed_input,
        qkv_raw,
        qkv_full,
        query_scale[None],
        key_scale[None],
        cosine.reshape(slots, quarter, -1),
        sine.reshape(slots, quarter, -1),
    )
    hidden_grad = hidden_grad[None]
    block_output = block_output.reshape(seqs, tok_here, width)
    input_part = input_part.reshape(tensor, ctx, quarter, width)
    gain_grads = head_gain_grads.T.reshape(fsdp, gain_rows, 2)
    gain_grads = jnp.pad(
        gain_grads, ((0, 0), (0, shard_rows - gain_rows), (0, 126))
    ).reshape(width, 128).astype(bf16)
    attention_grad = jnp.concatenate(
        [qkv_weight_grad, output_weight_grad, gain_grads], axis=1
    )
    feedforward_parts = in_order(feedforward_share[None], "ctx", 0)
    attention_grad, feedforward_parts = lax.optimization_barrier(
        (attention_grad, feedforward_parts)
    )
    attention_parts, normed_input_grad = finish_sums(attention_grad, input_part)
    attention_parts = attention_parts.astype(f32)
    normed_input_grad = normed_input_grad[None]
    _, norm_one_back = jax.vjp(lambda v: rms_scale(v, operator_scale), own_f32)
    (input_norm_grad,) = norm_one_back(normed_input_grad)
    input_grad = in_order(hidden_grad + input_norm_grad, "tensor", 1)

    def columns(parts):
        return jnp.concatenate([parts[step] for step in range(ctx)], axis=1)

    def head_columns(parts):
        every = columns(parts)
        if copies == 1:
            return every
        return every.reshape(shard_rows, kv_shard, copies, head_width).sum(axis=2).reshape(
            shard_rows, -1
        )

    query_weight_grad = columns(attention_parts[:, :, :q_cols])
    key_weight_grad = head_columns(attention_parts[:, :, q_cols : q_cols + kv_cols])
    value_weight_grad = head_columns(attention_parts[:, :, q_cols + kv_cols : qkv_cols])
    gate_weight_grad = columns(feedforward_parts[:, :, :hidden_units].astype(f32))
    up_weight_grad = columns(
        feedforward_parts[:, :, hidden_units : 2 * hidden_units].astype(f32)
    )
    down_weight_grad = jnp.swapaxes(feedforward_parts[:, :, 2 * hidden_units :], 1, 2)
    down_weight_grad = down_weight_grad.astype(f32).reshape(-1, shard_rows)
    gain_parts = attention_parts[:, :, qkv_cols + q_cols : qkv_cols + q_cols + 2].sum(axis=0)

    def gain_part(pairs, gain):
        total = 0.0
        for weight, grad in pairs:
            total = total + jnp.sum(weight.astype(f32) * grad, axis=1)
        return total / gain.astype(f32)

    gain_columns = jnp.concatenate(
        [
            gain_part(
                [
                    (query_weight, query_weight_grad),
                    (key_weight, key_weight_grad),
                    (value_weight, value_weight_grad),
                ],
                operator_gain,
            )[:, None],
            gain_part(
                [(gate_weight, gate_weight_grad), (up_weight, up_weight_grad)], feedforward_gain
            )[:, None],
            gain_parts,
        ],
        axis=1,
    )
    gain_totals = gain_columns
    for step in range(1, tensor):
        gain_totals = gain_totals + shift(gain_columns, "tensor", step)

    return (
        block_output,
        input_grad,
        gain_totals[:, 0],
        query_weight_grad,
        key_weight_grad,
        value_weight_grad,
        jnp.swapaxes(attention_parts[:, :, qkv_cols : qkv_cols + q_cols], 1, 2).reshape(
            -1, shard_rows
        ),
        gain_totals[:, 1],
        gate_weight_grad,
        up_weight_grad,
        down_weight_grad,
        gain_totals[:gain_rows, 2],
        gain_totals[:gain_rows, 3],
    )


def solution(mesh):
    in_specs = (
        P("fsdp", "ctx", None),
        P("fsdp"),
        P("fsdp", "tensor"),
        P("fsdp", "tensor"),
        P("fsdp", "tensor"),
        P("tensor", "fsdp"),
        P("fsdp"),
        P("fsdp", "tensor"),
        P("fsdp", "tensor"),
        P("tensor", "fsdp"),
        P("fsdp"),
        P("fsdp"),
        P("fsdp", "ctx", None),
    )
    out_specs = (
        P("fsdp", "ctx", None),
        P("fsdp", "ctx", None),
        P("fsdp"),
        P("fsdp", "tensor"),
        P("fsdp", "tensor"),
        P("fsdp", "tensor"),
        P("tensor", "fsdp"),
        P("fsdp"),
        P("fsdp", "tensor"),
        P("fsdp", "tensor"),
        P("tensor", "fsdp"),
        P("fsdp"),
        P("fsdp"),
    )
    return jax.shard_map(shards, mesh=mesh, in_specs=in_specs, out_specs=out_specs, check_vma=False)
```

```python
import jax
import jax.numpy as jnp
from jax import lax
from jax.experimental import pallas as pl
from jax.experimental.pallas import tpu as pltpu
from jax.sharding import PartitionSpec as P

EPS = 1e-05
THETA = 1000000.0


def rms_scale(values_in, gain):
    return (
        values_in * lax.rsqrt(jnp.mean(values_in * values_in, axis=-1, keepdims=True) + EPS) * gain
    )


def rotary_tables(positions, head_width):
    half_width = head_width // 2
    freqs = THETA ** (-jnp.arange(half_width).astype(jnp.float32) * 2.0 / head_width)
    angles = positions.astype(jnp.float32)[:, None] * freqs[None, :]
    return (jnp.cos(angles), jnp.sin(angles))


def rotate_halves(heads_in, cosine, sine):
    half_width = heads_in.shape[-1] // 2
    front_half = heads_in[..., :half_width]
    back_half = heads_in[..., half_width:]
    cos_rows = cosine[:, None, :]
    sin_rows = sine[:, None, :]
    return jnp.concatenate(
        [
            front_half * cos_rows - back_half * sin_rows,
            back_half * cos_rows + front_half * sin_rows,
        ],
        axis=-1,
    )


def head_prepare(raw, gain, cosine, sine):
    head_width = gain.shape[0]
    shaped = raw.reshape(raw.shape[:-1] + (raw.shape[-1] // head_width, head_width))
    return rotate_halves(rms_scale(shaped, gain), cosine, sine)


def swiglu(gate, upper):
    return jax.nn.silu(gate) * upper


def contract(left, right, left_dim, right_dim):
    return lax.dot_general(
        left, right, (((left_dim,), (right_dim,)), ((), ())), preferred_element_type=jnp.float32
    )


def block_scores(query_block, keys, query_pos, key_pos):
    scale = 1.0 / query_block.shape[-1] ** 0.5
    scores = (
        jnp.einsum("qhd,khd->hqk", query_block, keys, preferred_element_type=jnp.float32) * scale
    )
    allowed = key_pos[None, :] <= query_pos[:, None]
    return jnp.where(allowed[None, :, :], scores, -1e30)


def attend(queries, keys, values, positions):
    length = queries.shape[0]
    block_rows = min(512, length)
    outputs = []
    totals = []
    for start in range(0, length, block_rows):
        rows = slice(start, start + block_rows)
        scores = block_scores(queries[rows], keys, positions[rows], positions)
        peak = jnp.max(scores, axis=-1, keepdims=True)
        log_total = peak + jnp.log(jnp.sum(jnp.exp(scores - peak), axis=-1, keepdims=True))
        probs = jnp.exp(scores - log_total).astype(jnp.bfloat16)
        block_out = jnp.einsum("hqk,khd->qhd", probs, values, preferred_element_type=jnp.float32)
        outputs.append(block_out.astype(jnp.bfloat16))
        totals.append(log_total[..., 0])
    return (jnp.concatenate(outputs, axis=0), jnp.concatenate(totals, axis=1))


def attend_grad(queries, keys, values, outputs, totals, out_grad, positions):
    length = queries.shape[0]
    block_rows = min(512, length)
    scale = 1.0 / queries.shape[-1] ** 0.5
    key_acc = jnp.zeros(keys.shape, jnp.float32)
    value_acc = jnp.zeros(values.shape, jnp.float32)
    query_parts = []
    for start in range(0, length, block_rows):
        rows = slice(start, start + block_rows)
        query_block = queries[rows]
        scores = block_scores(query_block, keys, positions[rows], positions)
        probs = jnp.exp(scores - totals[:, rows][..., None])
        grad_block = out_grad[rows]
        value_acc = value_acc + jnp.einsum(
            "hqk,qhd->khd",
            probs.astype(jnp.bfloat16),
            grad_block,
            preferred_element_type=jnp.float32,
        )
        prob_grad = jnp.einsum(
            "qhd,khd->hqk", grad_block, values, preferred_element_type=jnp.float32
        )
        delta = jnp.sum(
            grad_block.astype(jnp.float32) * outputs[rows].astype(jnp.float32),
            axis=-1,
        ).T
        score_grad = (probs * (prob_grad - delta[..., None])).astype(jnp.bfloat16)
        query_parts.append(
            (
                jnp.einsum("hqk,khd->qhd", score_grad, keys, preferred_element_type=jnp.float32)
                * scale
            ).astype(jnp.bfloat16)
        )
        key_acc = (
            key_acc
            + jnp.einsum(
                "hqk,qhd->khd", score_grad, query_block, preferred_element_type=jnp.float32
            )
            * scale
        )
    return (
        jnp.concatenate(query_parts, axis=0),
        key_acc.astype(jnp.bfloat16),
        value_acc.astype(jnp.bfloat16),
    )


def shift(array, axis_name, step):
    size = lax.axis_size(axis_name)
    return lax.ppermute(array, axis_name, [(i, (i + step) % size) for i in range(size)])


def around(array, axis_name, dim):
    size = lax.axis_size(axis_name)
    return jnp.concatenate(
        [array] + [shift(array, axis_name, step) for step in range(1, size)], axis=dim
    )


def group_rows(array):
    return around(around(array, "ctx", 1), "tensor", 1)


def sum_around(array, axis_name):
    size = lax.axis_size(axis_name)
    part = array.shape[1] // size
    total = array[:, :part].astype(jnp.float32)
    for step in range(1, size):
        piece = array[:, step * part : (step + 1) * part].astype(jnp.bfloat16)
        total = total + shift(piece, axis_name, -step).astype(jnp.float32)
    return total


def group_sum(array):
    return sum_around(sum_around(array, "tensor"), "ctx")


def in_order(array, axis_name, dim):
    size = lax.axis_size(axis_name)
    me = lax.axis_index(axis_name)
    width = array.shape[dim]
    shape = list(array.shape)
    shape[dim] = width * size
    out = jnp.zeros(shape, array.dtype)
    for step in range(size):
        piece = array if step == 0 else shift(array, axis_name, step)
        owner = lax.rem(me - step + size, size)
        out = lax.dynamic_update_slice_in_dim(out, piece, owner * width, dim)
    return out


def ring_index(place, size):
    if size % 2:
        return place
    turn = size // 2
    return jnp.where(place < turn, 2 * place, 2 * (size - 1 - place) + 1)


def ring_place(index, size):
    if size % 2:
        return index
    return jnp.where(lax.rem(index, 2) == 0, lax.div(index, 2), size - 1 - lax.div(index, 2))


def ring_order(size):
    if size % 2:
        return list(range(size))
    return [2 * i for i in range(size // 2)] + [2 * i + 1 for i in reversed(range(size // 2))]


def ring_shift(array, axis_name, step):
    size = lax.axis_size(axis_name)
    order = ring_order(size)
    pairs = [(order[i], order[(i + step) % size]) for i in range(size)]
    return lax.ppermute(array, axis_name, pairs)


def ring_gather(shard, axis_name, dim=0):
    size = lax.axis_size(axis_name)
    place = ring_place(lax.axis_index(axis_name), size)
    shape = list(shard.shape)
    shape[dim] *= size
    half = shard.shape[0] // 2
    out = jnp.zeros(shape, shard.dtype)

    def put(out, piece, at, offset):
        owner = ring_index(lax.rem(at + size, size), size)
        starts = [offset, 0]
        starts[dim] += owner * shard.shape[dim]
        return lax.dynamic_update_slice(out, piece, starts)

    out = put(out, shard, place, 0)
    rightward = leftward = shard
    for step in range(1, (size + 1) // 2):
        rightward = ring_shift(rightward, axis_name, 1)
        leftward = ring_shift(leftward, axis_name, -1)
        out = put(out, rightward, place - step, 0)
        out = put(out, leftward, place + step, 0)
    if size % 2 == 0:
        rightward = ring_shift(rightward[:half], axis_name, 1)
        leftward = ring_shift(leftward[half:], axis_name, -1)
        out = put(out, rightward, place + size // 2, 0)
        out = put(out, leftward, place + size // 2, half)
    return out, rightward


def ring_scatter(piece_for, axis_name):
    size = lax.axis_size(axis_name)
    place = ring_place(lax.axis_index(axis_name), size)

    def piece(offset):
        return piece_for(ring_index(lax.rem(place + offset + size, size), size))

    mine = piece(0).astype(jnp.float32)
    if size == 1:
        return mine
    half = mine.shape[0] // 2
    far = size // 2
    bf16 = jnp.bfloat16
    f32 = jnp.float32
    if size % 2 == 0:
        across = piece(far)
        rightward = ring_shift(across[:half].astype(bf16), axis_name, 1).astype(f32)
        leftward = ring_shift(across[half:].astype(bf16), axis_name, -1).astype(f32)
        zero = jnp.zeros_like(mine[:half])
        rightward = jnp.concatenate([rightward, zero], axis=0)
        leftward = jnp.concatenate([zero, leftward], axis=0)
        steps = far - 1
    else:
        rightward = leftward = jnp.zeros_like(mine)
        steps = far
    for step in range(steps, 0, -1):
        rightward = ring_shift((rightward + piece(step)).astype(bf16), axis_name, 1).astype(f32)
        leftward = ring_shift((leftward + piece(-step)).astype(bf16), axis_name, -1).astype(f32)
    return mine + rightward + leftward


def other(axis_name, step):
    size = lax.axis_size(axis_name)
    return {axis_name: lax.rem(lax.axis_index(axis_name) + step + size, size)}


def send(source, target, send_sem, recv_sem, device):
    copy = pltpu.make_async_remote_copy(
        src_ref=source,
        dst_ref=target,
        send_sem=send_sem,
        recv_sem=recv_sem,
        device_id=device,
        device_id_type=pl.DeviceIdType.MESH,
    )
    copy.start()
    return copy


def ring_ends():
    size = lax.axis_size("fsdp")
    place = ring_place(lax.axis_index("fsdp"), size)

    def at(offset):
        return ring_index(lax.rem(place + offset + size, size), size)

    return at, ({"fsdp": at(1)}, {"fsdp": at(-1)})


def greet():
    _, ends = ring_ends()
    partners = list(ends)
    for axis_name in ("ctx", "tensor"):
        partners += [other(axis_name, step) for step in range(1, lax.axis_size(axis_name))]
    barrier = pltpu.get_barrier_semaphore()
    for device in partners:
        pl.semaphore_signal(
            barrier, inc=1, device_id=device, device_id_type=pl.DeviceIdType.MESH
        )
    pl.semaphore_wait(barrier, len(partners))


def start_kernel(
    pack_ref,
    input_ref,
    upstream_ref,
    full_ref,
    all_input_ref,
    all_upstream_ref,
    ring_send,
    ring_recv,
    ctx_send,
    ctx_recv,
    tensor_send,
    tensor_recv,
    local_sem,
):
    size = lax.axis_size("fsdp")
    ctx = lax.axis_size("ctx")
    tensor = lax.axis_size("tensor")
    me_t = lax.axis_index("tensor")
    far = size // 2
    rows = pack_ref.shape[0]
    sub_rows = rows // 2
    quarter = all_input_ref.shape[2]
    at, ends = ring_ends()
    greet()
    pairs = ((input_ref, all_input_ref), (upstream_ref, all_upstream_ref))

    def block(owner, sub):
        start = pl.multiple_of(owner * rows + sub * sub_rows, sub_rows)
        return full_ref.at[pl.ds(start, sub_rows)]

    sends = []
    arrivals = {}

    def ring_step(step):
        for sub in range(2):
            for way in range(2):
                if step == far and sub != way:
                    continue
                if step > 1:
                    arrivals.pop((way, step - 1, sub)).wait_recv()
                owner = at((1 - step) if way == 0 else (step - 1))
                source = (
                    pack_ref.at[pl.ds(sub * sub_rows, sub_rows)] if step == 1 else block(owner, sub)
                )
                copy = send(
                    source,
                    block(owner, sub),
                    ring_send.at[way, step - 1, sub],
                    ring_recv.at[way, step - 1, sub],
                    ends[way],
                )
                sends.append(copy)
                arrivals[way, step, sub] = copy

    def own_rows(source, step):
        quarter_at = lax.rem(me_t - step + tensor, tensor)
        return source.at[0, pl.ds(pl.multiple_of(quarter_at * quarter, quarter), quarter)]

    ring_step(1)
    crossed = {}
    locals_ = []
    for which, (source, target) in enumerate(pairs):
        for step in range(1, ctx):
            copy = send(
                own_rows(source, 0),
                target.at[0, step],
                ctx_send.at[which, step - 1],
                ctx_recv.at[which, step - 1],
                other("ctx", step),
            )
            sends.append(copy)
            crossed[which, step] = copy
    for which, (source, target) in enumerate(pairs):
        for step in range(tensor):
            copy = pltpu.make_async_copy(
                own_rows(source, step), target.at[step, 0], local_sem.at[which, step]
            )
            copy.start()
            locals_.append(copy)
    own_copy = pltpu.make_async_copy(
        pack_ref,
        full_ref.at[pl.ds(pl.multiple_of(at(0) * rows, rows), rows)],
        local_sem.at[2, 0],
    )
    own_copy.start()
    locals_.append(own_copy)
    handed = []

    def hand_over(which):
        _, target = pairs[which]
        for step in range(1, ctx):
            crossed[which, step].wait_recv()
            for core in range(1, tensor):
                copy = send(
                    target.at[0, step],
                    target.at[core, step],
                    tensor_send.at[which, core - 1, step - 1],
                    tensor_recv.at[which, core - 1, step - 1],
                    other("tensor", core),
                )
                sends.append(copy)
                handed.append(copy)

    for step in range(2, far + 1):
        if step == far:
            hand_over(0)
        ring_step(step)
    if far < 2:
        hand_over(0)
    hand_over(1)
    for copy in arrivals.values():
        copy.wait_recv()
    for copy in handed:
        copy.wait_recv()
    for copy in sends:
        copy.wait_send()
    for copy in locals_:
        copy.wait()


def start_gather(pack, block_input, cotangent):
    size = lax.axis_size("fsdp")
    ctx = lax.axis_size("ctx")
    tensor = lax.axis_size("tensor")
    far = size // 2
    rows, columns = pack.shape
    _, tok_here, width = block_input.shape
    every = (tensor, ctx, tok_here // tensor, width)
    in_vmem = pl.BlockSpec(memory_space=pltpu.VMEM)
    dma = pltpu.SemaphoreType.DMA
    return pl.pallas_call(
        start_kernel,
        out_shape=(
            jax.ShapeDtypeStruct((rows * size, columns), pack.dtype),
            jax.ShapeDtypeStruct(every, block_input.dtype),
            jax.ShapeDtypeStruct(every, cotangent.dtype),
        ),
        in_specs=[in_vmem] * 3,
        out_specs=(in_vmem,) * 3,
        scratch_shapes=[
            dma((2, far, 2)),
            dma((2, far, 2)),
            dma((2, ctx)),
            dma((2, ctx)),
            dma((2, tensor, ctx)),
            dma((2, tensor, ctx)),
            dma((3, tensor)),
        ],
        compiler_params=pltpu.CompilerParams(
            collective_id=0, has_side_effects=True, vmem_limit_bytes=32 * 1024 * 1024
        ),
        name="start_gather",
    )(pack, block_input, cotangent)


def add_rows(count, block_rows, body):
    def step(index, carry):
        body(pl.ds(pl.multiple_of(index * block_rows, block_rows), block_rows))
        return carry

    lax.fori_loop(0, count // block_rows, step, 0)


def finish_kernel(
    grad_ref,
    wide_ref,
    sum_ref,
    going_in,
    hidden_grad_ref,
    own_ref,
    gain_ref,
    parts_ref,
    wide_parts_ref,
    input_grad_ref,
    going,
    coming,
    share,
    own_grad,
    coming_in,
    ring_send,
    ring_recv,
    in_send,
    in_recv,
    wide_send,
    wide_recv,
    share_send,
    share_recv,
    core_send,
    core_recv,
    local_sem,
):
    f32 = jnp.float32
    bf16 = jnp.bfloat16
    size = lax.axis_size("fsdp")
    ctx = lax.axis_size("ctx")
    tensor = lax.axis_size("tensor")
    me_c = lax.axis_index("ctx")
    me_t = lax.axis_index("tensor")
    far = size // 2
    rows = share.shape[0]
    sub_rows = rows // 2
    quarter = own_ref.shape[0]
    at, ends = ring_ends()
    greet()
    sends = []
    arrivals = {}

    def own_block(owner, sub):
        return pl.ds(pl.multiple_of(owner * rows + sub * sub_rows, sub_rows), sub_rows)

    def ring_step(step):
        for sub in range(2):
            for way in range(2):
                if step == 1 and sub != way:
                    continue
                ahead = far + 1 - step
                owner = at(ahead if way == 0 else -ahead)
                mine = own_block(owner, sub)
                if step == 1:
                    source = grad_ref.at[mine]
                else:
                    source = going.at[way, step - 2, sub]
                    if (way, step - 1, sub) in arrivals:
                        arrivals.pop((way, step - 1, sub)).wait_recv()
                        source[...] = (
                            grad_ref[mine, :].astype(f32)
                            + coming[way, step - 2, sub].astype(f32)
                        ).astype(bf16)
                    else:
                        source = grad_ref.at[mine]
                copy = send(
                    source,
                    coming.at[way, step - 1, sub],
                    ring_send.at[way, step - 1, sub],
                    ring_recv.at[way, step - 1, sub],
                    ends[way],
                )
                sends.append(copy)
                arrivals[way, step, sub] = copy

    ring_step(1)
    shared = []
    locals_ = []

    def keep(index, source, target):
        copy = pltpu.make_async_copy(source, target, local_sem.at[index])
        copy.start()
        locals_.append(copy)

    landing = []
    for step in range(1, ctx):
        copy = send(
            going_in.at[step - 1],
            coming_in.at[step - 1],
            in_send.at[step - 1],
            in_recv.at[step - 1],
            other("ctx", -step),
        )
        sends.append(copy)
        landing.append(copy)
    for step in range(1, ctx):
        copy = send(
            wide_ref,
            wide_parts_ref.at[me_c],
            wide_send.at[step - 1],
            wide_recv.at[step - 1],
            other("ctx", step),
        )
        sends.append(copy)
        shared.append(copy)
    keep(0, wide_ref, wide_parts_ref.at[me_c])

    def norm_back(block):
        value = own_ref[block].astype(f32)
        scale = lax.rsqrt(jnp.mean(value * value, axis=-1, keepdims=True) + EPS)
        grad = sum_ref[block]
        for step in range(1, ctx):
            grad = grad + coming_in[step - 1, block].astype(f32)
        grad = grad * gain_ref[...]
        inner = jnp.mean(grad * value, axis=-1, keepdims=True) * (scale * scale)
        own_grad[block] = hidden_grad_ref[block] + scale * (grad - value * inner)

    for step in range(2, far):
        ring_step(step)
    for copy in landing:
        copy.wait_recv()
    add_rows(quarter, 16, norm_back)
    for core in range(1, tensor):
        copy = send(
            own_grad,
            input_grad_ref.at[me_t],
            core_send.at[core],
            core_recv.at[core],
            other("tensor", core),
        )
        sends.append(copy)
        shared.append(copy)
    keep(1, own_grad, input_grad_ref.at[me_t])
    if far > 1:
        ring_step(far)
    mine = at(0)
    for sub in range(2):
        value = grad_ref[own_block(mine, sub), :].astype(f32)
        for way in range(2):
            if (way, far, sub) in arrivals:
                arrivals.pop((way, far, sub)).wait_recv()
                value = value + coming[way, far - 1, sub].astype(f32)
        share[sub * sub_rows : (sub + 1) * sub_rows, :] = value.astype(bf16)
    for step in range(1, ctx):
        copy = send(
            share,
            parts_ref.at[me_c],
            share_send.at[step - 1],
            share_recv.at[step - 1],
            other("ctx", step),
        )
        sends.append(copy)
        shared.append(copy)
    keep(2, share, parts_ref.at[me_c])
    for copy in shared:
        copy.wait_recv()
    for copy in sends:
        copy.wait_send()
    for copy in locals_:
        copy.wait()


def finish_sums(grad, wide, summed, going_in, hidden_grad, own, gain):
    size = lax.axis_size("fsdp")
    ctx = lax.axis_size("ctx")
    tensor = lax.axis_size("tensor")
    quarter, width = own.shape
    far = size // 2
    rows, columns = grad.shape[0] // size, grad.shape[1]
    in_vmem = pl.BlockSpec(memory_space=pltpu.VMEM)
    dma = pltpu.SemaphoreType.DMA
    bf16 = jnp.bfloat16
    f32 = jnp.float32
    return pl.pallas_call(
        finish_kernel,
        out_shape=(
            jax.ShapeDtypeStruct((ctx, rows, columns), bf16),
            jax.ShapeDtypeStruct((ctx,) + wide.shape, bf16),
            jax.ShapeDtypeStruct((tensor, quarter, width), f32),
        ),
        in_specs=[in_vmem] * 7,
        out_specs=(in_vmem,) * 3,
        scratch_shapes=[
            pltpu.VMEM((2, max(1, far - 1), 2, rows // 2, columns), bf16),
            pltpu.VMEM((2, far, 2, rows // 2, columns), bf16),
            pltpu.VMEM((rows, columns), bf16),
            pltpu.VMEM((quarter, width), f32),
            pltpu.VMEM(going_in.shape, bf16),
            dma((2, far, 2)),
            dma((2, far, 2)),
            dma((ctx,)),
            dma((ctx,)),
            dma((ctx,)),
            dma((ctx,)),
            dma((ctx,)),
            dma((ctx,)),
            dma((tensor,)),
            dma((tensor,)),
            dma((3,)),
        ],
        compiler_params=pltpu.CompilerParams(
            collective_id=1, has_side_effects=True, vmem_limit_bytes=48 * 1024 * 1024
        ),
        name="finish_sums",
    )(grad, wide, summed, going_in, hidden_grad, own, gain)


def gather_ring(shard_ref, full_ref, send_sem, recv_sem):
    size = lax.axis_size("fsdp")
    far = size // 2
    rows = shard_ref.shape[0]
    sub_rows = rows // 2
    at, ends = ring_ends()
    sends = []
    arrivals = {}
    queue = [(step, sub) for step in range(1, far + 1) for sub in range(2)]

    def block(owner, sub):
        start = pl.multiple_of(owner * rows + sub * sub_rows, sub_rows)
        return full_ref.at[pl.ds(start, sub_rows)]

    def go(count):
        for _ in range(min(count, len(queue))):
            step, sub = queue.pop(0)
            for way in range(2):
                if (way, step - 1, sub) in arrivals and (step < far or sub == way):
                    arrivals.pop((way, step - 1, sub)).wait_recv()
                if step == far and sub != way:
                    continue
                owner = at((1 - step) if way == 0 else (step - 1))
                source = (
                    shard_ref.at[pl.ds(sub * sub_rows, sub_rows)] if step == 1 else block(owner, sub)
                )
                copy = send(
                    source,
                    block(owner, sub),
                    send_sem.at[way, step - 1, sub],
                    recv_sem.at[way, step - 1, sub],
                    ends[way],
                )
                sends.append(copy)
                arrivals[way, step, sub] = copy

    def land(step):
        while len(queue) > 0 and queue[0][0] <= step:
            go(1)
        for key in [key for key in arrivals if key[1] <= step]:
            arrivals.pop(key).wait_recv()

    def finish():
        go(len(queue))
        land(far)
        for copy in sends:
            copy.wait_send()

    return go, land, finish


def scatter_ring(grad_ref, first_ref, coming, send_sem, recv_sem):
    f32 = jnp.float32
    size = lax.axis_size("fsdp")
    far = size // 2
    rows = grad_ref.shape[0] // size
    sub_rows = rows // 2
    step_rows = 16
    at, ends = ring_ends()
    sends = []
    arrivals = {}
    queue = [(1, 0, 0), (1, 1, 1)]
    for step in range(2, far + 1):
        queue += [(step, 1, 0), (step, 0, 1), (step, 0, 0), (step, 1, 1)]

    def start_of(owner, sub):
        return pl.multiple_of(owner * rows + sub * sub_rows, sub_rows)

    def go(count):
        for _ in range(min(count, len(queue))):
            step, way, sub = queue.pop(0)
            ahead = far + 1 - step
            first = start_of(at(ahead if way == 0 else -ahead), sub)
            if (way, step - 1, sub) in arrivals:
                arrivals.pop((way, step - 1, sub)).wait_recv()

                def add(index, carry, way=way, step=step, sub=sub, first=first):
                    here = pl.ds(pl.multiple_of(index * step_rows, step_rows), step_rows)
                    there = pl.ds(
                        pl.multiple_of(first + index * step_rows, step_rows), step_rows
                    )
                    grad_ref[there] = (
                        grad_ref[there].astype(f32) + coming[way, step - 2, sub, here].astype(f32)
                    ).astype(grad_ref.dtype)
                    return carry

                lax.fori_loop(0, sub_rows // step_rows, add, 0)
            source = (
                first_ref.at[pl.ds(sub * sub_rows, sub_rows)]
                if step == 1
                else grad_ref.at[pl.ds(first, sub_rows)]
            )
            copy = send(
                source,
                coming.at[way, step - 1, sub],
                send_sem.at[way, step - 1, sub],
                recv_sem.at[way, step - 1, sub],
                ends[way],
            )
            sends.append(copy)
            arrivals[way, step, sub] = copy

    def finish(share_ref):
        go(len(queue))
        for copy in sends:
            copy.wait_send()
        for sub in range(2):
            landed = []
            for way in range(2):
                if (way, far, sub) in arrivals:
                    arrivals.pop((way, far, sub)).wait_recv()
                    landed.append(way)

            def add(index, carry, sub=sub, landed=landed):
                here = pl.ds(pl.multiple_of(index * step_rows, step_rows), step_rows)
                there = pl.ds(
                    pl.multiple_of(start_of(at(0), sub) + index * step_rows, step_rows), step_rows
                )
                out = pl.ds(
                    pl.multiple_of(sub * sub_rows + index * step_rows, step_rows), step_rows
                )
                value = grad_ref[there].astype(f32)
                for way in landed:
                    value = value + coming[way, far - 1, sub, here].astype(f32)
                share_ref[out] = value.astype(share_ref.dtype)
                return carry

            lax.fori_loop(0, sub_rows // step_rows, add, 0)

    return go, finish


def slot_base(slot, quarter):
    ctx = lax.axis_size("ctx")
    tensor = lax.axis_size("tensor")
    of_core = lax.rem(lax.axis_index("tensor") - lax.div(slot, ctx) + tensor, tensor)
    of_ctx = lax.rem(lax.axis_index("ctx") - lax.rem(slot, ctx) + ctx, ctx)
    return of_core * quarter + of_ctx * (quarter * tensor)


def reachable(query_slot, key_slot, quarter):
    gap = slot_base(query_slot, quarter) - slot_base(key_slot, quarter)
    return gap, gap > -quarter


def masked_scores(keys, queries, gap):
    scores = lax.dot_general(
        keys, queries, (((1,), (1,)), ((), ())), preferred_element_type=jnp.float32
    ) * (1.0 / queries.shape[-1] ** 0.5)
    key_at = lax.broadcasted_iota(jnp.int32, scores.shape, 0)
    query_at = lax.broadcasted_iota(jnp.int32, scores.shape, 1)
    return jnp.where(key_at - query_at <= gap, scores, -1e30)


def attend_slot(slot, q_ref, k_ref, vt_ref, attended_ref, turned_ref, total_ref, work):
    scores_ref, peak_ref, sum_ref, out_ref = work
    slots, heads, quarter, head_width = q_ref.shape
    group = heads // k_ref.shape[1]

    def one_head(head, carry):
        kv_head = lax.div(head, group)
        peak_ref[...] = jnp.full(peak_ref.shape, -1e30, jnp.float32)
        sum_ref[...] = jnp.zeros(sum_ref.shape, jnp.float32)
        out_ref[...] = jnp.zeros(out_ref.shape, jnp.float32)

        def score(key_slot, carry):
            gap, seen = reachable(slot, key_slot, quarter)

            @pl.when(seen)
            def _():
                scores = masked_scores(k_ref[key_slot, kv_head], q_ref[slot, head], gap)
                scores_ref[key_slot] = scores
                peak_ref[...] = jnp.maximum(peak_ref[...], jnp.max(scores, axis=0, keepdims=True))

            return carry

        lax.fori_loop(0, slots, score, 0)

        def weigh(key_slot, carry):
            _, seen = reachable(slot, key_slot, quarter)

            @pl.when(seen)
            def _():
                raised = jnp.exp(scores_ref[key_slot] - peak_ref[...])
                sum_ref[...] += jnp.sum(raised, axis=0, keepdims=True)
                out_ref[...] += jnp.dot(
                    vt_ref[key_slot, kv_head],
                    raised.astype(jnp.bfloat16),
                    preferred_element_type=jnp.float32,
                )

            return carry

        lax.fori_loop(0, slots, weigh, 0)
        total_ref[slot, head] = peak_ref[...] + jnp.log(sum_ref[...])
        rows = pl.ds(pl.multiple_of(head * head_width, head_width), head_width)
        turned_ref[slot, rows] = (out_ref[...] / sum_ref[...]).astype(jnp.bfloat16)
        return carry

    lax.fori_loop(0, heads, one_head, 0)
    attended_ref[slot] = turned_ref[slot].astype(jnp.float32).T.astype(jnp.bfloat16)


def rotated(raw, gain, cosine, sine):
    half = raw.shape[-1] // 2
    scale = lax.rsqrt(jnp.mean(raw * raw, axis=-1, keepdims=True) + EPS)
    scaled = raw * scale * gain
    front, back = scaled[:, :half], scaled[:, half:]
    return jnp.concatenate(
        [front * cosine - back * sine, back * cosine + front * sine], axis=1
    )


def rotated_back(grad, raw, gain, cosine, sine):
    half = raw.shape[-1] // 2
    scale = lax.rsqrt(jnp.mean(raw * raw, axis=-1, keepdims=True) + EPS)
    normed = raw * scale
    front, back = grad[:, :half], grad[:, half:]
    grad = jnp.concatenate(
        [front * cosine + back * sine, back * cosine - front * sine], axis=1
    )
    gain_grad = jnp.sum(grad * normed, axis=0, keepdims=True)
    grad = grad * gain
    inner = jnp.mean(grad * normed, axis=-1, keepdims=True)
    return scale * (grad - normed * inner), gain_grad


def forward_kernel(
    shard_ref,
    input_ref,
    upstream_ref,
    qkv_ref,
    weight_ref,
    operator_gain_ref,
    gain_ref,
    query_gain_ref,
    key_gain_ref,
    cosine_ref,
    sine_ref,
    full_ref,
    attended_ref,
    turned_ref,
    total_ref,
    hidden_ref,
    normed_blocks,
    upstream_blocks,
    normed_input_ref,
    raw_ref,
    q_ref,
    k_ref,
    kt_ref,
    v_ref,
    gate_up_grad_ref,
    activation_ref,
    vt_ref,
    normed_ref,
    total_acc,
    scores_ref,
    peak_ref,
    sum_ref,
    out_ref,
    part_ref,
    core_going,
    core_coming,
    ctx_going,
    ctx_coming,
    ring_send,
    ring_recv,
    core_send,
    core_recv,
    ctx_send,
    ctx_recv,
    spread_send,
    spread_recv,
    local_sem,
):
    f32 = jnp.float32
    bf16 = jnp.bfloat16
    size = lax.axis_size("fsdp")
    ctx = lax.axis_size("ctx")
    tensor = lax.axis_size("tensor")
    far = size // 2
    slots, heads, quarter, head_width = q_ref.shape
    kv = k_ref.shape[1]
    rows = shard_ref.shape[0]
    tokens = slots * quarter
    hidden_units = activation_ref.shape[1]
    at, _ = ring_ends()
    greet()
    go, land, finish = gather_ring(shard_ref, full_ref, ring_send, ring_recv)
    go(2)
    keep = pltpu.make_async_copy(
        shard_ref,
        full_ref.at[pl.ds(pl.multiple_of(at(0) * rows, rows), rows)],
        local_sem,
    )
    keep.start()
    work = (scores_ref, peak_ref, sum_ref, out_ref)

    def prepare(slot, carry):
        def norm(block):
            value = input_ref[slot, block].astype(f32)
            scale = lax.rsqrt(jnp.mean(value * value, axis=-1, keepdims=True) + EPS)
            normed_input_ref[slot, block] = (value * scale * operator_gain_ref[...]).astype(bf16)

        add_rows(quarter, 32, norm)
        raw_ref[slot] = jnp.dot(
            normed_input_ref[slot], qkv_ref[...], preferred_element_type=f32
        )
        cosine = cosine_ref[slot]
        sine = sine_ref[slot]
        for head in range(heads):
            raw = raw_ref[slot, :, head * head_width : (head + 1) * head_width]
            q_ref[slot, head] = rotated(raw, query_gain_ref[...], cosine, sine).astype(bf16)
        for head in range(kv):
            start = (heads + head) * head_width
            raw = raw_ref[slot, :, start : start + head_width]
            turned = rotated(raw, key_gain_ref[...], cosine, sine)
            k_ref[slot, head] = turned.astype(bf16)
            kt_ref[slot, head] = turned.T.astype(bf16)
            start = (heads + kv + head) * head_width
            raw = raw_ref[slot, :, start : start + head_width]
            v_ref[slot, head] = raw.astype(bf16)
            vt_ref[slot, head] = raw.T.astype(bf16)
        here = pl.ds(pl.multiple_of(slot * quarter, quarter), quarter)
        for owner in range(size):
            upstream_blocks[owner, here] = upstream_ref[
                slot, :, owner * rows : (owner + 1) * rows
            ]
        return carry

    lax.fori_loop(0, slots, prepare, 0)
    go(1)

    def accumulate(offset, lhs, start, stop, first=False):
        owner = at(offset)
        there = pl.ds(pl.multiple_of(owner * rows, rows), rows)
        for column in range(start, stop):
            columns = slice(column * hidden_units, (column + 1) * hidden_units)

            def add(here, columns=columns):
                value = jnp.dot(
                    lhs[owner, here], full_ref[there, columns], preferred_element_type=f32
                )
                if first:
                    total_acc[here, columns] = value
                else:
                    total_acc[here, columns] += value

            add_rows(tokens, quarter, add)

    def project(slot):
        attend_slot(slot, q_ref, k_ref, vt_ref, attended_ref, turned_ref, total_ref, work)
        return lax.dot_general(
            attended_ref[slot],
            weight_ref[...],
            (((1,), (1,)), ((), ())),
            preferred_element_type=f32,
        )

    sends = []
    by_core = {}
    by_ctx = {}
    for core in range(1, tensor):
        for step in list(range(1, ctx)) + [0]:
            core_going[core - 1, step] = project(core * ctx + step).astype(bf16)
            copy = send(
                core_going.at[core - 1, step],
                core_coming.at[core - 1, step],
                core_send.at[core - 1, step],
                core_recv.at[core - 1, step],
                other("tensor", -core),
            )
            sends.append(copy)
            by_core[core, step] = copy
    for step in list(range(1, ctx)) + [0]:
        part_ref[...] = project(step)
        for core in range(1, tensor):
            by_core[core, step].wait_recv()
            part_ref[...] += core_coming[core - 1, step].astype(f32)
        if step > 0:
            ctx_going[step - 1] = part_ref[...].astype(bf16)
            copy = send(
                ctx_going.at[step - 1],
                ctx_coming.at[step - 1],
                ctx_send.at[step - 1],
                ctx_recv.at[step - 1],
                other("ctx", -step),
            )
            sends.append(copy)
            by_ctx[step] = copy
        if step < 2:
            go(1)
    keep.wait()
    accumulate(0, upstream_blocks, 2, 3, True)
    for step in range(1, ctx):
        by_ctx[step].wait_recv()
        part_ref[...] += ctx_coming[step - 1].astype(f32)

    def norm(block):
        hidden = input_ref[0, block].astype(f32) + part_ref[block]
        hidden_ref[block] = hidden
        scale = lax.rsqrt(jnp.mean(hidden * hidden, axis=-1, keepdims=True) + EPS)
        normed_ref[0, 0, block] = (hidden * scale * gain_ref[...]).astype(bf16)

    add_rows(quarter, 16, norm)
    spread = []
    for step in range(1, ctx):
        copy = send(
            normed_ref.at[0, 0],
            normed_ref.at[0, step],
            spread_send.at[0, step],
            spread_recv.at[0, step],
            other("ctx", step),
        )
        sends.append(copy)
        spread.append(copy)
    handed = []

    def hand_over(step):
        for core in range(1, tensor):
            copy = send(
                normed_ref.at[0, step],
                normed_ref.at[core, step],
                spread_send.at[core, step],
                spread_recv.at[core, step],
                other("tensor", core),
            )
            sends.append(copy)
            handed.append(copy)

    hand_over(0)
    go(1)

    def keep_blocks(slot):
        here = slice(slot * quarter, (slot + 1) * quarter)
        for owner in range(size):
            normed_blocks[owner, here] = normed_ref[
                slot // ctx, slot % ctx, :, owner * rows : (owner + 1) * rows
            ]

    near = max(0, far - 2)
    if far > 3:
        land(near)
        for offset in range(1, near + 1):
            accumulate(offset, upstream_blocks, 2, 3)
            accumulate(-offset, upstream_blocks, 2, 3)
    keep_blocks(0)
    go(1)
    for step in range(1, ctx):
        spread[step - 1].wait_recv()
        hand_over(step)
        keep_blocks(step)
    for core in range(1, tensor):
        for step in range(ctx):
            handed[(core - 1) + step * (tensor - 1)].wait_recv()
            keep_blocks(core * ctx + step)
    accumulate(0, normed_blocks, 0, 2, True)
    if far > 3:
        accumulate(1, normed_blocks, 0, 2)
        accumulate(-1, normed_blocks, 0, 2)
        go(2)
        for offset in range(2, near + 1):
            accumulate(offset, normed_blocks, 0, 2)
            accumulate(-offset, normed_blocks, 0, 2)
    else:
        near = 0
    go(2 * far)
    for offset in range(near + 1, far):
        land(offset)
        accumulate(offset, upstream_blocks, 2, 3)
        accumulate(-offset, upstream_blocks, 2, 3)
        accumulate(offset, normed_blocks, 0, 2)
        accumulate(-offset, normed_blocks, 0, 2)
    land(far)
    accumulate(far, upstream_blocks, 2, 3)
    accumulate(far, normed_blocks, 0, 2)

    def activate(here):
        gate = total_acc[here, :hidden_units]
        upper = total_acc[here, hidden_units : 2 * hidden_units]
        grad = total_acc[here, 2 * hidden_units :]
        sigmoid = 1.0 / (1.0 + jnp.exp(-gate))
        silu = gate * sigmoid
        activation_ref[here] = (silu * upper).astype(bf16)
        slope = sigmoid * (1.0 + gate * (1.0 - sigmoid))
        gate_up_grad_ref[here, :hidden_units] = (grad * upper * slope).astype(bf16)
        gate_up_grad_ref[here, hidden_units:] = (grad * silu).astype(bf16)

    add_rows(tokens, 16, activate)
    finish()
    for copy in sends:
        copy.wait_send()


def forward_gather(shard, inputs, upstream, qkv, weight, gains, cosine, sine):
    size = lax.axis_size("fsdp")
    ctx = lax.axis_size("ctx")
    tensor = lax.axis_size("tensor")
    far = size // 2
    rows, columns = shard.shape
    slots, quarter, width = inputs.shape
    q_cols = weight.shape[1]
    head_width = gains[2].shape[1]
    heads = q_cols // head_width
    kv = (qkv.shape[1] // head_width - heads) // 2
    tokens = slots * quarter
    hidden_units = columns // 3
    in_vmem = pl.BlockSpec(memory_space=pltpu.VMEM)
    dma = pltpu.SemaphoreType.DMA
    bf16 = jnp.bfloat16
    f32 = jnp.float32
    cores = max(1, tensor - 1)
    shape = jax.ShapeDtypeStruct
    return pl.pallas_call(
        forward_kernel,
        out_shape=(
            shape((rows * size, columns), bf16),
            shape((slots, quarter, q_cols), bf16),
            shape((slots, q_cols, quarter), bf16),
            shape((slots, heads, 1, quarter), f32),
            shape((quarter, width), f32),
            shape((size, tokens, rows), bf16),
            shape((size, tokens, rows), bf16),
            shape((slots, quarter, width), bf16),
            shape((slots, quarter, qkv.shape[1]), f32),
            shape((slots, heads, quarter, head_width), bf16),
            shape((slots, kv, quarter, head_width), bf16),
            shape((slots, kv, head_width, quarter), bf16),
            shape((slots, kv, quarter, head_width), bf16),
            shape((tokens, 2 * hidden_units), bf16),
            shape((tokens, hidden_units), bf16),
        ),
        in_specs=[in_vmem] * 11,
        out_specs=(in_vmem,) * 15,
        scratch_shapes=[
            pltpu.VMEM((slots, kv, head_width, quarter), bf16),
            pltpu.VMEM((tensor, ctx, quarter, width), bf16),
            pltpu.VMEM((tokens, columns), f32),
            pltpu.VMEM((slots, quarter, quarter), f32),
            pltpu.VMEM((1, quarter), f32),
            pltpu.VMEM((1, quarter), f32),
            pltpu.VMEM((head_width, quarter), f32),
            pltpu.VMEM((quarter, width), f32),
            pltpu.VMEM((cores, ctx, quarter, width), bf16),
            pltpu.VMEM((cores, ctx, quarter, width), bf16),
            pltpu.VMEM((max(1, ctx - 1), quarter, width), bf16),
            pltpu.VMEM((max(1, ctx - 1), quarter, width), bf16),
            dma((2, far, 2)),
            dma((2, far, 2)),
            dma((cores, ctx)),
            dma((cores, ctx)),
            dma((ctx,)),
            dma((ctx,)),
            dma((tensor, ctx)),
            dma((tensor, ctx)),
            dma(()),
        ],
        compiler_params=pltpu.CompilerParams(
            collective_id=2, has_side_effects=True, vmem_limit_bytes=62 * 1024 * 1024
        ),
        name="forward_gather",
    )(shard, inputs, upstream, qkv, weight, *gains, cosine, sine)


def group_reduce(part_ref, core_coming, ctx_going, ctx_coming, sems, sends):
    f32 = jnp.float32
    ctx = lax.axis_size("ctx")
    tensor = lax.axis_size("tensor")
    quarter = part_ref.shape[1]
    core_send, core_recv, ctx_send, ctx_recv = sems
    by_core = []
    by_ctx = []

    def over_cores():
        for core in range(1, tensor):
            copy = send(
                part_ref.at[pl.ds(core * ctx, ctx)],
                core_coming.at[core - 1],
                core_send.at[core - 1],
                core_recv.at[core - 1],
                other("tensor", -core),
            )
            sends.append(copy)
            by_core.append(copy)

    def over_ctx(sum_ref, hold=False):
        for copy in by_core:
            copy.wait_recv()
        for step in list(range(1, ctx)) + [0]:

            def add(block, step=step):
                value = part_ref[step, block].astype(f32)
                for core in range(1, tensor):
                    value = value + core_coming[core - 1, step, block].astype(f32)
                if step == 0:
                    sum_ref[block] = value
                else:
                    ctx_going[step - 1, block] = value.astype(jnp.bfloat16)

            add_rows(quarter, 16, add)
            if step > 0 and not hold:
                copy = send(
                    ctx_going.at[step - 1],
                    ctx_coming.at[step - 1],
                    ctx_send.at[step - 1],
                    ctx_recv.at[step - 1],
                    other("ctx", -step),
                )
                sends.append(copy)
                by_ctx.append(copy)

    def finish():
        for copy in by_ctx:
            copy.wait_recv()

    return over_cores, over_ctx, finish


def attend_slot_grad(slot, refs, turned_grad, accumulators):
    q_ref, k_ref, kt_ref, v_ref, turned_ref, total_ref, dq_ref = refs
    dq_acc, dk_acc, dv_acc = accumulators
    f32 = jnp.float32
    bf16 = jnp.bfloat16
    slots, heads, quarter, head_width = q_ref.shape
    group = heads // k_ref.shape[1]
    scale = 1.0 / head_width**0.5

    def one_head(head, carry):
        kv_head = lax.div(head, group)
        rows = pl.ds(pl.multiple_of(head * head_width, head_width), head_width)
        grad = turned_grad[rows]
        delta = jnp.sum(
            grad.astype(f32) * turned_ref[slot, rows].astype(f32), axis=0, keepdims=True
        )
        dq_acc[...] = jnp.zeros(dq_acc.shape, f32)

        def one_key_slot(key_slot, carry):
            gap, seen = reachable(slot, key_slot, quarter)

            @pl.when(seen)
            def _():
                queries = q_ref[slot, head]
                scores = masked_scores(k_ref[key_slot, kv_head], queries, gap)
                probs = jnp.exp(scores - total_ref[slot, head])
                prob_grad = jnp.dot(v_ref[key_slot, kv_head], grad, preferred_element_type=f32)
                score_grad = (probs * (prob_grad - delta)).astype(bf16)
                dv_acc[key_slot, head] += lax.dot_general(
                    probs.astype(bf16), grad, (((1,), (1,)), ((), ())), preferred_element_type=f32
                )
                dk_acc[key_slot, head] += jnp.dot(score_grad, queries, preferred_element_type=f32)
                dq_acc[...] += jnp.dot(
                    kt_ref[key_slot, kv_head], score_grad, preferred_element_type=f32
                )

            return carry

        lax.fori_loop(0, slots, one_key_slot, 0)
        dq_ref[slot, head] = (dq_acc[...] * scale).astype(bf16)
        return carry

    lax.fori_loop(0, heads, one_head, 0)


def backward_kernel(
    full_ref,
    normed_ref,
    upstream_ref,
    gate_up_ref,
    activation_ref,
    hidden_ref,
    own_upstream_ref,
    gain_ref,
    weight_ref,
    q_ref,
    k_ref,
    kt_ref,
    v_ref,
    turned_ref,
    total_ref,
    attended_ref,
    normed_input_ref,
    raw_ref,
    qkv_ref,
    query_gain_ref,
    key_gain_ref,
    cosine_ref,
    sine_ref,
    share_ref,
    hidden_grad_ref,
    output_ref,
    input_sum_ref,
    input_going,
    qkv_grad_ref,
    weight_grad_ref,
    gain_grad_ref,
    all_grad_ref,
    dq_ref,
    raw_grad_ref,
    hidden_part_ref,
    down_part_ref,
    grad_ref,
    coming,
    core_coming,
    ctx_going,
    ctx_coming,
    out_sum_ref,
    turned_grad,
    own_output,
    dq_acc,
    dk_acc,
    dv_acc,
    ring_send,
    ring_recv,
    core_send,
    core_recv,
    ctx_send,
    ctx_recv,
    spread_send,
    spread_recv,
    output_send,
    output_recv,
    local_sem,
    full_sem,
):
    f32 = jnp.float32
    bf16 = jnp.bfloat16
    size = lax.axis_size("fsdp")
    ctx = lax.axis_size("ctx")
    tensor = lax.axis_size("tensor")
    me_t = lax.axis_index("tensor")
    far = size // 2
    slots, heads, quarter, head_width = q_ref.shape
    rows = grad_ref.shape[0] // size
    gate_up_cols = gate_up_ref.shape[1]
    hidden_units = activation_ref.shape[1]
    at, _ = ring_ends()
    sends = []
    load = pltpu.make_async_copy(full_ref, grad_ref, full_sem)
    load.start()
    greet()
    reduce_hidden = group_reduce(
        hidden_part_ref,
        core_coming.at[0],
        ctx_going.at[0],
        ctx_coming.at[0],
        (core_send.at[0], core_recv.at[0], ctx_send.at[0], ctx_recv.at[0]),
        sends,
    )
    reduce_down = group_reduce(
        down_part_ref,
        core_coming.at[1],
        ctx_going.at[1],
        ctx_coming.at[1],
        (core_send.at[1], core_recv.at[1], ctx_send.at[1], ctx_recv.at[1]),
        sends,
    )
    reduce_input = group_reduce(
        hidden_part_ref,
        core_coming.at[2],
        input_going,
        None,
        (core_send.at[2], core_recv.at[2], None, None),
        sends,
    )
    go, finish_ring = scatter_ring(grad_ref, share_ref, coming, ring_send, ring_recv)

    def piece(offset):
        here = pl.ds(pl.multiple_of(at(offset) * rows, rows), rows)
        target_ref = grad_ref
        if offset == far:
            here = slice(0, rows)
            target_ref = share_ref
        for start in range(0, gate_up_cols, hidden_units):
            columns = slice(start, start + hidden_units)
            target_ref[here, columns] = lax.dot_general(
                normed_ref[at(offset)],
                gate_up_ref[:, columns],
                (((0,), (0,)), ((), ())),
                preferred_element_type=f32,
            ).astype(bf16)
        target_ref[here, gate_up_cols:] = lax.dot_general(
            upstream_ref[at(offset)],
            activation_ref[...],
            (((0,), (0,)), ((), ())),
            preferred_element_type=f32,
        ).astype(bf16)

    def pieces(offset):
        piece(offset)
        piece(-offset)

    piece(far)
    go(2)
    load.wait()

    def part_of_slot(target_ref, lhs_ref, columns):
        def one(slot, carry):
            here = pl.ds(pl.multiple_of(slot * quarter, quarter), quarter)
            target_ref[slot] = lax.dot_general(
                lhs_ref[here],
                grad_ref[:, columns],
                (((1,), (1,)), ((), ())),
                preferred_element_type=f32,
            ).astype(bf16)
            return carry

        lax.fori_loop(0, slots, one, 0)

    part_of_slot(hidden_part_ref, gate_up_ref, slice(0, gate_up_cols))
    reduce_hidden[0]()
    parts_sent = list(sends)
    sends.clear()
    part_of_slot(down_part_ref, activation_ref, slice(gate_up_cols, None))
    reduce_hidden[1](input_sum_ref)
    reduce_down[0]()
    ready = 0
    if far > 1:
        pieces(far - 1)
        go(2)
        ready = 1
    dk_acc[...] = jnp.zeros(dk_acc.shape, f32)
    dv_acc[...] = jnp.zeros(dv_acc.shape, f32)
    if far > 2:
        pieces(far - 2)
        ready = 2
    go(2)
    reduce_hidden[2]()

    def norm_back(block):
        grad = input_sum_ref[block]
        for step in range(1, ctx):
            grad = grad + ctx_coming[0, step - 1, block].astype(f32)
        hidden = hidden_ref[block]
        scale = lax.rsqrt(jnp.mean(hidden * hidden, axis=-1, keepdims=True) + EPS)
        grad = grad * gain_ref[...]
        inner = jnp.mean(grad * hidden, axis=-1, keepdims=True) * (scale * scale)
        grad = own_upstream_ref[block].astype(f32) + scale * (grad - hidden * inner)
        hidden_grad_ref[block] = grad
        all_grad_ref[0, block] = grad.astype(bf16)

    add_rows(quarter, 16, norm_back)
    spread = []
    handed = {}
    for step in range(1, ctx):
        copy = send(
            all_grad_ref.at[0],
            all_grad_ref.at[step],
            spread_send.at[0, step],
            spread_recv.at[0, step],
            other("ctx", step),
        )
        sends.append(copy)
        spread.append(copy)

    def hand_over(step):
        for core in range(1, tensor):
            copy = send(
                all_grad_ref.at[step],
                all_grad_ref.at[core * ctx + step],
                spread_send.at[core, step],
                spread_recv.at[core, step],
                other("tensor", core),
            )
            sends.append(copy)
            handed[core, step] = copy

    hand_over(0)
    reduce_down[1](out_sum_ref)

    def attention_back(slot):
        grad = jnp.dot(all_grad_ref[slot], weight_ref[...], preferred_element_type=f32)
        turned_grad[...] = grad.T.astype(bf16)
        attend_slot_grad(
            slot,
            (q_ref, k_ref, kt_ref, v_ref, turned_ref, total_ref, dq_ref),
            turned_grad,
            (dq_acc, dk_acc, dv_acc),
        )

    if far > 2:
        go(2)
    attention_back(0)
    for core in range(1, tensor):
        handed[core, 0].wait_recv()
        attention_back(core * ctx)
    if far > 2:
        go(2)
    for step in range(1, ctx):
        spread[step - 1].wait_recv()
        hand_over(step)
        attention_back(step)
    for offset in range(far - ready - 1, 0, -1):
        pieces(offset)
    piece(0)
    go(2)
    for step in range(1, ctx):
        for core in range(1, tensor):
            handed[core, step].wait_recv()
            attention_back(core * ctx + step)
    go(2)
    reduce_down[2]()

    def output(block):
        value = hidden_ref[block] + out_sum_ref[block]
        for step in range(1, ctx):
            value = value + ctx_coming[1, step - 1, block].astype(f32)
        own_output[block] = value.astype(bf16)

    add_rows(quarter, 16, output)
    keep = pltpu.make_async_copy(own_output, output_ref.at[me_t], local_sem)
    keep.start()
    given = []
    for core in range(1, tensor):
        copy = send(
            own_output,
            output_ref.at[me_t],
            output_send.at[core],
            output_recv.at[core],
            other("tensor", core),
        )
        sends.append(copy)
        given.append(copy)
    kv = k_ref.shape[1]
    group = heads // kv
    scale = 1.0 / head_width**0.5
    gain_grad_ref[...] = jnp.zeros(gain_grad_ref.shape, f32)

    def rounded(value):
        return value.astype(bf16).astype(f32)

    def heads_back(slot, carry):
        cosine = cosine_ref[slot]
        sine = sine_ref[slot]
        columns = []
        for head in range(heads + kv):
            raw = raw_ref[slot, :, head * head_width : (head + 1) * head_width]
            if head < heads:
                grad = dq_ref[slot, head].astype(f32).T
                gain_ref_here, row = query_gain_ref, 0
            else:
                first = (head - heads) * group
                grad = rounded(dk_acc[slot, first] * scale)
                for member in range(first + 1, first + group):
                    grad = grad + rounded(dk_acc[slot, member] * scale)
                gain_ref_here, row = key_gain_ref, 1
            grad, gain_grad = rotated_back(grad, raw, gain_ref_here[...], cosine, sine)
            gain_grad_ref[row : row + 1] += gain_grad
            columns.append(grad.astype(bf16))
        for head in range(kv):
            grad = rounded(dv_acc[slot, head * group])
            for member in range(head * group + 1, (head + 1) * group):
                grad = grad + rounded(dv_acc[slot, member])
            columns.append(grad.astype(bf16))
        raw_grad_ref[slot] = jnp.concatenate(columns, axis=1)
        hidden_part_ref[slot] = lax.dot_general(
            raw_grad_ref[slot],
            qkv_ref[...],
            (((1,), (1,)), ((), ())),
            preferred_element_type=f32,
        ).astype(bf16)
        return carry

    for copy in parts_sent:
        copy.wait_send()
    lax.fori_loop(0, slots, heads_back, 0)
    reduce_input[0]()
    wide = rows * max(1, 256 // rows)

    def over_tokens(left_ref, right_ref, columns):
        total = 0.0
        for slot in range(slots):
            total = total + lax.dot_general(
                left_ref[slot, :, columns],
                right_ref[slot],
                (((0,), (0,)), ((), ())),
                preferred_element_type=f32,
            )
        return total.astype(bf16)

    def weights_back(index, carry):
        columns = pl.ds(pl.multiple_of(index * wide, wide), wide)
        qkv_grad_ref[columns] = over_tokens(normed_input_ref, raw_grad_ref, columns)
        weight_grad_ref[columns] = over_tokens(all_grad_ref, attended_ref, columns)
        return carry

    lax.fori_loop(0, grad_ref.shape[0] // wide, weights_back, 0)
    reduce_input[1](input_sum_ref, True)
    finish_ring(share_ref)
    for copy in given:
        copy.wait_recv()
    for copy in sends:
        copy.wait_send()
    keep.wait()


def backward_scatter(
    full,
    normed_blocks,
    upstream_blocks,
    gate_up_grad,
    activation,
    hidden,
    own_upstream,
    gain,
    weight,
    queries,
    keys,
    keys_turned,
    values,
    attended_turned,
    totals,
    attended,
    normed_input,
    raw,
    qkv,
    query_gain,
    key_gain,
    cosine,
    sine,
):
    size = lax.axis_size("fsdp")
    ctx = lax.axis_size("ctx")
    tensor = lax.axis_size("tensor")
    far = size // 2
    slots, heads, quarter, head_width = queries.shape
    width = weight.shape[0]
    q_cols = weight.shape[1]
    rows = width // size
    columns = gate_up_grad.shape[1] + activation.shape[1]
    in_vmem = pl.BlockSpec(memory_space=pltpu.VMEM)
    dma = pltpu.SemaphoreType.DMA
    bf16 = jnp.bfloat16
    f32 = jnp.float32
    cores = max(1, tensor - 1)
    apart = max(1, ctx - 1)
    by_head = (slots, heads, quarter, head_width)
    return pl.pallas_call(
        backward_kernel,
        out_shape=(
            jax.ShapeDtypeStruct((rows, columns), bf16),
            jax.ShapeDtypeStruct((quarter, width), f32),
            jax.ShapeDtypeStruct((tensor, quarter, width), bf16),
            jax.ShapeDtypeStruct((quarter, width), f32),
            jax.ShapeDtypeStruct((apart, quarter, width), bf16),
            jax.ShapeDtypeStruct(qkv.shape, bf16),
            jax.ShapeDtypeStruct(weight.shape, bf16),
            jax.ShapeDtypeStruct((2, head_width), f32),
        ),
        in_specs=[pl.BlockSpec(memory_space=pl.ANY)] + [in_vmem] * 22,
        out_specs=(in_vmem,) * 8,
        scratch_shapes=[
            pltpu.VMEM((slots, quarter, width), bf16),
            pltpu.VMEM((slots, heads, head_width, quarter), bf16),
            pltpu.VMEM((slots, quarter, qkv.shape[1]), bf16),
            pltpu.VMEM((slots, quarter, width), bf16),
            pltpu.VMEM((slots, quarter, width), bf16),
            pltpu.VMEM((width, columns), bf16),
            pltpu.VMEM((2, far, 2, rows // 2, columns), bf16),
            pltpu.VMEM((3, cores, ctx, quarter, width), bf16),
            pltpu.VMEM((2, apart, quarter, width), bf16),
            pltpu.VMEM((2, apart, quarter, width), bf16),
            pltpu.VMEM((quarter, width), f32),
            pltpu.VMEM((q_cols, quarter), bf16),
            pltpu.VMEM((quarter, width), bf16),
            pltpu.VMEM((head_width, quarter), f32),
            pltpu.VMEM(by_head, f32),
            pltpu.VMEM(by_head, f32),
            dma((2, far, 2)),
            dma((2, far, 2)),
            dma((3, cores)),
            dma((3, cores)),
            dma((2, ctx)),
            dma((2, ctx)),
            dma((tensor, ctx)),
            dma((tensor, ctx)),
            dma((tensor,)),
            dma((tensor,)),
            dma(()),
            dma(()),
        ],
        compiler_params=pltpu.CompilerParams(
            collective_id=3, has_side_effects=True, vmem_limit_bytes=63 * 1024 * 1024
        ),
        name="backward_scatter",
    )(
        full,
        normed_blocks,
        upstream_blocks,
        gate_up_grad,
        activation,
        hidden,
        own_upstream,
        gain,
        weight,
        queries,
        keys,
        keys_turned,
        values,
        attended_turned,
        totals,
        attended,
        normed_input,
        raw,
        qkv,
        query_gain,
        key_gain,
        cosine,
        sine,
    )


def part_of(array, dim, count, start):
    return lax.dynamic_slice_in_dim(array, start, count, dim)


def shards(
    block_input,
    operator_gain,
    query_weight,
    key_weight,
    value_weight,
    output_weight,
    feedforward_gain,
    gate_weight,
    up_weight,
    down_weight,
    query_gain,
    key_gain,
    cotangent,
):
    bf16 = jnp.bfloat16
    f32 = jnp.float32
    fsdp = lax.axis_size("fsdp")
    ctx = lax.axis_size("ctx")
    tensor = lax.axis_size("tensor")
    me_c = lax.axis_index("ctx")
    me_t = lax.axis_index("tensor")
    seqs, tok_here, width = block_input.shape
    quarter = tok_here // tensor
    tokens = tok_here * ctx
    rows = seqs * tokens
    gain_rows = query_gain.shape[0]
    head_width = gain_rows * fsdp
    heads_shard = query_weight.shape[1] // head_width
    kv_shard = key_weight.shape[1] // head_width
    spread = heads_shard // kv_shard
    heads = heads_shard // ctx
    kv = max(1, kv_shard // ctx)
    group = heads // kv
    copies = max(1, ctx // kv_shard)
    q_cols = heads * head_width
    kv_cols = kv * head_width
    kv_start = ((me_c * heads) // spread) * head_width
    hidden_units = gate_weight.shape[1] // ctx
    shard_rows = query_weight.shape[0]

    gains = jnp.stack(
        [
            operator_gain,
            feedforward_gain,
            jnp.pad(query_gain, (0, shard_rows - gain_rows)),
            jnp.pad(key_gain, (0, shard_rows - gain_rows)),
        ],
        axis=1,
    )
    attention_pack = jnp.concatenate(
        [
            part_of(query_weight, 1, q_cols, me_c * q_cols),
            part_of(key_weight, 1, kv_cols, kv_start),
            part_of(value_weight, 1, kv_cols, kv_start),
            part_of(output_weight, 0, q_cols, me_c * q_cols).T,
            jnp.pad(gains, ((0, 0), (0, 124))),
        ],
        axis=1,
    )
    feedforward_shard = jnp.concatenate(
        [
            part_of(gate_weight, 1, hidden_units, me_c * hidden_units),
            part_of(up_weight, 1, hidden_units, me_c * hidden_units),
            part_of(down_weight, 0, hidden_units, me_c * hidden_units).T,
        ],
        axis=1,
    )
    attention_full, all_input, upstream = start_gather(attention_pack, block_input, cotangent)
    all_input = all_input.reshape(rows, width)
    upstream = upstream.reshape(rows, width)
    qkv_cols = q_cols + 2 * kv_cols
    qkv_full = attention_full[:, :qkv_cols]
    output_full = attention_full[:, qkv_cols : qkv_cols + q_cols]
    gains_full = attention_full[:, qkv_cols + q_cols :].astype(f32)
    operator_scale = gains_full[:, 0]
    feedforward_scale = gains_full[:, 1]
    query_scale = gains_full[:, 2].reshape(fsdp, shard_rows)[:, :gain_rows].reshape(-1)
    key_scale = gains_full[:, 3].reshape(fsdp, shard_rows)[:, :gain_rows].reshape(-1)

    own_input = part_of(block_input, 1, quarter, me_t * quarter)
    upstream_own = part_of(cotangent, 1, quarter, me_t * quarter)

    ctx_order = lax.rem(me_c - jnp.arange(ctx) + ctx, ctx)
    tensor_order = lax.rem(me_t - jnp.arange(tensor) + tensor, tensor)
    positions = (
        tensor_order[:, None, None] * quarter
        + ctx_order[None, :, None] * tok_here
        + jnp.arange(quarter)[None, None, :]
    ).reshape(tokens)
    cosine, sine = rotary_tables(positions, head_width)

    slots = tensor * ctx
    own_f32 = own_input.astype(f32)
    (
        feedforward_full,
        attended,
        attended_turned,
        totals,
        hidden,
        normed_blocks,
        upstream_blocks,
        normed_input,
        qkv_raw,
        queries,
        keys,
        keys_turned,
        values,
        gate_up_grad,
        activation,
    ) = forward_gather(
        feedforward_shard,
        all_input.reshape(slots, quarter, width),
        upstream.reshape(slots, quarter, width),
        qkv_full,
        output_full,
        (
            operator_scale[None],
            feedforward_scale[None],
            query_scale[None],
            key_scale[None],
        ),
        cosine.reshape(slots, quarter, -1),
        sine.reshape(slots, quarter, -1),
    )
    (
        feedforward_share,
        hidden_grad,
        block_output,
        normed_input_grad,
        input_going,
        qkv_weight_grad,
        output_weight_grad,
        head_gain_grads,
    ) = backward_scatter(
        feedforward_full,
        normed_blocks,
        upstream_blocks,
        gate_up_grad,
        activation,
        hidden,
        upstream_own.reshape(quarter, width),
        feedforward_scale.reshape(1, width),
        output_full,
        queries,
        keys,
        keys_turned,
        values,
        attended_turned,
        totals,
        attended,
        normed_input,
        qkv_raw,
        qkv_full,
        query_scale[None],
        key_scale[None],
        cosine.reshape(slots, quarter, -1),
        sine.reshape(slots, quarter, -1),
    )
    block_output = block_output.reshape(seqs, tok_here, width)
    gain_grads = head_gain_grads.T.reshape(fsdp, gain_rows, 2)
    gain_grads = jnp.pad(
        gain_grads, ((0, 0), (0, shard_rows - gain_rows), (0, 126))
    ).reshape(width, 128).astype(bf16)
    attention_grad = jnp.concatenate(
        [qkv_weight_grad, output_weight_grad, gain_grads], axis=1
    )
    attention_parts, feedforward_parts, input_grad = finish_sums(
        attention_grad,
        feedforward_share,
        normed_input_grad,
        input_going,
        hidden_grad,
        own_input.reshape(quarter, width),
        operator_scale[None],
    )
    attention_parts = attention_parts.astype(f32)
    input_grad = input_grad.reshape(seqs, tok_here, width)

    def columns(parts):
        return jnp.concatenate([parts[step] for step in range(ctx)], axis=1)

    def head_columns(parts):
        every = columns(parts)
        if copies == 1:
            return every
        return every.reshape(shard_rows, kv_shard, copies, head_width).sum(axis=2).reshape(
            shard_rows, -1
        )

    query_weight_grad = columns(attention_parts[:, :, :q_cols])
    key_weight_grad = head_columns(attention_parts[:, :, q_cols : q_cols + kv_cols])
    value_weight_grad = head_columns(attention_parts[:, :, q_cols + kv_cols : qkv_cols])
    gate_weight_grad = columns(feedforward_parts[:, :, :hidden_units].astype(f32))
    up_weight_grad = columns(
        feedforward_parts[:, :, hidden_units : 2 * hidden_units].astype(f32)
    )
    down_weight_grad = jnp.swapaxes(feedforward_parts[:, :, 2 * hidden_units :], 1, 2)
    down_weight_grad = down_weight_grad.astype(f32).reshape(-1, shard_rows)
    gain_parts = attention_parts[:, :, qkv_cols + q_cols : qkv_cols + q_cols + 2].sum(axis=0)

    def gain_part(pairs, gain):
        total = 0.0
        for weight, grad in pairs:
            total = total + jnp.sum(weight.astype(f32) * grad, axis=1)
        return total / gain.astype(f32)

    gain_columns = jnp.concatenate(
        [
            gain_part(
                [
                    (query_weight, query_weight_grad),
                    (key_weight, key_weight_grad),
                    (value_weight, value_weight_grad),
                ],
                operator_gain,
            )[:, None],
            gain_part(
                [(gate_weight, gate_weight_grad), (up_weight, up_weight_grad)], feedforward_gain
            )[:, None],
            gain_parts,
        ],
        axis=1,
    )
    gain_totals = gain_columns
    for step in range(1, tensor):
        gain_totals = gain_totals + shift(gain_columns, "tensor", step)

    return (
        block_output,
        input_grad,
        gain_totals[:, 0],
        query_weight_grad,
        key_weight_grad,
        value_weight_grad,
        jnp.swapaxes(attention_parts[:, :, qkv_cols : qkv_cols + q_cols], 1, 2).reshape(
            -1, shard_rows
        ),
        gain_totals[:, 1],
        gate_weight_grad,
        up_weight_grad,
        down_weight_grad,
        gain_totals[:gain_rows, 2],
        gain_totals[:gain_rows, 3],
    )


def solution(mesh):
    in_specs = (
        P("fsdp", "ctx", None),
        P("fsdp"),
        P("fsdp", "tensor"),
        P("fsdp", "tensor"),
        P("fsdp", "tensor"),
        P("tensor", "fsdp"),
        P("fsdp"),
        P("fsdp", "tensor"),
        P("fsdp", "tensor"),
        P("tensor", "fsdp"),
        P("fsdp"),
        P("fsdp"),
        P("fsdp", "ctx", None),
    )
    out_specs = (
        P("fsdp", "ctx", None),
        P("fsdp", "ctx", None),
        P("fsdp"),
        P("fsdp", "tensor"),
        P("fsdp", "tensor"),
        P("fsdp", "tensor"),
        P("tensor", "fsdp"),
        P("fsdp"),
        P("fsdp", "tensor"),
        P("fsdp", "tensor"),
        P("tensor", "fsdp"),
        P("fsdp"),
        P("fsdp"),
    )
    return jax.shard_map(shards, mesh=mesh, in_specs=in_specs, out_specs=out_specs, check_vma=False)
```
